256 devices in a mesh: sta: 32 (over y, z), tpl: 8 (over x, core).
Axes of the slice: x: 4, y: 4, z: 8, core: 2. Of those that a mesh axis runs over, the one named last changes fastest.
Arguments:
- station_data: float32 [3, 512, 3200], P(None, ('sta', 'tpl'))
- channel_mask: int32 [3, 512], P(None, 'sta'), may hold values 0 or 1
- template_waves: bfloat16 [256, 32, 3, 640], P('tpl', 'sta')
- pick_station: int32 [256, 32], P('tpl'), may hold values from 0 to 511, as said below
- pick_lag: int32 [256, 32], P('tpl'), may hold values from 0 to 1024, as said below
Outputs:
- network_stack: float32 [1536, 256], P('sta', 'tpl')
The draws below stay inside these ranges and needn't reach their ends.
Inputs may be any that keep to these rules, and one draw needn't show every extreme that they name: `pick_station`: the 32 picks of a template lie on distinct stations. Within each aligned block of 32 templates and for each pick index p, at most 4 templates have pick p on one aligned block of 16 stations; for every p this is reached on some block of stations. `pick_lag`: every template has a pick at lag 0 and a pick at lag 1024.
All inputs are finite; a program needn't handle non-finite values. No bound on the sum of `channel_mask` on one device may be relied on, other than what follows from the above.
Results may differ from the reference program's by a relative error of at most 0.0041.
Values may be sent and summed in bfloat16 or wider, within the bound.
No kernel may reach another device: no remote copies, remote signals or barrier semaphores. Data moves between devices by JAX's collectives and lax.ppermute only.
A program may use at most 64 MiB of HBM per device.

```python
import math
import jax
import jax.numpy as jnp
from jax import lax

S_DEV = 16
NT = 1536
L = 640
LAGS = 1024
BLOCK = 128
STATIONS = 512
PICKS = 32
TPL_GROUP = 32
TEMPLATES = 256
CAP = 4
SAMPLES = 3200
N_STA = 32
N_TPL = 8


def envelope(key, leading, length):
    blocks = length // 16 + 1
    levels = jnp.exp(jax.random.uniform(key, leading + (blocks,), minval=0.0, maxval=math.log(10.0)))
    return jnp.repeat(levels, 16, axis=-1)[..., :length]


def arrivals(key, shape):
    key_a, key_b, key_c = jax.random.split(key, 3)
    hits = jax.random.randint(key_a, (1,) + shape[1:], 0, 192) == 0
    sizes = jax.random.uniform(key_b, shape, minval=40.0, maxval=80.0)
    signs = jnp.where(jax.random.randint(key_c, shape, 0, 2) == 0, -1.0, 1.0)
    return jnp.where(hits, sizes * signs, 0.0)


def draw_station_data(key, part):
    key_a = jax.random.fold_in(key, 0)
    key_b = jax.random.fold_in(key, 1)
    key_c = jax.random.fold_in(key, 2)
    key_e = jax.random.fold_in(key, 4)
    shape = (3, STATIONS, SAMPLES)
    level = jnp.exp(jax.random.uniform(key_b, (3, STATIONS, 1), minval=0.0, maxval=math.log(10.0)))
    shaping = envelope(key_c, (1, STATIONS), SAMPLES)
    impulses = arrivals(key_e, shape)
    base = jnp.clip(jax.random.normal(key_a, shape), -6.0, 6.0)
    return (base + impulses) * shaping * level


def draw_template_waves(key, part):
    key_a, key_b, key_c = jax.random.split(key, 3)
    shape = (TEMPLATES, PICKS, 3, L)
    level = jnp.exp(jax.random.uniform(key_b, (TEMPLATES, PICKS, 3, 1), minval=0.0, maxval=math.log(10.0)))
    shaping = envelope(key_c, (TEMPLATES, PICKS, 1), L)
    base = jnp.clip(jax.random.normal(key_a, shape), -6.0, 6.0)
    return (base * shaping * level).astype(jnp.bfloat16)


def one_group(group_key):
    key_a, key_b, key_c = jax.random.split(group_key, 3)
    leader = jax.random.randint(key_a, (), 0, N_STA)
    order = jax.random.permutation(key_b, TPL_GROUP)
    rest = TPL_GROUP - 2 * CAP
    round_count = rest // (N_STA - 2) + 1
    round_keys = jax.random.split(key_c, round_count)
    shuffles = jax.vmap(lambda round_key: jax.random.permutation(round_key, N_STA - 2))(round_keys).reshape(-1)
    position = jnp.arange(TPL_GROUP)
    later = jnp.clip(position - 2 * CAP, 0, round_count * (N_STA - 2) - 1)
    offsets = jnp.where(position < CAP, 0, jnp.where(position < 2 * CAP, N_STA - 1, shuffles[later] + 1))
    by_position = (leader + offsets) % N_STA
    return by_position[order]


def draw_pick_station(key, part):
    key_a, key_b = jax.random.split(key, 2)
    group_keys = jax.vmap(lambda index: jax.random.fold_in(key_a, index))(jnp.arange(N_TPL))
    centres = jax.vmap(one_group)(group_keys).reshape(TEMPLATES, 1)
    shifts = jax.random.randint(key_b, (TEMPLATES, 1), 0, S_DEV)
    column = jnp.arange(PICKS).reshape(1, PICKS)
    owners = (centres + column) % N_STA
    locals_here = shifts % S_DEV
    return (owners * S_DEV + locals_here).astype(jnp.int32)


def draw_pick_lag(key, part):
    key_a, key_b, key_c = jax.random.split(key, 3)
    lags = jax.random.randint(key_a, (TEMPLATES, PICKS), 0, LAGS + 1)
    zero_at = jax.random.randint(key_b, (TEMPLATES, 1), 0, PICKS)
    top_at = (zero_at + jax.random.randint(key_c, (TEMPLATES, 1), 1, PICKS)) % PICKS
    column = jnp.arange(PICKS).reshape(1, PICKS)
    lags = jnp.where(column == zero_at, 0, lags)
    return jnp.where(column == top_at, LAGS, lags).astype(jnp.int32)


def with_ends(values, own_key, low, largest):
    longest = values.shape.index(max(values.shape))
    spots = []
    for shift in (0, 1):
        where = [jax.random.randint(jax.random.fold_in(own_key, axis), (), 0, length) for axis, length in enumerate(values.shape)]
        where[longest] = (where[longest] + shift) % values.shape[longest]
        spots.append(tuple(where))
    return values.at[spots[0]].set(low).at[spots[1]].set(largest)


def setup_inputs(seed: int = 0) -> dict:
    streams_of = jax.random.split(jax.random.key(seed), 6)
    station_data = draw_station_data(jax.random.fold_in(streams_of[5], 71), 0)
    channel_mask = with_ends((jax.random.randint(streams_of[1], (3, STATIONS), 0, 10) < 9).astype(jnp.int32), jax.random.fold_in(streams_of[1], 1), 0, 1)
    template_waves = draw_template_waves(jax.random.fold_in(streams_of[5], 71), 0)
    pick_station = draw_pick_station(jax.random.fold_in(streams_of[5], 71), 0)
    pick_lag = draw_pick_lag(jax.random.fold_in(streams_of[5], 71), 0)
    return dict(station_data=station_data, channel_mask=channel_mask, template_waves=template_waves, pick_station=pick_station, pick_lag=pick_lag)


epsilon = 1e-05

def window_scales(samples):
    leading = jnp.zeros(samples.shape[:-1] + (1,), jnp.float32)
    sum_one = jnp.concatenate([leading, jnp.cumsum(samples, axis=-1)], axis=-1)
    sum_two = jnp.concatenate([leading, jnp.cumsum(samples * samples, axis=-1)], axis=-1)
    starts = NT + LAGS
    mean_one = (sum_one[..., L:L + starts] - sum_one[..., :starts]) / L
    mean_two = (sum_two[..., L:L + starts] - sum_two[..., :starts]) / L
    return 1.0 / (L * jnp.sqrt(mean_two - mean_one * mean_one + epsilon))

def unit_waves(raw_waves):
    values = raw_waves.astype(jnp.float32)
    centred = values - lax.optimization_barrier(jnp.mean(values, axis=-1, keepdims=True))
    spread = jnp.sqrt(lax.optimization_barrier(jnp.mean(centred * centred, axis=-1, keepdims=True)) + epsilon)
    return (centred / spread).astype(jnp.bfloat16)

def toeplitz_rows(units):
    batch = units.shape[0]
    row_width = units.shape[1] + BLOCK
    padded = jnp.concatenate([units, jnp.zeros((batch, BLOCK), units.dtype)], axis=1)
    tiled = jnp.tile(padded, (1, BLOCK))
    trimmed = tiled[:, :BLOCK * (row_width - 1)].reshape(batch, BLOCK, row_width - 1)
    return jnp.concatenate([trimmed, jnp.zeros((batch, BLOCK, 1), units.dtype)], axis=2)

def frames_of(windows):
    batch, length = windows.shape
    row_total = (length - L) // BLOCK
    columns = [windows[:, BLOCK * offset:BLOCK * offset + row_total * BLOCK].reshape(batch, row_total, BLOCK) for offset in range((L + BLOCK) // BLOCK)]
    return jnp.concatenate(columns, axis=2)

def correlate(windows, units):
    frames = frames_of(windows).astype(jnp.float32)
    toeplitz = toeplitz_rows(units).astype(jnp.float32)
    product = jnp.einsum('bim,bjm->bij', frames, toeplitz, precision=lax.Precision.HIGHEST)
    return product.reshape(windows.shape[0], -1)

def reference(station_data, channel_mask, template_waves, pick_station, pick_lag):
    scales = window_scales(station_data)
    rounded = station_data.astype(jnp.bfloat16)
    weights = channel_mask.astype(jnp.float32).T

    def one_template(inputs):
        raw_waves, stations, pick_lags = inputs
        units = unit_waves(raw_waves)

        def take_window(station, lag_here):
            zero_start = jnp.zeros((), jnp.int32)
            station_start = station.astype(jnp.int32)
            lag_start = lag_here.astype(jnp.int32)
            window = lax.dynamic_slice(rounded, (zero_start, station_start, lag_start), (3, 1, NT + L))[:, 0]
            scale_rows = lax.dynamic_slice(scales, (zero_start, station_start, lag_start), (3, 1, NT))[:, 0]
            return (window, scale_rows)
        windows, factors = jax.vmap(take_window)(stations, pick_lags)
        correlation = correlate(windows.reshape(PICKS * 3, NT + L), units.reshape(PICKS * 3, L)).reshape(PICKS, 3, NT)
        available = weights[stations]
        return lax.optimization_barrier(jnp.sum(correlation * factors * available[:, :, None], axis=(0, 1)))
    network = lax.map(one_template, (template_waves, pick_station, pick_lag))
    return network.T
```

```python
import jax
import jax.numpy as jnp
from jax import lax
from jax.experimental import pallas as pl
from jax.experimental.pallas import tpu as pltpu
from jax.sharding import PartitionSpec as P

NT = 1536
L = 640
LAGS = 1024
SAMPLES = 3200
CAP = 4
STEP = 32
LANES = 128
BLOCKS = SAMPLES // STEP
OUT_BLOCKS = NT // STEP
TILES = L // LANES
DEPTH = L + LANES
EPSILON = 1e-05
VALID = 1 << 20


def exclusive_prefix(values):
    groups = values.reshape(STEP // 8, 8, values.shape[-1])
    row = lax.broadcasted_iota(jnp.int32, groups.shape, 1)
    total = groups
    for shift in (1, 2, 4):
        total = total + jnp.where(row >= shift, pltpu.roll(total, shift, 1), 0.0)
    inner = jnp.where(row >= 1, pltpu.roll(total, 1, 1), 0.0)
    pieces = [inner[0]]
    carry = total[0, 7:8]
    for group in range(1, STEP // 8):
        pieces.append(inner[group] + carry)
        carry = carry + total[group, 7:8]
    return jnp.concatenate(pieces, axis=0)


def window_sums(values):
    width = values.shape[-1]
    span = L // STEP
    ahead = pltpu.roll(values, width - span, 1) - values
    two = jnp.sum(values, axis=0, keepdims=True)
    two = two + pltpu.roll(two, width - 1, 1)
    four = two + pltpu.roll(two, width - 2, 1)
    eight = four + pltpu.roll(four, width - 4, 1)
    sixteen = eight + pltpu.roll(eight, width - 8, 1)
    whole = sixteen + pltpu.roll(four, width - 16, 1)
    return whole + exclusive_prefix(ahead)


def kernel(meta_ref, mask_ref, tiles_ref, waves_ref, out_ref,
           frames, scales, units, acc, twice, dense, slots):
    peers = meta_ref.shape[1]

    def list_slot(slot, count):
        slots[count] = slot
        held = meta_ref[slot & (CAP - 1), slot >> 2] >> 20
        return count + held

    count = lax.fori_loop(0, peers * CAP, list_slot, jnp.int32(0))

    @pl.loop(0, peers * CAP // 16)
    def _(chunk):
        rows = pl.ds(pl.multiple_of(chunk * 16, 16), 16)
        for c in range(3):
            values = waves_ref[rows, c * L:(c + 1) * L].astype(jnp.float32)
            centred = values - jnp.mean(values, axis=-1, keepdims=True)
            power = jnp.mean(centred * centred, axis=-1, keepdims=True)
            unit = centred / jnp.sqrt(power + EPSILON)
            unit = unit.astype(jnp.bfloat16).astype(jnp.float32)
            for tile in range(TILES):
                units[c * TILES + tile, rows, :] = unit[:, tile * LANES:(tile + 1) * LANES]

    @pl.loop(0, tiles_ref.shape[0])
    def _(record):
        tile = tiles_ref[record]
        for turn in range(DEPTH // STEP):
            rolled = tile if turn == 0 else pltpu.roll(tile, LANES - turn, 1)
            frames[record, turn * STEP:(turn + 1) * STEP, :] = rolled.astype(jnp.bfloat16)
        mean_one = window_sums(tile) * (1.0 / L)
        mean_two = window_sums(tile * tile) * (1.0 / L)
        within = lax.rem(record, 6)
        station = (record // 6) * 2 + (within & 1)
        weight = mask_ref[within >> 1, station].astype(jnp.float32)
        spread = L * jnp.sqrt(mean_two - mean_one * mean_one + EPSILON)
        scales[record] = weight / spread

    acc[...] = jnp.zeros_like(acc)
    row = lax.broadcasted_iota(jnp.int32, (STEP, LANES), 0)
    lane = lax.broadcasted_iota(jnp.int32, (STEP, LANES), 1)
    own = lane >= row
    lane_used = lane < BLOCKS - L // STEP

    @pl.loop(0, count)
    def _(index):
        slot = slots[index]
        packed = meta_ref[slot & (CAP - 1), slot >> 2]
        template = packed & 31
        station = (packed >> 5) & 15
        lag = (packed >> 9) & 2047
        total = jnp.zeros((STEP, LANES), jnp.float32)
        for c in range(3):
            record = (station >> 1) * 6 + 2 * c + (station & 1)
            before = jnp.zeros((STEP, LANES), jnp.float32)
            columns = []
            for tile in range(TILES):
                wave = units[c * TILES + tile, pl.ds(slot, STEP, stride=0), :]
                spread = pltpu.roll(wave, 0, 1, stride=1, stride_axis=0)
                columns.append(jnp.where(own, spread, before).astype(jnp.bfloat16))
                before = spread
            columns.append(jnp.where(own, 0.0, before).astype(jnp.bfloat16))
            toeplitz = jnp.concatenate(columns, axis=1)
            product = jnp.dot(toeplitz, frames[record], preferred_element_type=jnp.float32)
            total = total + product * scales[record]
        total = jnp.where(lane_used, total, 0.0)
        first = pltpu.roll(total, LANES - (lag >> 5), 1)
        twice[0:STEP, :] = first
        twice[STEP:2 * STEP, :] = pltpu.roll(first, LANES - 1, 1)
        rows = pl.ds(pl.multiple_of(template * STEP, STEP), STEP)
        acc[rows, :] += twice[pl.ds(lag & (STEP - 1), STEP), :]

    for group in range(STEP // 4):
        parts = [acc[pl.ds(4 * group + j, STEP, stride=STEP), :] for j in range(4)]
        turned = jnp.concatenate(parts, axis=0).T
        dense[pl.ds(group, OUT_BLOCKS, stride=8), :] = turned[:OUT_BLOCKS]
    out_ref[...] = dense[...].astype(out_ref.dtype)


def partial_stack(meta, channel_mask, gathered, received):
    group_size = meta.shape[1]
    slot_count = received.shape[0]
    records = gathered.shape[0]
    return pl.pallas_call(
        kernel,
        out_shape=jax.ShapeDtypeStruct((NT * group_size // LANES, LANES), jnp.bfloat16),
        in_specs=[
            pl.BlockSpec(memory_space=pltpu.SMEM),
            pl.BlockSpec(memory_space=pltpu.SMEM),
            pl.BlockSpec(memory_space=pltpu.VMEM),
            pl.BlockSpec(memory_space=pltpu.VMEM),
        ],
        out_specs=pl.BlockSpec(memory_space=pltpu.VMEM),
        scratch_shapes=[
            pltpu.VMEM((records, DEPTH, LANES), jnp.bfloat16),
            pltpu.VMEM((records, STEP, LANES), jnp.float32),
            pltpu.VMEM((3 * TILES, slot_count, LANES), jnp.float32),
            pltpu.VMEM((group_size * STEP, LANES), jnp.float32),
            pltpu.VMEM((2 * STEP, LANES), jnp.float32),
            pltpu.VMEM((NT * group_size // LANES, LANES), jnp.float32),
            pltpu.SMEM((slot_count + 1,), jnp.int32),
        ],
        compiler_params=pltpu.CompilerParams(vmem_limit_bytes=40 * 1024 * 1024),
        name="matched_filter",
    )(meta, channel_mask, gathered, received)


def body(station_data, channel_mask, template_waves, pick_station, pick_lag):
    sta_size = lax.axis_size("sta")
    my_index = lax.axis_index("sta")
    group_size = pick_station.shape[0]
    station_count = channel_mask.shape[1]
    stations_here = station_data.shape[1]
    owners = pick_station // station_count
    order = lax.broadcasted_iota(jnp.int32, (group_size, group_size), 0)
    earlier = lax.broadcasted_iota(jnp.int32, (group_size, group_size), 1) < order

    column = lax.broadcasted_iota(jnp.int32, owners.shape, 1)
    own_owner = jnp.sum(jnp.where(column == my_index, owners, 0), axis=1)
    place = jnp.sum((earlier & (own_owner[:, None] == own_owner[None, :])).astype(jnp.int32), axis=1)
    slot_count = sta_size * CAP
    slot_rows = lax.broadcasted_iota(jnp.int32, (slot_count, group_size), 0)
    select = (slot_rows == (own_owner * CAP + place)[None, :]).astype(jnp.bfloat16)
    waves = template_waves.reshape(group_size, 3 * L)
    outgoing = jnp.dot(select, waves, preferred_element_type=jnp.float32).astype(jnp.bfloat16)
    received = lax.all_to_all(outgoing, "sta", split_axis=0, concat_axis=0, tiled=True)

    tiles = station_data.reshape(3, stations_here, BLOCKS, STEP).transpose(0, 1, 3, 2)
    tiles = jnp.pad(tiles, ((0, 0), (0, 0), (0, 0), (0, LANES - BLOCKS)))
    tiles = tiles.reshape(3 * stations_here, STEP, LANES)
    gathered = lax.all_gather(tiles, "tpl", axis=0, tiled=True)

    landing = owners == my_index
    arrival = jnp.dot(earlier.astype(jnp.bfloat16), landing.astype(jnp.bfloat16),
                      preferred_element_type=jnp.float32).astype(jnp.int32)
    template_ids = lax.broadcasted_iota(jnp.int32, owners.shape, 0)
    packed = VALID + (pick_lag << 9) + ((pick_station - my_index * station_count) << 5) + template_ids
    places = lax.broadcasted_iota(jnp.int32, (CAP,) + owners.shape, 0)
    meta = jnp.sum(jnp.where(landing[None] & (arrival[None] == places), packed[None], 0), axis=1)

    partial_sums = partial_stack(meta, channel_mask, gathered, received)
    sent = partial_sums.reshape(sta_size, -1, LANES)
    arrived = lax.all_to_all(sent, "sta", split_axis=0, concat_axis=0, tiled=True)
    return jnp.sum(arrived.astype(jnp.float32), axis=0).reshape(NT // sta_size, group_size)


def solution(mesh):
    in_specs = (
        P(None, ("sta", "tpl"), None),
        P(None, "sta"),
        P("tpl", "sta", None, None),
        P("tpl", None),
        P("tpl", None),
    )
    return jax.shard_map(body, mesh=mesh, in_specs=in_specs, out_specs=P("sta", "tpl"), check_vma=False)
```

```python
import jax
import jax.numpy as jnp
from jax import lax
from jax.experimental import pallas as pl
from jax.experimental.pallas import tpu as pltpu
from jax.sharding import PartitionSpec as P

NT = 1536
L = 640
LAGS = 1024
SAMPLES = 3200
CAP = 4
STEP = 32
LANES = 128
BLOCKS = SAMPLES // STEP
OUT_BLOCKS = NT // STEP
TILES = L // LANES
DEPTH = L + LANES
EPSILON = 1e-05
VALID = 1 << 20


def exclusive_prefix(values):
    groups = values.reshape(STEP // 8, 8, values.shape[-1])
    row = lax.broadcasted_iota(jnp.int32, groups.shape, 1)
    total = groups
    for shift in (1, 2, 4):
        total = total + jnp.where(row >= shift, pltpu.roll(total, shift, 1), 0.0)
    inner = jnp.where(row >= 1, pltpu.roll(total, 1, 1), 0.0)
    pieces = [inner[0]]
    carry = total[0, 7:8]
    for group in range(1, STEP // 8):
        pieces.append(inner[group] + carry)
        carry = carry + total[group, 7:8]
    return jnp.concatenate(pieces, axis=0)


def window_sums(values):
    width = values.shape[-1]
    span = L // STEP
    ahead = pltpu.roll(values, width - span, 1) - values
    two = jnp.sum(values, axis=0, keepdims=True)
    two = two + pltpu.roll(two, width - 1, 1)
    four = two + pltpu.roll(two, width - 2, 1)
    eight = four + pltpu.roll(four, width - 4, 1)
    sixteen = eight + pltpu.roll(eight, width - 8, 1)
    whole = sixteen + pltpu.roll(four, width - 16, 1)
    return whole + exclusive_prefix(ahead)


def kernel(meta_ref, mask_ref, *refs):
    *tile_refs, waves_ref, out_ref = refs[:-7]
    (frames, scales, units, acc, twice, dense, slots) = refs[-7:]
    peers = meta_ref.shape[1]

    def list_slot(slot, count):
        slots[count] = slot
        held = meta_ref[slot & (CAP - 1), slot >> 2] >> 20
        return count + held

    count = lax.fori_loop(0, peers * CAP, list_slot, jnp.int32(0))

    @pl.loop(0, peers * CAP // 16)
    def _(chunk):
        rows = pl.ds(pl.multiple_of(chunk * 16, 16), 16)
        for c in range(3):
            values = waves_ref[rows, c * L:(c + 1) * L].astype(jnp.float32)
            centred = values - jnp.mean(values, axis=-1, keepdims=True)
            power = jnp.mean(centred * centred, axis=-1, keepdims=True)
            unit = centred / jnp.sqrt(power + EPSILON)
            unit = unit.astype(jnp.bfloat16).astype(jnp.float32)
            for tile in range(TILES):
                units[c * TILES + tile, rows, :] = unit[:, tile * LANES:(tile + 1) * LANES]

    here = mask_ref[0, 0] >> 1
    for hop, tile_ref in enumerate(tile_refs):
        owner = (here - hop) & (len(tile_refs) - 1)

        @pl.loop(0, tile_ref.shape[0])
        def _(within):
            record = owner * 6 + within
            tile = tile_ref[within]
            for turn in range(DEPTH // STEP):
                rolled = tile if turn == 0 else pltpu.roll(tile, LANES - turn, 1)
                frames[record, turn * STEP:(turn + 1) * STEP, :] = rolled.astype(jnp.bfloat16)
            mean_one = window_sums(tile) * (1.0 / L)
            mean_two = window_sums(tile * tile) * (1.0 / L)
            weight = (mask_ref[within >> 1, owner * 2 + (within & 1)] & 1).astype(jnp.float32)
            spread = L * jnp.sqrt(mean_two - mean_one * mean_one + EPSILON)
            scales[record] = weight / spread

    acc[...] = jnp.zeros_like(acc)
    row = lax.broadcasted_iota(jnp.int32, (STEP, LANES), 0)
    lane = lax.broadcasted_iota(jnp.int32, (STEP, LANES), 1)
    own = lane >= row
    lane_used = lane < BLOCKS - L // STEP

    @pl.loop(0, count)
    def _(index):
        slot = slots[index]
        packed = meta_ref[slot & (CAP - 1), slot >> 2]
        template = packed & 31
        station = (packed >> 5) & 15
        lag = (packed >> 9) & 2047
        total = jnp.zeros((STEP, LANES), jnp.float32)
        for c in range(3):
            record = (station >> 1) * 6 + 2 * c + (station & 1)
            before = jnp.zeros((STEP, LANES), jnp.float32)
            columns = []
            for tile in range(TILES):
                wave = units[c * TILES + tile, pl.ds(slot, STEP, stride=0), :]
                spread = pltpu.roll(wave, 0, 1, stride=1, stride_axis=0)
                columns.append(jnp.where(own, spread, before).astype(jnp.bfloat16))
                before = spread
            columns.append(jnp.where(own, 0.0, before).astype(jnp.bfloat16))
            toeplitz = jnp.concatenate(columns, axis=1)
            product = jnp.dot(toeplitz, frames[record], preferred_element_type=jnp.float32)
            total = total + product * scales[record]
        total = jnp.where(lane_used, total, 0.0)
        first = pltpu.roll(total, LANES - (lag >> 5), 1)
        twice[0:STEP, :] = first
        twice[STEP:2 * STEP, :] = pltpu.roll(first, LANES - 1, 1)
        rows = pl.ds(pl.multiple_of(template * STEP, STEP), STEP)
        acc[rows, :] += twice[pl.ds(lag & (STEP - 1), STEP), :]

    for group in range(STEP // 4):
        parts = [acc[pl.ds(4 * group + j, STEP, stride=STEP), :] for j in range(4)]
        turned = jnp.concatenate(parts, axis=0).T
        dense[pl.ds(group, OUT_BLOCKS, stride=8), :] = turned[:OUT_BLOCKS]
    for part in range(out_ref.shape[1] // LANES):
        rows = dense[pl.ds(part, out_ref.shape[0], stride=3), :]
        out_ref[:, part * LANES:(part + 1) * LANES] = rows.astype(out_ref.dtype)


def partial_stack(meta, mask, tiles, received):
    group_size = meta.shape[1]
    slot_count = received.shape[0]
    records = len(tiles) * tiles[0].shape[0]
    return pl.pallas_call(
        kernel,
        out_shape=jax.ShapeDtypeStruct((slot_count, NT * group_size // slot_count), jnp.bfloat16),
        in_specs=[
            pl.BlockSpec(memory_space=pltpu.SMEM),
            pl.BlockSpec(memory_space=pltpu.SMEM),
        ] + [pl.BlockSpec(memory_space=pltpu.VMEM)] * (len(tiles) + 1),
        out_specs=pl.BlockSpec(memory_space=pltpu.VMEM),
        scratch_shapes=[
            pltpu.VMEM((records, DEPTH, LANES), jnp.bfloat16),
            pltpu.VMEM((records, STEP, LANES), jnp.float32),
            pltpu.VMEM((3 * TILES, slot_count, LANES), jnp.float32),
            pltpu.VMEM((group_size * STEP, LANES), jnp.float32),
            pltpu.VMEM((2 * STEP, LANES), jnp.float32),
            pltpu.VMEM((NT * group_size // LANES, LANES), jnp.float32),
            pltpu.SMEM((slot_count + 1,), jnp.int32),
        ],
        compiler_params=pltpu.CompilerParams(vmem_limit_bytes=40 * 1024 * 1024),
        name="matched_filter",
    )(meta, mask, *tiles, received)


def body(station_data, channel_mask, template_waves, pick_station, pick_lag):
    sta_size = lax.axis_size("sta")
    my_index = lax.axis_index("sta")
    group_size = pick_station.shape[0]
    station_count = channel_mask.shape[1]
    stations_here = station_data.shape[1]
    owners = pick_station // station_count
    order = lax.broadcasted_iota(jnp.int32, (group_size, group_size), 0)
    earlier = lax.broadcasted_iota(jnp.int32, (group_size, group_size), 1) < order

    column = lax.broadcasted_iota(jnp.int32, owners.shape, 1)
    own_owner = jnp.sum(jnp.where(column == my_index, owners, 0), axis=1)
    place = jnp.sum((earlier & (own_owner[:, None] == own_owner[None, :])).astype(jnp.int32), axis=1)
    slot_count = sta_size * CAP
    slot_rows = lax.broadcasted_iota(jnp.int32, (slot_count, group_size), 0)
    select = (slot_rows == (own_owner * CAP + place)[None, :]).astype(jnp.bfloat16)
    waves = template_waves.reshape(group_size, 3 * L)
    outgoing = jnp.dot(select, waves, preferred_element_type=jnp.float32).astype(jnp.bfloat16)
    received = lax.all_to_all(outgoing, "sta", split_axis=0, concat_axis=0, tiled=True)

    tiles = station_data.reshape(3, stations_here, BLOCKS, STEP).transpose(0, 1, 3, 2)
    tiles = jnp.pad(tiles, ((0, 0), (0, 0), (0, 0), (0, LANES - BLOCKS)))
    tiles = tiles.reshape(3 * stations_here, STEP, LANES)
    tpl_size = lax.axis_size("tpl")
    held = [tiles]
    for hop in range(1, tpl_size):
        held.append(lax.ppermute(tiles, "tpl", [(i, (i + hop) % tpl_size) for i in range(tpl_size)]))
    mask = channel_mask + 2 * lax.axis_index("tpl")

    landing = owners == my_index
    arrival = jnp.dot(earlier.astype(jnp.bfloat16), landing.astype(jnp.bfloat16),
                      preferred_element_type=jnp.float32).astype(jnp.int32)
    template_ids = lax.broadcasted_iota(jnp.int32, owners.shape, 0)
    packed = VALID + (pick_lag << 9) + ((pick_station - my_index * station_count) << 5) + template_ids
    places = lax.broadcasted_iota(jnp.int32, (CAP,) + owners.shape, 0)
    meta = jnp.sum(jnp.where(landing[None] & (arrival[None] == places), packed[None], 0), axis=1)

    partial_sums = partial_stack(meta, mask, held, received)
    arrived = lax.all_to_all(partial_sums, "sta", split_axis=0, concat_axis=0, tiled=True)
    arrived = arrived.reshape(sta_size, CAP, -1).astype(jnp.float32)
    return jnp.sum(arrived, axis=0).reshape(NT // sta_size, group_size)


def solution(mesh):
    in_specs = (
        P(None, ("sta", "tpl"), None),
        P(None, "sta"),
        P("tpl", "sta", None, None),
        P("tpl", None),
        P("tpl", None),
    )
    return jax.shard_map(body, mesh=mesh, in_specs=in_specs, out_specs=P("sta", "tpl"), check_vma=False)
```

```python
import jax
import jax.numpy as jnp
from jax import lax
from jax.experimental import pallas as pl
from jax.experimental.pallas import tpu as pltpu
from jax.sharding import PartitionSpec as P

NT = 1536
L = 640
LAGS = 1024
SAMPLES = 3200
CAP = 4
STEP = 32
LANES = 128
BLOCKS = SAMPLES // STEP
OUT_BLOCKS = NT // STEP
TILES = L // LANES
TURNS = 8
UNROLL = 2
STATION_BITS = 4
EPSILON = 1e-05
VALID = 1 << 20


def exclusive_prefix(values):
    lanes = values.shape[-1]
    groups = values.reshape(-1, 8, lanes)
    row = lax.broadcasted_iota(jnp.int32, groups.shape, 1)
    total = groups
    for shift in (1, 2, 4):
        total = total + jnp.where(row >= shift, pltpu.roll(total, shift, 1), 0.0)
    inner = jnp.where(row >= 1, pltpu.roll(total, 1, 1), 0.0).reshape(-1, STEP // 8, 8, lanes)
    last = total.reshape(-1, STEP // 8, 8, lanes)[:, :, 7:8]
    pieces = [inner[:, 0:1]]
    carry = last[:, 0:1]
    for group in range(1, STEP // 8):
        pieces.append(inner[:, group:group + 1] + carry)
        carry = carry + last[:, group:group + 1]
    return jnp.concatenate(pieces, axis=1).reshape(values.shape)


def window_sums(values):
    width = values.shape[-1]
    span = L // STEP
    ahead = pltpu.roll(values, width - span, 1) - values
    two = jnp.sum(values.reshape(-1, STEP, width), axis=1)
    two = two + pltpu.roll(two, width - 1, 1)
    four = two + pltpu.roll(two, width - 2, 1)
    eight = four + pltpu.roll(four, width - 4, 1)
    sixteen = eight + pltpu.roll(eight, width - 8, 1)
    whole = sixteen + pltpu.roll(four, width - 16, 1)
    inner = exclusive_prefix(ahead).reshape(-1, STEP, width)
    return whole[:, None, :] + inner


def select_kernel(index_ref, station_ref, waves_ref, out_ref):
    group_size = station_ref.shape[0]
    square = (group_size, group_size)
    row = lax.broadcasted_iota(jnp.int32, square, 0)
    column = lax.broadcasted_iota(jnp.int32, square, 1)
    owners = station_ref[...] >> STATION_BITS
    down = jnp.sum(jnp.where(column == index_ref[0], owners, 0), axis=1, keepdims=True)
    down = jnp.broadcast_to(down, square)
    across = jnp.sum(jnp.where(row == column, down, 0), axis=0, keepdims=True)
    same = (down == across) & (row < column)
    place = jnp.sum(same.astype(jnp.int32), axis=0, keepdims=True)
    slot = across * CAP + place
    slots = lax.broadcasted_iota(jnp.int32, (out_ref.shape[0], group_size), 0)
    select = (slots == slot).astype(jnp.float32).astype(jnp.bfloat16)
    for c in range(3):
        values = waves_ref[c].astype(jnp.float32)
        centred = values - jnp.mean(values, axis=-1, keepdims=True)
        power = jnp.mean(centred * centred, axis=-1, keepdims=True)
        unit = (centred / jnp.sqrt(power + EPSILON)).astype(jnp.bfloat16)
        picked = jnp.dot(select, unit, preferred_element_type=jnp.float32)
        out_ref[:, c * L:(c + 1) * L] = picked.astype(jnp.bfloat16)


def records_kernel(meta_ref, mask_ref, *refs):
    *tile_refs, frames, scales, slots = refs

    def list_slot(slot, count):
        slots[count] = slot
        held = meta_ref[slot & (CAP - 1), slot >> 2] >> 20
        return count + held

    total = meta_ref.shape[1] * CAP
    count = lax.fori_loop(0, total, list_slot, jnp.int32(0))
    slots[count] = -1
    slots[total + 1] = count

    here = mask_ref[0, 0] >> 1
    for hop, tile_ref in enumerate(tile_refs):
        owner = (here - hop) & (len(tile_refs) - 1)
        size = tile_ref.shape[0]
        first = owner * size
        values = tile_ref[...].reshape(size * STEP, LANES)
        for turn in range(TURNS):
            rolled = values if turn == 0 else pltpu.roll(values, LANES - turn, 1)
            frames[pl.ds(first, size), turn * STEP:(turn + 1) * STEP, :] = (
                rolled.astype(jnp.bfloat16).reshape(size, STEP, LANES)
            )
        mean_one = window_sums(values) * (1.0 / L)
        mean_two = window_sums(values * values) * (1.0 / L)
        spread = L * jnp.sqrt(mean_two - mean_one * mean_one + EPSILON)
        for within in range(size):
            weight = (mask_ref[within >> 1, owner * 2 + (within & 1)] & 1).astype(jnp.float32)
            scales[first + within] = weight / spread[within]


def stack_kernel(meta_ref, slots, frames, scales, waves_ref, out_ref, units, acc, twice, dense):
    slot_count = waves_ref.shape[0]
    count = slots[slot_count + 1]
    for start in range(3 * TILES):
        units[start] = waves_ref[:, start * LANES:(start + 1) * LANES].astype(jnp.float32)
    acc[...] = jnp.zeros_like(acc)
    row = lax.broadcasted_iota(jnp.int32, (STEP, LANES), 0)
    lane = lax.broadcasted_iota(jnp.int32, (STEP, LANES), 1)
    own = lane >= row

    def one_pick(slot, spare):
        held = slot >= 0
        slot = jnp.maximum(slot, 0)
        packed = meta_ref[slot & (CAP - 1), slot >> 2]
        template = jnp.where(held, packed & 31, acc.shape[0] // STEP - 1)
        station = (packed >> 5) & 15
        lag = (packed >> 9) & 2047
        total = jnp.zeros((STEP, LANES), jnp.float32)
        for c in range(3):
            record = (station >> 1) * 6 + 2 * c + (station & 1)
            before = jnp.zeros((STEP, LANES), jnp.float32)
            columns = []
            for tile in range(TILES):
                wave = units[c * TILES + tile, pl.ds(slot, STEP, stride=0), :]
                spread = pltpu.roll(wave, 0, 1, stride=1, stride_axis=0)
                columns.append(jnp.where(own, spread, before).astype(jnp.bfloat16))
                before = spread
            columns.append(jnp.where(own, 0.0, before).astype(jnp.bfloat16))
            left = jnp.concatenate(
                [jnp.concatenate(columns[i:i + 2], axis=1) for i in range(0, TILES + 1, 2)], axis=0
            )
            product = jnp.dot(left, frames[record], preferred_element_type=jnp.float32)
            summed = product[:STEP]
            for part in range(1, (TILES + 1) // 2):
                later = product[part * STEP:(part + 1) * STEP]
                summed = summed + pltpu.roll(later, LANES - TURNS * part, 1)
            total = total + summed * scales[record]
        first = pltpu.roll(total, LANES - (lag >> 5), 1)
        twice[spare, 0:STEP, :] = first
        twice[spare, STEP:2 * STEP, :] = pltpu.roll(first, LANES - 1, 1)
        shifted = twice[spare, pl.ds(lag & (STEP - 1), STEP), :]
        return pl.ds(pl.multiple_of(template * STEP, STEP), STEP), shifted

    @pl.loop(0, (count + UNROLL - 1) // UNROLL)
    def _(index):
        done = [one_pick(slots[index * UNROLL + spare], spare) for spare in range(UNROLL)]
        for rows, shifted in done:
            acc[rows, :] += shifted

    for group in range(STEP // 4):
        parts = [acc[pl.ds(4 * group + j, STEP, stride=STEP), :] for j in range(4)]
        turned = jnp.concatenate(parts, axis=0).T
        dense[pl.ds(group, OUT_BLOCKS, stride=8), :] = turned[:OUT_BLOCKS]
    for part in range(out_ref.shape[1] // LANES):
        rows = dense[pl.ds(part, out_ref.shape[0], stride=3), :]
        out_ref[:, part * LANES:(part + 1) * LANES] = rows.astype(out_ref.dtype)


SMEM = pl.BlockSpec(memory_space=pltpu.SMEM)
VMEM = pl.BlockSpec(memory_space=pltpu.VMEM)


def slot_waves(my_index, pick_station, template_waves, slot_count):
    return pl.pallas_call(
        select_kernel,
        out_shape=jax.ShapeDtypeStruct((slot_count, 3 * L), jnp.bfloat16),
        in_specs=[SMEM, VMEM, VMEM],
        out_specs=VMEM,
        name="select_waves",
    )(my_index.reshape(1), pick_station, template_waves)


def frames_and_scales(meta, mask, tiles):
    records = len(tiles) * tiles[0].shape[0]
    slot_count = meta.size
    return pl.pallas_call(
        records_kernel,
        out_shape=(
            jax.ShapeDtypeStruct((records, TURNS * STEP, LANES), jnp.bfloat16),
            jax.ShapeDtypeStruct((records, STEP, LANES), jnp.float32),
            jax.ShapeDtypeStruct((slot_count + 2,), jnp.int32),
        ),
        in_specs=[SMEM, SMEM] + [VMEM] * len(tiles),
        out_specs=(VMEM, VMEM, SMEM),
        compiler_params=pltpu.CompilerParams(vmem_limit_bytes=16 * 1024 * 1024),
        cost_estimate=pl.CostEstimate(flops=20_000_000, transcendentals=200_000, bytes_accessed=5_000_000),
        name="frames_and_scales",
    )(meta, mask, *tiles)


def partial_stack(meta, slots, frames, scales, received):
    group_size = meta.shape[1]
    slot_count = received.shape[0]
    rows = NT * group_size // LANES
    return pl.pallas_call(
        stack_kernel,
        out_shape=jax.ShapeDtypeStruct((slot_count, rows * LANES // slot_count), jnp.bfloat16),
        in_specs=[SMEM, SMEM, VMEM, VMEM, VMEM],
        out_specs=VMEM,
        scratch_shapes=[
            pltpu.VMEM((3 * TILES, slot_count, LANES), jnp.float32),
            pltpu.VMEM(((group_size + 1) * STEP, LANES), jnp.float32),
            pltpu.VMEM((UNROLL, 2 * STEP, LANES), jnp.float32),
            pltpu.VMEM((rows, LANES), jnp.float32),
        ],
        compiler_params=pltpu.CompilerParams(vmem_limit_bytes=20 * 1024 * 1024),
        cost_estimate=pl.CostEstimate(flops=200_000_000, transcendentals=0, bytes_accessed=8_000_000),
        name="stack_picks",
    )(meta, slots, frames, scales, received)


def body(station_data, channel_mask, template_waves, pick_station, pick_lag):
    sta_size = lax.axis_size("sta")
    tpl_size = lax.axis_size("tpl")
    my_index = lax.axis_index("sta")
    group_size = pick_station.shape[0]
    station_count = channel_mask.shape[1]
    stations_here = station_data.shape[1]

    waves = template_waves.reshape(group_size, 3, L).transpose(1, 0, 2)
    outgoing = slot_waves(my_index, pick_station, waves, sta_size * CAP)
    received = lax.all_to_all(outgoing, "sta", split_axis=0, concat_axis=0, tiled=True)

    tiles = station_data.reshape(3, stations_here, BLOCKS, STEP).transpose(0, 1, 3, 2)
    tiles = jnp.pad(tiles, ((0, 0), (0, 0), (0, 0), (0, LANES - BLOCKS)))
    tiles = tiles.reshape(3 * stations_here, STEP, LANES)
    held = [tiles]
    for hop in range(1, tpl_size):
        held.append(lax.ppermute(tiles, "tpl", [(i, (i + hop) % tpl_size) for i in range(tpl_size)]))
    mask = channel_mask + 2 * lax.axis_index("tpl")

    owners = pick_station // station_count
    order = lax.broadcasted_iota(jnp.int32, (group_size, group_size), 0)
    earlier = lax.broadcasted_iota(jnp.int32, (group_size, group_size), 1) < order
    landing = owners == my_index
    arrival = jnp.dot(earlier.astype(jnp.bfloat16), landing.astype(jnp.bfloat16),
                      preferred_element_type=jnp.float32).astype(jnp.int32)
    template_ids = lax.broadcasted_iota(jnp.int32, owners.shape, 0)
    packed = VALID + (pick_lag << 9) + ((pick_station - my_index * station_count) << 5) + template_ids
    places = lax.broadcasted_iota(jnp.int32, (CAP,) + owners.shape, 0)
    meta = jnp.sum(jnp.where(landing[None] & (arrival[None] == places), packed[None], 0), axis=1)

    frames, scales, slots = frames_and_scales(meta, mask, held)
    partial_sums = partial_stack(meta, slots, frames, scales, received)
    arrived = lax.all_to_all(partial_sums, "sta", split_axis=0, concat_axis=0, tiled=True)
    arrived = arrived.reshape(sta_size, CAP, -1).astype(jnp.float32)
    return jnp.sum(arrived, axis=0).reshape(NT // sta_size, group_size)


def solution(mesh):
    in_specs = (
        P(None, ("sta", "tpl"), None),
        P(None, "sta"),
        P("tpl", "sta", None, None),
        P("tpl", None),
        P("tpl", None),
    )
    return jax.shard_map(body, mesh=mesh, in_specs=in_specs, out_specs=P("sta", "tpl"), check_vma=False)
```

```python
import jax
import jax.numpy as jnp
from jax import lax
from jax.experimental import pallas as pl
from jax.experimental.pallas import tpu as pltpu
from jax.sharding import PartitionSpec as P

NT = 1536
L = 640
LAGS = 1024
SAMPLES = 3200
CAP = 4
STEP = 32
LANES = 128
BLOCKS = SAMPLES // STEP
OUT_BLOCKS = NT // STEP
TILES = L // LANES
TURNS = 8
UNROLL = 8
SLOT_ROWS = 64
STATION_BITS = 4
EPSILON = 1e-05
VALID = 1 << 20


def exclusive_prefix(values):
    lanes = values.shape[-1]
    groups = values.reshape(-1, 8, lanes)
    row = lax.broadcasted_iota(jnp.int32, groups.shape, 1)
    total = groups
    for shift in (1, 2, 4):
        total = total + jnp.where(row >= shift, pltpu.roll(total, shift, 1), 0.0)
    inner = jnp.where(row >= 1, pltpu.roll(total, 1, 1), 0.0).reshape(-1, STEP // 8, 8, lanes)
    last = total.reshape(-1, STEP // 8, 8, lanes)[:, :, 7:8]
    pieces = [inner[:, 0:1]]
    carry = last[:, 0:1]
    for group in range(1, STEP // 8):
        pieces.append(inner[:, group:group + 1] + carry)
        carry = carry + last[:, group:group + 1]
    return jnp.concatenate(pieces, axis=1).reshape(values.shape)


def window_sums(values):
    width = values.shape[-1]
    span = L // STEP
    ahead = pltpu.roll(values, width - span, 1) - values
    two = jnp.sum(values.reshape(-1, STEP, width), axis=1)
    two = two + pltpu.roll(two, width - 1, 1)
    four = two + pltpu.roll(two, width - 2, 1)
    eight = four + pltpu.roll(four, width - 4, 1)
    sixteen = eight + pltpu.roll(eight, width - 8, 1)
    whole = sixteen + pltpu.roll(four, width - 16, 1)
    inner = exclusive_prefix(ahead).reshape(-1, STEP, width)
    return whole[:, None, :] + inner


def select_kernel(index_ref, station_ref, waves_ref, out_ref, staged):
    group_size = station_ref.shape[0]
    square = (group_size, group_size)
    row = lax.broadcasted_iota(jnp.int32, square, 0)
    column = lax.broadcasted_iota(jnp.int32, square, 1)
    owners = station_ref[...] >> STATION_BITS
    down = jnp.sum(jnp.where(column == index_ref[0], owners, 0), axis=1, keepdims=True)
    down = jnp.broadcast_to(down, square)
    across = jnp.sum(jnp.where(row == column, down, 0), axis=0, keepdims=True)
    same = (down == across) & (row < column)
    place = jnp.sum(same.astype(jnp.int32), axis=0, keepdims=True)
    slot = across * CAP + place
    peers = out_ref.shape[0]
    peer = lax.broadcasted_iota(jnp.int32, (peers, group_size), 0)
    selects = [(peer * CAP + k == slot).astype(jnp.float32).astype(jnp.bfloat16) for k in range(CAP)]
    select = jnp.concatenate(selects, axis=0)
    for c in range(3):
        values = waves_ref[c].astype(jnp.float32)
        centred = values - jnp.mean(values, axis=-1, keepdims=True)
        power = jnp.mean(centred * centred, axis=-1, keepdims=True)
        unit = (centred / jnp.sqrt(power + EPSILON)).astype(jnp.bfloat16)
        picked = jnp.dot(select, unit, preferred_element_type=jnp.float32)
        for tile in range(TILES):
            columns = slice(tile * LANES, (tile + 1) * LANES)
            for k in range(CAP):
                at = (c * TILES + tile) * CAP + k
                staged[pl.ds(at, peers, stride=SLOT_ROWS), :] = picked[k * peers:(k + 1) * peers, columns]
    for at in range(3 * TILES * CAP, SLOT_ROWS):
        staged[pl.ds(at, peers, stride=SLOT_ROWS), :] = jnp.zeros((peers, LANES), jnp.float32)
    out_ref[...] = staged[...].astype(jnp.bfloat16).reshape(out_ref.shape)


def records_kernel(meta_ref, mask_ref, *refs):
    *tile_refs, frames, scales, slots = refs

    def list_slot(slot, count):
        slots[count] = slot
        held = meta_ref[slot & (CAP - 1), slot >> 2] >> 20
        return count + held

    total = meta_ref.shape[1] * CAP
    count = lax.fori_loop(0, total, list_slot, jnp.int32(0), unroll=16)
    for spare in range(UNROLL):
        slots[count + spare] = -1
    slots[total + UNROLL] = count

    here = mask_ref[0, 0] >> 1
    for core, tile_ref in enumerate(tile_refs):
        size = 6
        for hop in range(tile_ref.shape[0] // size):
            owner = ((here - 2 * hop) & (2 * (tile_ref.shape[0] // size) - 1)) ^ core
            first = owner * size
            values = tile_ref[hop * size:(hop + 1) * size].reshape(size * STEP, LANES)
            for turn in range(TURNS):
                rolled = values if turn == 0 else pltpu.roll(values, LANES - turn, 1)
                frames[pl.ds(first, size), turn * STEP:(turn + 1) * STEP, :] = (
                    rolled.astype(jnp.bfloat16).reshape(size, STEP, LANES)
                )
            mean_one = window_sums(values) * (1.0 / L)
            mean_two = window_sums(values * values) * (1.0 / L)
            factor = lax.rsqrt(mean_two - mean_one * mean_one + EPSILON)
            for within in range(size):
                weight = mask_ref[within >> 1, owner * 2 + (within & 1)] & 1
                weight = weight.astype(jnp.float32) * (1.0 / L)
                scales[first + within] = factor[within] * weight


def stack_kernel(meta_ref, slots, frames, scales, waves_ref, out_ref, units, acc, twice, dense):
    count = slots[slots.shape[0] - 1]
    units[...] = waves_ref[...].reshape(units.shape).astype(jnp.float32)
    acc[...] = jnp.zeros_like(acc)
    row = lax.broadcasted_iota(jnp.int32, (STEP, LANES), 0)
    lane = lax.broadcasted_iota(jnp.int32, (STEP, LANES), 1)
    own = lane >= row

    def one_pick(slot, spare):
        held = slot >= 0
        slot = jnp.maximum(slot, 0)
        packed = meta_ref[slot & (CAP - 1), slot >> 2]
        template = jnp.where(held, packed & 31, acc.shape[0] // STEP - 1)
        station = (packed >> 5) & 15
        lag = (packed >> 9) & 2047
        total = jnp.zeros((STEP, LANES), jnp.float32)
        for c in range(3):
            record = (station >> 1) * 6 + 2 * c + (station & 1)
            before = jnp.zeros((STEP, LANES), jnp.float32)
            columns = []
            for tile in range(TILES):
                at = (slot >> 2) * SLOT_ROWS + (c * TILES + tile) * CAP + (slot & (CAP - 1))
                wave = units[pl.ds(at, STEP, stride=0), :]
                spread = pltpu.roll(wave, 0, 1, stride=1, stride_axis=0)
                columns.append(jnp.where(own, spread, before).astype(jnp.bfloat16))
                before = spread
            columns.append(jnp.where(own, 0.0, before).astype(jnp.bfloat16))
            left = jnp.concatenate(
                [jnp.concatenate(columns[i:i + 2], axis=1) for i in range(0, TILES + 1, 2)], axis=0
            )
            product = jnp.dot(left, frames[record], preferred_element_type=jnp.float32)
            summed = product[:STEP]
            for part in range(1, (TILES + 1) // 2):
                later = product[part * STEP:(part + 1) * STEP]
                summed = summed + pltpu.roll(later, LANES - TURNS * part, 1)
            total = total + summed * scales[record]
        first = pltpu.roll(total, LANES - (lag >> 5), 1)
        twice[spare, 0:STEP, :] = first
        twice[spare, STEP:2 * STEP, :] = pltpu.roll(first, LANES - 1, 1)
        shifted = twice[spare, pl.ds(lag & (STEP - 1), STEP), :]
        return pl.ds(pl.multiple_of(template * STEP, STEP), STEP), shifted

    @pl.loop(0, (count + UNROLL - 1) // UNROLL)
    def _(index):
        done = [one_pick(slots[index * UNROLL + spare], spare) for spare in range(UNROLL)]
        for rows, shifted in done:
            acc[rows, :] += shifted

    for group in range(STEP // 4):
        parts = [acc[pl.ds(4 * group + j, STEP, stride=STEP), :] for j in range(4)]
        turned = jnp.concatenate(parts, axis=0).T
        dense[pl.ds(group, OUT_BLOCKS, stride=8), :] = turned[:OUT_BLOCKS]
    for part in range(out_ref.shape[1] // LANES):
        rows = dense[pl.ds(part, out_ref.shape[0], stride=3), :]
        out_ref[:, part * LANES:(part + 1) * LANES] = rows.astype(out_ref.dtype)


SMEM = pl.BlockSpec(memory_space=pltpu.SMEM)
VMEM = pl.BlockSpec(memory_space=pltpu.VMEM)


def slot_waves(my_index, pick_station, template_waves, peers):
    return pl.pallas_call(
        select_kernel,
        out_shape=jax.ShapeDtypeStruct((peers, SLOT_ROWS, LANES), jnp.bfloat16),
        in_specs=[SMEM, VMEM, VMEM],
        out_specs=VMEM,
        scratch_shapes=[pltpu.VMEM((peers * SLOT_ROWS, LANES), jnp.float32)],
        compiler_params=pltpu.CompilerParams(vmem_limit_bytes=4 * 1024 * 1024),
        cost_estimate=pl.CostEstimate(flops=16_000_000, transcendentals=100, bytes_accessed=620_000),
        name="select_waves",
    )(my_index.reshape(1), pick_station, template_waves)


def frames_and_scales(meta, mask, tiles):
    records = len(tiles) * tiles[0].shape[0]
    slot_count = meta.size
    return pl.pallas_call(
        records_kernel,
        out_shape=(
            jax.ShapeDtypeStruct((records, TURNS * STEP, LANES), jnp.bfloat16),
            jax.ShapeDtypeStruct((records, STEP, LANES), jnp.float32),
            jax.ShapeDtypeStruct((slot_count + UNROLL + 1,), jnp.int32),
        ),
        in_specs=[SMEM, SMEM] + [VMEM] * len(tiles),
        out_specs=(VMEM, VMEM, SMEM),
        compiler_params=pltpu.CompilerParams(vmem_limit_bytes=10 * 1024 * 1024),
        cost_estimate=pl.CostEstimate(flops=20_000_000, transcendentals=200_000, bytes_accessed=5_000_000),
        name="frames_and_scales",
    )(meta, mask, *tiles)


def partial_stack(meta, slots, frames, scales, received):
    group_size = meta.shape[1]
    slot_count = received.shape[0] * CAP
    rows = NT * group_size // LANES
    return pl.pallas_call(
        stack_kernel,
        out_shape=jax.ShapeDtypeStruct((slot_count, rows * LANES // slot_count), jnp.bfloat16),
        in_specs=[SMEM, SMEM, VMEM, VMEM, VMEM],
        out_specs=VMEM,
        scratch_shapes=[
            pltpu.VMEM((received.shape[0] * SLOT_ROWS, LANES), jnp.float32),
            pltpu.VMEM(((group_size + 1) * STEP, LANES), jnp.float32),
            pltpu.VMEM((UNROLL, 2 * STEP, LANES), jnp.float32),
            pltpu.VMEM((rows, LANES), jnp.float32),
        ],
        compiler_params=pltpu.CompilerParams(vmem_limit_bytes=10 * 1024 * 1024),
        cost_estimate=pl.CostEstimate(flops=200_000_000, transcendentals=0, bytes_accessed=8_000_000),
        name="stack_picks",
    )(meta, slots, frames, scales, received)


def body(station_data, channel_mask, template_waves, pick_station, pick_lag):
    sta_size = lax.axis_size("sta")
    tpl_size = lax.axis_size("tpl")
    my_index = lax.axis_index("sta")
    group_size = pick_station.shape[0]
    station_count = channel_mask.shape[1]
    stations_here = station_data.shape[1]

    waves = template_waves.reshape(group_size, 3, L).transpose(1, 0, 2)
    outgoing = slot_waves(my_index, pick_station, waves, sta_size)
    received = lax.all_to_all(outgoing, "sta", split_axis=0, concat_axis=0, tiled=True)

    tiles = station_data.reshape(3, stations_here, BLOCKS, STEP).transpose(0, 1, 3, 2)
    tiles = jnp.pad(tiles, ((0, 0), (0, 0), (0, 0), (0, LANES - BLOCKS)))
    tiles = tiles.reshape(3 * stations_here, STEP, LANES)
    row = [tiles]
    for hop in range(2, tpl_size, 2):
        row.append(lax.ppermute(tiles, "tpl", [(i, (i + hop) % tpl_size) for i in range(tpl_size)]))
    row = jnp.concatenate(row, axis=0)
    held = [row, lax.ppermute(row, "tpl", [(i, i ^ 1) for i in range(tpl_size)])]
    mask = channel_mask + 2 * lax.axis_index("tpl")

    owners = pick_station // station_count
    order = lax.broadcasted_iota(jnp.int32, (group_size, group_size), 0)
    earlier = lax.broadcasted_iota(jnp.int32, (group_size, group_size), 1) < order
    landing = owners == my_index
    arrival = jnp.dot(earlier.astype(jnp.bfloat16), landing.astype(jnp.bfloat16),
                      preferred_element_type=jnp.float32).astype(jnp.int32)
    template_ids = lax.broadcasted_iota(jnp.int32, owners.shape, 0)
    packed = VALID + (pick_lag << 9) + ((pick_station - my_index * station_count) << 5) + template_ids
    places = lax.broadcasted_iota(jnp.int32, (CAP,) + owners.shape, 0)
    meta = jnp.sum(jnp.where(landing[None] & (arrival[None] == places), packed[None], 0), axis=1)

    frames, scales, slots = frames_and_scales(meta, mask, held)
    partial_sums = partial_stack(meta, slots, frames, scales, received)
    arrived = lax.all_to_all(partial_sums, "sta", split_axis=0, concat_axis=0, tiled=True)
    arrived = arrived.reshape(sta_size, CAP, -1).astype(jnp.float32)
    return jnp.sum(arrived, axis=0).reshape(NT // sta_size, group_size)


def solution(mesh):
    in_specs = (
        P(None, ("sta", "tpl"), None),
        P(None, "sta"),
        P("tpl", "sta", None, None),
        P("tpl", None),
        P("tpl", None),
    )
    return jax.shard_map(body, mesh=mesh, in_specs=in_specs, out_specs=P("sta", "tpl"), check_vma=False)
```

```python
import jax
import jax.numpy as jnp
from jax import lax
from jax.experimental import pallas as pl
from jax.experimental.pallas import tpu as pltpu
from jax.sharding import PartitionSpec as P

NT = 1536
L = 640
LAGS = 1024
SAMPLES = 3200
CAP = 4
STEP = 32
LANES = 128
BLOCKS = SAMPLES // STEP
OUT_BLOCKS = NT // STEP
TILES = L // LANES
TURNS = 8
UNROLL = 8
SLOT_ROWS = 64
RECORDS = 6
STATION_BITS = 4
EPSILON = 1e-05
VALID = 1 << 20


def exclusive_prefix(values):
    lanes = values.shape[-1]
    groups = values.reshape(-1, 8, lanes)
    row = lax.broadcasted_iota(jnp.int32, groups.shape, 1)
    total = groups
    for shift in (1, 2, 4):
        total = total + jnp.where(row >= shift, pltpu.roll(total, shift, 1), 0.0)
    inner = jnp.where(row >= 1, pltpu.roll(total, 1, 1), 0.0).reshape(-1, STEP // 8, 8, lanes)
    last = total.reshape(-1, STEP // 8, 8, lanes)[:, :, 7:8]
    pieces = [inner[:, 0:1]]
    carry = last[:, 0:1]
    for group in range(1, STEP // 8):
        pieces.append(inner[:, group:group + 1] + carry)
        carry = carry + last[:, group:group + 1]
    return jnp.concatenate(pieces, axis=1).reshape(values.shape)


def window_sums(values):
    width = values.shape[-1]
    span = L // STEP
    ahead = pltpu.roll(values, width - span, 1) - values
    two = jnp.sum(values.reshape(-1, STEP, width), axis=1)
    two = two + pltpu.roll(two, width - 1, 1)
    four = two + pltpu.roll(two, width - 2, 1)
    eight = four + pltpu.roll(four, width - 4, 1)
    sixteen = eight + pltpu.roll(eight, width - 8, 1)
    whole = sixteen + pltpu.roll(four, width - 16, 1)
    inner = exclusive_prefix(ahead).reshape(-1, STEP, width)
    return whole[:, None, :] + inner


def scales_kernel(index_ref, mask_hbm, tiles_ref, out_ref, mask_ref, sem):
    copy = pltpu.make_async_copy(mask_hbm, mask_ref, sem)
    copy.start()
    size = tiles_ref.shape[0]
    here = index_ref[1]
    values = tiles_ref[...].reshape(size * STEP, LANES)
    mean_one = window_sums(values) * (1.0 / L)
    mean_two = window_sums(values * values) * (1.0 / L)
    factor = lax.rsqrt(mean_two - mean_one * mean_one + EPSILON)
    out_ref[0:size] = tiles_ref[...]
    copy.wait()
    for record in range(size):
        weight = mask_ref[record >> 1, here * 2 + (record & 1)].astype(jnp.float32) * (1.0 / L)
        out_ref[size + record] = factor[record] * weight


def select_kernel(index_ref, station_hbm, lag_hbm, waves_hbm, out_ref, meta_ref,
                  station_ref, lag_ref, waves_ref, staged, sems):
    copies = [
        pltpu.make_async_copy(station_hbm, station_ref, sems.at[0]),
        pltpu.make_async_copy(lag_hbm, lag_ref, sems.at[1]),
        pltpu.make_async_copy(waves_hbm, waves_ref, sems.at[2]),
    ]
    for copy in copies:
        copy.start()
    peers = out_ref.shape[0]
    group_size = station_ref.shape[0]
    square = (group_size, group_size)
    row = lax.broadcasted_iota(jnp.int32, square, 0)
    column = lax.broadcasted_iota(jnp.int32, square, 1)
    for at in range(3 * TILES * CAP, SLOT_ROWS):
        staged[pl.ds(at, peers, stride=SLOT_ROWS), :] = jnp.zeros((peers, LANES), jnp.float32)
    copies[0].wait()
    stations = station_ref[...]
    owners = stations >> STATION_BITS
    down = jnp.sum(jnp.where(column == index_ref[0], owners, 0), axis=1, keepdims=True)
    down = jnp.broadcast_to(down, square)
    across = jnp.sum(jnp.where(row == column, down, 0), axis=0, keepdims=True)
    same = (down == across) & (row < column)
    place = jnp.sum(same.astype(jnp.int32), axis=0, keepdims=True)
    slot = across * CAP + place
    peer = lax.broadcasted_iota(jnp.int32, (peers, group_size), 0)
    selects = [(peer * CAP + k == slot).astype(jnp.float32).astype(jnp.bfloat16) for k in range(CAP)]
    select = jnp.concatenate(selects, axis=0)

    copies[1].wait()
    landing = owners == index_ref[0]
    earlier = (column < row).astype(jnp.float32).astype(jnp.bfloat16)
    arrival = jnp.dot(earlier, landing.astype(jnp.float32).astype(jnp.bfloat16), preferred_element_type=jnp.float32)
    packed = VALID + (lag_ref[...] << 9) + ((stations & (2**STATION_BITS - 1)) << 5) + row
    for k in range(CAP):
        held = landing & (arrival.astype(jnp.int32) == k)
        meta_ref[k:k + 1, :] = jnp.sum(jnp.where(held, packed, 0), axis=0, keepdims=True)

    copies[2].wait()
    for c in range(3):
        values = waves_ref[c].astype(jnp.float32)
        centred = values - jnp.mean(values, axis=-1, keepdims=True)
        power = jnp.mean(centred * centred, axis=-1, keepdims=True)
        unit = (centred / jnp.sqrt(power + EPSILON)).astype(jnp.bfloat16)
        picked = jnp.dot(select, unit, preferred_element_type=jnp.float32)
        for tile in range(TILES):
            columns = slice(tile * LANES, (tile + 1) * LANES)
            for k in range(CAP):
                at = (c * TILES + tile) * CAP + k
                staged[pl.ds(at, peers, stride=SLOT_ROWS), :] = picked[k * peers:(k + 1) * peers, columns]
    out_ref[...] = staged[...].astype(jnp.bfloat16).reshape(out_ref.shape)


def owner_of(here, core, hop, hops):
    return ((here - 2 * hop) & (2 * hops - 1)) ^ core


def stack_kernel(meta_ref, index_ref, near_ref, far_ref, waves_hbm, out_ref,
                 waves_ref, tiles, scales, frames, units, acc, twice, dense, slots, sems):
    here = index_ref[1]
    hops = near_ref.shape[0] // (2 * RECORDS)
    waves_copy = pltpu.make_async_copy(waves_hbm, waves_ref, sems.at[2])
    row_copies = [pltpu.make_async_copy(row_ref, tiles.at[core], sems.at[core])
                  for core, row_ref in enumerate((near_ref, far_ref))]
    for copy in row_copies + [waves_copy]:
        copy.start()

    def list_slot(slot, count):
        slots[count] = slot
        held = meta_ref[slot & (CAP - 1), slot >> 2] >> 20
        return count + held

    count = lax.fori_loop(0, meta_ref.shape[1] * CAP, list_slot, jnp.int32(0), unroll=16)
    for spare in range(UNROLL):
        slots[count + spare] = -1
    acc[...] = jnp.zeros_like(acc)

    for core, copy in enumerate(row_copies):
        copy.wait()
        for hop in range(hops):
            first = owner_of(here, core, hop, hops) * RECORDS
            at = 2 * RECORDS * hop
            values = tiles[core, at:at + RECORDS].reshape(RECORDS * STEP, LANES).astype(jnp.bfloat16)
            for turn in range(TURNS):
                rolled = values if turn == 0 else pltpu.roll(values, LANES - turn, 1)
                frames[pl.ds(first, RECORDS), turn * STEP:(turn + 1) * STEP, :] = (
                    rolled.reshape(RECORDS, STEP, LANES)
                )
            scales[pl.ds(first, RECORDS)] = tiles[core, at + RECORDS:at + 2 * RECORDS]
    waves_copy.wait()
    units[...] = waves_ref[...].reshape(units.shape).astype(jnp.float32)
    row = lax.broadcasted_iota(jnp.int32, (STEP, LANES), 0)
    lane = lax.broadcasted_iota(jnp.int32, (STEP, LANES), 1)
    own = lane >= row

    def one_pick(slot, spare):
        held = slot >= 0
        slot = jnp.maximum(slot, 0)
        packed = meta_ref[slot & (CAP - 1), slot >> 2]
        template = jnp.where(held, packed & 31, acc.shape[0] // STEP - 1)
        station = (packed >> 5) & 15
        lag = (packed >> 9) & 2047
        total = jnp.zeros((STEP, LANES), jnp.float32)
        for c in range(3):
            record = (station >> 1) * RECORDS + 2 * c + (station & 1)
            before = jnp.zeros((STEP, LANES), jnp.float32)
            columns = []
            for tile in range(TILES):
                at = (slot >> 2) * SLOT_ROWS + (c * TILES + tile) * CAP + (slot & (CAP - 1))
                wave = units[pl.ds(at, STEP, stride=0), :]
                spread = pltpu.roll(wave, 0, 1, stride=1, stride_axis=0)
                columns.append(jnp.where(own, spread, before).astype(jnp.bfloat16))
                before = spread
            columns.append(jnp.where(own, 0.0, before).astype(jnp.bfloat16))
            left = jnp.concatenate(
                [jnp.concatenate(columns[i:i + 2], axis=1) for i in range(0, TILES + 1, 2)], axis=0
            )
            product = jnp.dot(left, frames[record], preferred_element_type=jnp.float32)
            summed = product[:STEP]
            for part in range(1, (TILES + 1) // 2):
                later = product[part * STEP:(part + 1) * STEP]
                summed = summed + pltpu.roll(later, LANES - TURNS * part, 1)
            total = total + summed * scales[record]
        first = pltpu.roll(total, LANES - (lag >> 5), 1)
        twice[spare, 0:STEP, :] = first
        twice[spare, STEP:2 * STEP, :] = pltpu.roll(first, LANES - 1, 1)
        shifted = twice[spare, pl.ds(lag & (STEP - 1), STEP), :]
        return pl.ds(pl.multiple_of(template * STEP, STEP), STEP), shifted

    @pl.loop(0, (count + UNROLL - 1) // UNROLL)
    def _(index):
        done = [one_pick(slots[index * UNROLL + spare], spare) for spare in range(UNROLL)]
        for rows, shifted in done:
            acc[rows, :] += shifted

    for group in range(STEP // 4):
        parts = [acc[pl.ds(4 * group + j, STEP, stride=STEP), :] for j in range(4)]
        turned = jnp.concatenate(parts, axis=0).T
        dense[pl.ds(group, OUT_BLOCKS, stride=8), :] = turned[:OUT_BLOCKS]
    for part in range(out_ref.shape[1] // LANES):
        rows = dense[pl.ds(part, out_ref.shape[0], stride=3), :]
        out_ref[:, part * LANES:(part + 1) * LANES] = rows.astype(out_ref.dtype)


SMEM = pl.BlockSpec(memory_space=pltpu.SMEM)
VMEM = pl.BlockSpec(memory_space=pltpu.VMEM)
ANY = pl.BlockSpec(memory_space=pl.ANY)
HBM = pl.BlockSpec(memory_space=pltpu.HBM)


def with_scales(index, channel_mask, tiles):
    return pl.pallas_call(
        scales_kernel,
        out_shape=jax.ShapeDtypeStruct((2 * tiles.shape[0], STEP, LANES), jnp.float32),
        in_specs=[SMEM, HBM, VMEM],
        out_specs=VMEM,
        scratch_shapes=[pltpu.SMEM(channel_mask.shape, jnp.int32), pltpu.SemaphoreType.DMA],
        compiler_params=pltpu.CompilerParams(vmem_limit_bytes=4 * 1024 * 1024),
        cost_estimate=pl.CostEstimate(flops=2_000_000, transcendentals=25_000, bytes_accessed=300_000),
        name="record_scales",
    )(index, channel_mask, tiles)


def slot_waves(index, pick_station, pick_lag, template_waves, peers):
    group_size = pick_station.shape[0]
    return pl.pallas_call(
        select_kernel,
        out_shape=(
            jax.ShapeDtypeStruct((peers, SLOT_ROWS, LANES), jnp.bfloat16),
            jax.ShapeDtypeStruct((CAP, peers), jnp.int32),
        ),
        in_specs=[SMEM, HBM, HBM, HBM],
        out_specs=(VMEM, VMEM),
        scratch_shapes=[
            pltpu.VMEM((group_size, peers), jnp.int32),
            pltpu.VMEM((group_size, peers), jnp.int32),
            pltpu.VMEM(template_waves.shape, jnp.bfloat16),
            pltpu.VMEM((peers * SLOT_ROWS, LANES), jnp.float32),
            pltpu.SemaphoreType.DMA((3,)),
        ],
        compiler_params=pltpu.CompilerParams(vmem_limit_bytes=6 * 1024 * 1024),
        cost_estimate=pl.CostEstimate(flops=16_000_000, transcendentals=100, bytes_accessed=620_000),
        name="select_waves",
    )(index, pick_station, pick_lag, template_waves)


def partial_stack(meta, index, rows, received):
    group_size = meta.shape[1]
    peers = received.shape[0]
    slot_count = peers * CAP
    lines = NT * group_size // LANES
    records = rows[0].shape[0]
    return pl.pallas_call(
        stack_kernel,
        out_shape=jax.ShapeDtypeStruct((slot_count, lines * LANES // slot_count), jnp.bfloat16),
        in_specs=[SMEM, SMEM, ANY, ANY, ANY],
        out_specs=VMEM,
        scratch_shapes=[
            pltpu.VMEM(received.shape, jnp.bfloat16),
            pltpu.VMEM((2, records, STEP, LANES), jnp.float32),
            pltpu.VMEM((records, STEP, LANES), jnp.float32),
            pltpu.VMEM((records, TURNS * STEP, LANES), jnp.bfloat16),
            pltpu.VMEM((peers * SLOT_ROWS, LANES), jnp.float32),
            pltpu.VMEM(((group_size + 1) * STEP, LANES), jnp.float32),
            pltpu.VMEM((UNROLL, 2 * STEP, LANES), jnp.float32),
            pltpu.VMEM((lines, LANES), jnp.float32),
            pltpu.SMEM((slot_count + UNROLL,), jnp.int32),
            pltpu.SemaphoreType.DMA((3,)),
        ],
        compiler_params=pltpu.CompilerParams(vmem_limit_bytes=16 * 1024 * 1024),
        cost_estimate=pl.CostEstimate(flops=200_000_000, transcendentals=0, bytes_accessed=8_000_000),
        name="stack_picks",
    )(meta, index, *rows, received)


def body(station_data, channel_mask, template_waves, pick_station, pick_lag):
    sta_size = lax.axis_size("sta")
    tpl_size = lax.axis_size("tpl")
    group_size = pick_station.shape[0]
    stations_here = station_data.shape[1]
    index = jnp.stack([lax.axis_index("sta"), lax.axis_index("tpl")]).astype(jnp.int32)

    tiles = station_data.reshape(3, stations_here, BLOCKS, STEP).transpose(0, 1, 3, 2)
    tiles = jnp.pad(tiles, ((0, 0), (0, 0), (0, 0), (0, LANES - BLOCKS)))
    own = with_scales(index, channel_mask, tiles.reshape(3 * stations_here, STEP, LANES))
    row = [own]
    for hop in range(2, tpl_size, 2):
        row.append(lax.ppermute(own, "tpl", [(i, (i + hop) % tpl_size) for i in range(tpl_size)]))
    row = jnp.concatenate(row, axis=0)
    rows = [row, lax.ppermute(row, "tpl", [(i, i ^ 1) for i in range(tpl_size)])]

    waves = template_waves.reshape(group_size, 3, L).transpose(1, 0, 2)
    outgoing, meta = slot_waves(index, pick_station, pick_lag, waves, sta_size)
    received = lax.all_to_all(outgoing, "sta", split_axis=0, concat_axis=0, tiled=True)

    partial_sums = partial_stack(meta, index, rows, received)
    arrived = lax.all_to_all(partial_sums, "sta", split_axis=0, concat_axis=0, tiled=True)
    arrived = arrived.reshape(sta_size, CAP, -1).astype(jnp.float32)
    return jnp.sum(arrived, axis=0).reshape(NT // sta_size, group_size)


def solution(mesh):
    in_specs = (
        P(None, ("sta", "tpl"), None),
        P(None, "sta"),
        P("tpl", "sta", None, None),
        P("tpl", None),
        P("tpl", None),
    )
    return jax.shard_map(body, mesh=mesh, in_specs=in_specs, out_specs=P("sta", "tpl"), check_vma=False)
```

```python
import jax
import jax.numpy as jnp
from jax import lax
from jax.experimental import pallas as pl
from jax.experimental.pallas import tpu as pltpu
from jax.sharding import PartitionSpec as P

NT = 1536
L = 640
LAGS = 1024
SAMPLES = 3200
CAP = 4
STEP = 32
LANES = 128
BLOCKS = SAMPLES // STEP
OUT_BLOCKS = NT // STEP
TILES = L // LANES
TURNS = 8
UNROLL = 8
SLOT_ROWS = 64
RECORDS = 6
STATION_BITS = 4
EPSILON = 1e-05
VALID = 1 << 20


def exclusive_prefix(values):
    lanes = values.shape[-1]
    groups = values.reshape(-1, 8, lanes)
    row = lax.broadcasted_iota(jnp.int32, groups.shape, 1)
    total = groups
    for shift in (1, 2, 4):
        total = total + jnp.where(row >= shift, pltpu.roll(total, shift, 1), 0.0)
    inner = jnp.where(row >= 1, pltpu.roll(total, 1, 1), 0.0).reshape(-1, STEP // 8, 8, lanes)
    last = total.reshape(-1, STEP // 8, 8, lanes)[:, :, 7:8]
    pieces = [inner[:, 0:1]]
    carry = last[:, 0:1]
    for group in range(1, STEP // 8):
        pieces.append(inner[:, group:group + 1] + carry)
        carry = carry + last[:, group:group + 1]
    return jnp.concatenate(pieces, axis=1).reshape(values.shape)


def window_sums(values):
    width = values.shape[-1]
    span = L // STEP
    ahead = pltpu.roll(values, width - span, 1) - values
    two = jnp.sum(values.reshape(-1, STEP, width), axis=1)
    two = two + pltpu.roll(two, width - 1, 1)
    four = two + pltpu.roll(two, width - 2, 1)
    eight = four + pltpu.roll(four, width - 4, 1)
    sixteen = eight + pltpu.roll(eight, width - 8, 1)
    whole = sixteen + pltpu.roll(four, width - 16, 1)
    inner = exclusive_prefix(ahead).reshape(-1, STEP, width)
    return whole[:, None, :] + inner


def scales_kernel(index_ref, mask_hbm, tiles_ref, out_ref, mask_ref, sem):
    copy = pltpu.make_async_copy(mask_hbm, mask_ref, sem)
    copy.start()
    size = tiles_ref.shape[0]
    here = index_ref[1]
    values = tiles_ref[...].reshape(size * STEP, LANES)
    mean_one = window_sums(values) * (1.0 / L)
    mean_two = window_sums(values * values) * (1.0 / L)
    factor = lax.rsqrt(mean_two - mean_one * mean_one + EPSILON)
    out_ref[0:size] = tiles_ref[...]
    copy.wait()
    for record in range(size):
        weight = mask_ref[record >> 1, here * 2 + (record & 1)].astype(jnp.float32) * (1.0 / L)
        out_ref[size + record] = factor[record] * weight


def select_kernel(index_ref, station_hbm, lag_hbm, waves_hbm, out_ref, meta_ref,
                  station_ref, lag_ref, waves_ref, staged, sems):
    copies = [
        pltpu.make_async_copy(station_hbm, station_ref, sems.at[0]),
        pltpu.make_async_copy(lag_hbm, lag_ref, sems.at[1]),
        pltpu.make_async_copy(waves_hbm, waves_ref, sems.at[2]),
    ]
    for copy in copies:
        copy.start()
    peers = out_ref.shape[0]
    group_size = station_ref.shape[0]
    square = (group_size, group_size)
    row = lax.broadcasted_iota(jnp.int32, square, 0)
    column = lax.broadcasted_iota(jnp.int32, square, 1)
    for at in range(3 * TILES * CAP, SLOT_ROWS):
        staged[pl.ds(at, peers, stride=SLOT_ROWS), :] = jnp.zeros((peers, LANES), jnp.float32)
    copies[0].wait()
    stations = station_ref[...]
    owners = stations >> STATION_BITS
    down = jnp.sum(jnp.where(column == index_ref[0], owners, 0), axis=1, keepdims=True)
    down = jnp.broadcast_to(down, square)
    across = jnp.sum(jnp.where(row == column, down, 0), axis=0, keepdims=True)
    same = (down == across) & (row < column)
    place = jnp.sum(same.astype(jnp.int32), axis=0, keepdims=True)
    slot = across * CAP + place
    peer = lax.broadcasted_iota(jnp.int32, (peers, group_size), 0)
    selects = [(peer * CAP + k == slot).astype(jnp.float32).astype(jnp.bfloat16) for k in range(CAP)]
    select = jnp.concatenate(selects, axis=0)

    copies[1].wait()
    landing = owners == index_ref[0]
    earlier = (column < row).astype(jnp.float32).astype(jnp.bfloat16)
    arrival = jnp.dot(earlier, landing.astype(jnp.float32).astype(jnp.bfloat16), preferred_element_type=jnp.float32)
    packed = VALID + (lag_ref[...] << 9) + ((stations & (2**STATION_BITS - 1)) << 5) + row
    for k in range(CAP):
        held = landing & (arrival.astype(jnp.int32) == k)
        meta_ref[k:k + 1, :] = jnp.sum(jnp.where(held, packed, 0), axis=0, keepdims=True)

    copies[2].wait()
    for c in range(3):
        values = waves_ref[c].astype(jnp.float32)
        centred = values - jnp.mean(values, axis=-1, keepdims=True)
        power = jnp.mean(centred * centred, axis=-1, keepdims=True)
        unit = (centred / jnp.sqrt(power + EPSILON)).astype(jnp.bfloat16)
        picked = jnp.dot(select, unit, preferred_element_type=jnp.float32)
        for tile in range(TILES):
            columns = slice(tile * LANES, (tile + 1) * LANES)
            for k in range(CAP):
                at = (c * TILES + tile) * CAP + k
                staged[pl.ds(at, peers, stride=SLOT_ROWS), :] = picked[k * peers:(k + 1) * peers, columns]
    out_ref[...] = staged[...].astype(jnp.bfloat16).reshape(out_ref.shape)


def owner_of(here, core, hop, hops):
    return ((here - 2 * hop) & (2 * hops - 1)) ^ core


def stack_kernel(meta_ref, index_ref, *refs):
    *row_refs, waves_hbm, out_ref = refs[:-10]
    waves_ref, tiles, scales, frames, units, acc, twice, dense, slots, sems = refs[-10:]
    here = index_ref[1]
    hops = len(row_refs) // 2
    waves_copy = pltpu.make_async_copy(waves_hbm, waves_ref, sems.at[len(row_refs)])
    row_copies = [pltpu.make_async_copy(row_ref, tiles.at[at], sems.at[at]) for at, row_ref in enumerate(row_refs)]
    for copy in row_copies + [waves_copy]:
        copy.start()

    def list_slot(slot, count):
        slots[count] = slot
        held = meta_ref[slot & (CAP - 1), slot >> 2] >> 20
        return count + held

    count = lax.fori_loop(0, meta_ref.shape[1] * CAP, list_slot, jnp.int32(0), unroll=16)
    for spare in range(UNROLL):
        slots[count + spare] = -1
    acc[...] = jnp.zeros_like(acc)

    for at, copy in enumerate(row_copies):
        copy.wait()
        first = owner_of(here, at // hops, at % hops, hops) * RECORDS
        values = tiles[at, :RECORDS].reshape(RECORDS * STEP, LANES).astype(jnp.bfloat16)
        for turn in range(TURNS):
            rolled = values if turn == 0 else pltpu.roll(values, LANES - turn, 1)
            frames[pl.ds(first, RECORDS), turn * STEP:(turn + 1) * STEP, :] = rolled.reshape(RECORDS, STEP, LANES)
        scales[pl.ds(first, RECORDS)] = tiles[at, RECORDS:]
    waves_copy.wait()
    units[...] = waves_ref[...].reshape(units.shape).astype(jnp.float32)
    row = lax.broadcasted_iota(jnp.int32, (STEP, LANES), 0)
    lane = lax.broadcasted_iota(jnp.int32, (STEP, LANES), 1)
    own = lane >= row

    def one_pick(slot, spare):
        held = slot >= 0
        slot = jnp.maximum(slot, 0)
        packed = meta_ref[slot & (CAP - 1), slot >> 2]
        template = jnp.where(held, packed & 31, acc.shape[0] // STEP - 1)
        station = (packed >> 5) & 15
        lag = (packed >> 9) & 2047
        total = jnp.zeros((STEP, LANES), jnp.float32)
        for c in range(3):
            record = (station >> 1) * RECORDS + 2 * c + (station & 1)
            before = jnp.zeros((STEP, LANES), jnp.float32)
            columns = []
            for tile in range(TILES):
                at = (slot >> 2) * SLOT_ROWS + (c * TILES + tile) * CAP + (slot & (CAP - 1))
                wave = units[pl.ds(at, STEP, stride=0), :]
                spread = pltpu.roll(wave, 0, 1, stride=1, stride_axis=0)
                columns.append(jnp.where(own, spread, before).astype(jnp.bfloat16))
                before = spread
            columns.append(jnp.where(own, 0.0, before).astype(jnp.bfloat16))
            left = jnp.concatenate(
                [jnp.concatenate(columns[i:i + 2], axis=1) for i in range(0, TILES + 1, 2)], axis=0
            )
            product = jnp.dot(left, frames[record], preferred_element_type=jnp.float32)
            summed = product[:STEP]
            for part in range(1, (TILES + 1) // 2):
                later = product[part * STEP:(part + 1) * STEP]
                summed = summed + pltpu.roll(later, LANES - TURNS * part, 1)
            total = total + summed * scales[record]
        first = pltpu.roll(total, LANES - (lag >> 5), 1)
        twice[spare, 0:STEP, :] = first
        twice[spare, STEP:2 * STEP, :] = pltpu.roll(first, LANES - 1, 1)
        shifted = twice[spare, pl.ds(lag & (STEP - 1), STEP), :]
        return pl.ds(pl.multiple_of(template * STEP, STEP), STEP), shifted

    @pl.loop(0, (count + UNROLL - 1) // UNROLL)
    def _(index):
        done = [one_pick(slots[index * UNROLL + spare], spare) for spare in range(UNROLL)]
        for rows, shifted in done:
            acc[rows, :] += shifted

    for group in range(STEP // 4):
        parts = [acc[pl.ds(4 * group + j, STEP, stride=STEP), :] for j in range(4)]
        turned = jnp.concatenate(parts, axis=0).T
        dense[pl.ds(group, OUT_BLOCKS, stride=8), :] = turned[:OUT_BLOCKS]
    for part in range(out_ref.shape[1] // LANES):
        rows = dense[pl.ds(part, out_ref.shape[0], stride=3), :]
        out_ref[:, part * LANES:(part + 1) * LANES] = rows.astype(out_ref.dtype)


SMEM = pl.BlockSpec(memory_space=pltpu.SMEM)
VMEM = pl.BlockSpec(memory_space=pltpu.VMEM)
ANY = pl.BlockSpec(memory_space=pl.ANY)
HBM = pl.BlockSpec(memory_space=pltpu.HBM)


def with_scales(index, channel_mask, tiles):
    return pl.pallas_call(
        scales_kernel,
        out_shape=jax.ShapeDtypeStruct((2 * tiles.shape[0], STEP, LANES), jnp.float32),
        in_specs=[SMEM, HBM, VMEM],
        out_specs=VMEM,
        scratch_shapes=[pltpu.SMEM(channel_mask.shape, jnp.int32), pltpu.SemaphoreType.DMA],
        compiler_params=pltpu.CompilerParams(vmem_limit_bytes=4 * 1024 * 1024),
        cost_estimate=pl.CostEstimate(flops=2_000_000, transcendentals=25_000, bytes_accessed=300_000),
        name="record_scales",
    )(index, channel_mask, tiles)


def slot_waves(index, pick_station, pick_lag, template_waves, peers):
    group_size = pick_station.shape[0]
    return pl.pallas_call(
        select_kernel,
        out_shape=(
            jax.ShapeDtypeStruct((peers, SLOT_ROWS, LANES), jnp.bfloat16),
            jax.ShapeDtypeStruct((CAP, peers), jnp.int32),
        ),
        in_specs=[SMEM, HBM, HBM, HBM],
        out_specs=(VMEM, VMEM),
        scratch_shapes=[
            pltpu.VMEM((group_size, peers), jnp.int32),
            pltpu.VMEM((group_size, peers), jnp.int32),
            pltpu.VMEM(template_waves.shape, jnp.bfloat16),
            pltpu.VMEM((peers * SLOT_ROWS, LANES), jnp.float32),
            pltpu.SemaphoreType.DMA((3,)),
        ],
        compiler_params=pltpu.CompilerParams(vmem_limit_bytes=6 * 1024 * 1024),
        cost_estimate=pl.CostEstimate(flops=16_000_000, transcendentals=100, bytes_accessed=620_000),
        name="select_waves",
    )(index, pick_station, pick_lag, template_waves)


def partial_stack(meta, index, rows, received):
    group_size = meta.shape[1]
    peers = received.shape[0]
    slot_count = peers * CAP
    lines = NT * group_size // LANES
    records = len(rows) * RECORDS
    return pl.pallas_call(
        stack_kernel,
        out_shape=jax.ShapeDtypeStruct((slot_count, lines * LANES // slot_count), jnp.bfloat16),
        in_specs=[SMEM, SMEM] + [ANY] * (len(rows) + 1),
        out_specs=VMEM,
        scratch_shapes=[
            pltpu.VMEM(received.shape, jnp.bfloat16),
            pltpu.VMEM((len(rows), 2 * RECORDS, STEP, LANES), jnp.float32),
            pltpu.VMEM((records, STEP, LANES), jnp.float32),
            pltpu.VMEM((records, TURNS * STEP, LANES), jnp.bfloat16),
            pltpu.VMEM((peers * SLOT_ROWS, LANES), jnp.float32),
            pltpu.VMEM(((group_size + 1) * STEP, LANES), jnp.float32),
            pltpu.VMEM((UNROLL, 2 * STEP, LANES), jnp.float32),
            pltpu.VMEM((lines, LANES), jnp.float32),
            pltpu.SMEM((slot_count + UNROLL,), jnp.int32),
            pltpu.SemaphoreType.DMA((len(rows) + 1,)),
        ],
        compiler_params=pltpu.CompilerParams(vmem_limit_bytes=16 * 1024 * 1024),
        cost_estimate=pl.CostEstimate(flops=200_000_000, transcendentals=0, bytes_accessed=8_000_000),
        name="stack_picks",
    )(meta, index, *rows, received)


def body(station_data, channel_mask, template_waves, pick_station, pick_lag):
    sta_size = lax.axis_size("sta")
    tpl_size = lax.axis_size("tpl")
    group_size = pick_station.shape[0]
    stations_here = station_data.shape[1]
    index = jnp.stack([lax.axis_index("sta"), lax.axis_index("tpl")]).astype(jnp.int32)

    waves = template_waves.reshape(group_size, 3, L).transpose(1, 0, 2)
    outgoing, meta = slot_waves(index, pick_station, pick_lag, waves, sta_size)
    received = lax.all_to_all(outgoing, "sta", split_axis=0, concat_axis=0, tiled=True)

    tiles = station_data.reshape(3, stations_here, BLOCKS, STEP).transpose(0, 1, 3, 2)
    tiles = jnp.pad(tiles, ((0, 0), (0, 0), (0, 0), (0, LANES - BLOCKS)))
    own = with_scales(index, channel_mask, tiles.reshape(3 * stations_here, STEP, LANES))
    swap = [(i, i ^ 1) for i in range(tpl_size)]
    near = [own]
    for hop in range(2, tpl_size, 2):
        near.append(lax.ppermute(own, "tpl", [(i, (i + hop) % tpl_size) for i in range(tpl_size)]))
    rows = near + [lax.ppermute(row, "tpl", swap) for row in near]

    partial_sums = partial_stack(meta, index, rows, received)
    arrived = lax.all_to_all(partial_sums, "sta", split_axis=0, concat_axis=0, tiled=True)
    arrived = arrived.reshape(sta_size, CAP, -1).astype(jnp.float32)
    return jnp.sum(arrived, axis=0).reshape(NT // sta_size, group_size)


def solution(mesh):
    in_specs = (
        P(None, ("sta", "tpl"), None),
        P(None, "sta"),
        P("tpl", "sta", None, None),
        P("tpl", None),
        P("tpl", None),
    )
    return jax.shard_map(body, mesh=mesh, in_specs=in_specs, out_specs=P("sta", "tpl"), check_vma=False)
```

```python
import jax
import jax.numpy as jnp
from jax import lax
from jax.experimental import pallas as pl
from jax.experimental.pallas import tpu as pltpu
from jax.sharding import PartitionSpec as P

NT = 1536
L = 640
LAGS = 1024
SAMPLES = 3200
CAP = 4
STEP = 32
LANES = 128
BLOCKS = SAMPLES // STEP
OUT_BLOCKS = NT // STEP
TILES = L // LANES
TURNS = 8
UNROLL = 8
SLOT_ROWS = 64
RECORDS = 6
STATION_BITS = 4
EPSILON = 1e-05
VALID = 1 << 20


def exclusive_prefix(values):
    lanes = values.shape[-1]
    groups = values.reshape(-1, 8, lanes)
    row = lax.broadcasted_iota(jnp.int32, groups.shape, 1)
    total = groups
    for shift in (1, 2, 4):
        total = total + jnp.where(row >= shift, pltpu.roll(total, shift, 1), 0.0)
    inner = jnp.where(row >= 1, pltpu.roll(total, 1, 1), 0.0).reshape(-1, STEP // 8, 8, lanes)
    last = total.reshape(-1, STEP // 8, 8, lanes)[:, :, 7:8]
    pieces = [inner[:, 0:1]]
    carry = last[:, 0:1]
    for group in range(1, STEP // 8):
        pieces.append(inner[:, group:group + 1] + carry)
        carry = carry + last[:, group:group + 1]
    return jnp.concatenate(pieces, axis=1).reshape(values.shape)


def window_sums(values):
    width = values.shape[-1]
    span = L // STEP
    ahead = pltpu.roll(values, width - span, 1) - values
    two = jnp.sum(values.reshape(-1, STEP, width), axis=1)
    two = two + pltpu.roll(two, width - 1, 1)
    four = two + pltpu.roll(two, width - 2, 1)
    eight = four + pltpu.roll(four, width - 4, 1)
    sixteen = eight + pltpu.roll(eight, width - 8, 1)
    whole = sixteen + pltpu.roll(four, width - 16, 1)
    inner = exclusive_prefix(ahead).reshape(-1, STEP, width)
    return whole[:, None, :] + inner


def scales_kernel(index_ref, mask_hbm, tiles_ref, out_ref, mask_ref, sem):
    copy = pltpu.make_async_copy(mask_hbm, mask_ref, sem)
    copy.start()
    size = tiles_ref.shape[0]
    here = index_ref[1]
    values = tiles_ref[...].reshape(size * STEP, LANES)
    mean_one = window_sums(values) * (1.0 / L)
    mean_two = window_sums(values * values) * (1.0 / L)
    factor = lax.rsqrt(mean_two - mean_one * mean_one + EPSILON)
    out_ref[0:size] = tiles_ref[...].astype(jnp.bfloat16)
    copy.wait()
    for record in range(size):
        weight = mask_ref[record >> 1, here * 2 + (record & 1)].astype(jnp.float32) * (1.0 / L)
        scale = factor[record] * weight
        coarse = scale.astype(jnp.bfloat16)
        out_ref[size + record] = coarse
        out_ref[2 * size + record] = (scale - coarse.astype(jnp.float32)).astype(jnp.bfloat16)


def select_kernel(index_ref, station_hbm, lag_hbm, waves_hbm, out_ref, meta_ref,
                  station_ref, lag_ref, waves_ref, staged, sems):
    copies = [
        pltpu.make_async_copy(station_hbm, station_ref, sems.at[0]),
        pltpu.make_async_copy(lag_hbm, lag_ref, sems.at[1]),
        pltpu.make_async_copy(waves_hbm, waves_ref, sems.at[2]),
    ]
    for copy in copies:
        copy.start()
    peers = out_ref.shape[0]
    group_size = station_ref.shape[0]
    square = (group_size, group_size)
    row = lax.broadcasted_iota(jnp.int32, square, 0)
    column = lax.broadcasted_iota(jnp.int32, square, 1)
    for at in range(3 * TILES * CAP, SLOT_ROWS):
        staged[pl.ds(at, peers, stride=SLOT_ROWS), :] = jnp.zeros((peers, LANES), jnp.float32)
    copies[0].wait()
    stations = station_ref[...]
    owners = stations >> STATION_BITS
    down = jnp.sum(jnp.where(column == index_ref[0], owners, 0), axis=1, keepdims=True)
    down = jnp.broadcast_to(down, square)
    across = jnp.sum(jnp.where(row == column, down, 0), axis=0, keepdims=True)
    same = (down == across) & (row < column)
    place = jnp.sum(same.astype(jnp.int32), axis=0, keepdims=True)
    slot = across * CAP + place
    peer = lax.broadcasted_iota(jnp.int32, (peers, group_size), 0)
    selects = [(peer * CAP + k == slot).astype(jnp.float32).astype(jnp.bfloat16) for k in range(CAP)]
    select = jnp.concatenate(selects, axis=0)

    copies[1].wait()
    landing = owners == index_ref[0]
    earlier = (column < row).astype(jnp.float32).astype(jnp.bfloat16)
    arrival = jnp.dot(earlier, landing.astype(jnp.float32).astype(jnp.bfloat16), preferred_element_type=jnp.float32)
    packed = VALID + (lag_ref[...] << 9) + ((stations & (2**STATION_BITS - 1)) << 5) + row
    for k in range(CAP):
        held = landing & (arrival.astype(jnp.int32) == k)
        meta_ref[k:k + 1, :] = jnp.sum(jnp.where(held, packed, 0), axis=0, keepdims=True)

    copies[2].wait()
    for c in range(3):
        values = waves_ref[c].astype(jnp.float32)
        centred = values - jnp.mean(values, axis=-1, keepdims=True)
        power = jnp.mean(centred * centred, axis=-1, keepdims=True)
        unit = (centred / jnp.sqrt(power + EPSILON)).astype(jnp.bfloat16)
        picked = jnp.dot(select, unit, preferred_element_type=jnp.float32)
        for tile in range(TILES):
            columns = slice(tile * LANES, (tile + 1) * LANES)
            for k in range(CAP):
                at = (c * TILES + tile) * CAP + k
                staged[pl.ds(at, peers, stride=SLOT_ROWS), :] = picked[k * peers:(k + 1) * peers, columns]
    out_ref[...] = staged[...].astype(jnp.bfloat16).reshape(out_ref.shape)


def owner_of(here, core, hop, hops):
    return ((here - 2 * hop) & (2 * hops - 1)) ^ core


def stack_kernel(meta_ref, index_ref, near_ref, far_ref, waves_hbm, out_ref,
                 waves_ref, tiles, scales, frames, units, acc, twice, dense, slots, sems):
    here = index_ref[1]
    hops = near_ref.shape[0] // (3 * RECORDS)
    waves_copy = pltpu.make_async_copy(waves_hbm, waves_ref, sems.at[2])
    row_copies = [pltpu.make_async_copy(row_ref, tiles.at[core], sems.at[core])
                  for core, row_ref in enumerate((near_ref, far_ref))]
    for copy in row_copies + [waves_copy]:
        copy.start()

    def list_slot(slot, count):
        slots[count] = slot
        held = meta_ref[slot & (CAP - 1), slot >> 2] >> 20
        return count + held

    count = lax.fori_loop(0, meta_ref.shape[1] * CAP, list_slot, jnp.int32(0), unroll=16)
    for spare in range(UNROLL):
        slots[count + spare] = -1
    acc[...] = jnp.zeros_like(acc)

    for core, copy in enumerate(row_copies):
        copy.wait()
        for hop in range(hops):
            first = owner_of(here, core, hop, hops) * RECORDS
            at = 3 * RECORDS * hop
            values = tiles[core, at:at + RECORDS].reshape(RECORDS * STEP, LANES)
            for turn in range(TURNS):
                rolled = values if turn == 0 else pltpu.roll(values, LANES - turn, 1)
                frames[pl.ds(first, RECORDS), turn * STEP:(turn + 1) * STEP, :] = (
                    rolled.reshape(RECORDS, STEP, LANES)
                )
            coarse = tiles[core, at + RECORDS:at + 2 * RECORDS].astype(jnp.float32)
            fine = tiles[core, at + 2 * RECORDS:at + 3 * RECORDS].astype(jnp.float32)
            scales[pl.ds(first, RECORDS)] = coarse + fine
    waves_copy.wait()
    units[...] = waves_ref[...].reshape(units.shape).astype(jnp.float32)
    row = lax.broadcasted_iota(jnp.int32, (STEP, LANES), 0)
    lane = lax.broadcasted_iota(jnp.int32, (STEP, LANES), 1)
    own = lane >= row

    def one_pick(slot, spare):
        held = slot >= 0
        slot = jnp.maximum(slot, 0)
        packed = meta_ref[slot & (CAP - 1), slot >> 2]
        template = jnp.where(held, packed & 31, acc.shape[0] // STEP - 1)
        station = (packed >> 5) & 15
        lag = (packed >> 9) & 2047
        total = jnp.zeros((STEP, LANES), jnp.float32)
        for c in range(3):
            record = (station >> 1) * RECORDS + 2 * c + (station & 1)
            before = jnp.zeros((STEP, LANES), jnp.float32)
            columns = []
            for tile in range(TILES):
                at = (slot >> 2) * SLOT_ROWS + (c * TILES + tile) * CAP + (slot & (CAP - 1))
                wave = units[pl.ds(at, STEP, stride=0), :]
                spread = pltpu.roll(wave, 0, 1, stride=1, stride_axis=0)
                columns.append(jnp.where(own, spread, before).astype(jnp.bfloat16))
                before = spread
            columns.append(jnp.where(own, 0.0, before).astype(jnp.bfloat16))
            left = jnp.concatenate(
                [jnp.concatenate(columns[i:i + 2], axis=1) for i in range(0, TILES + 1, 2)], axis=0
            )
            product = jnp.dot(left, frames[record], preferred_element_type=jnp.float32)
            summed = product[:STEP]
            for part in range(1, (TILES + 1) // 2):
                later = product[part * STEP:(part + 1) * STEP]
                summed = summed + pltpu.roll(later, LANES - TURNS * part, 1)
            total = total + summed * scales[record]
        first = pltpu.roll(total, LANES - (lag >> 5), 1)
        twice[spare, 0:STEP, :] = first
        twice[spare, STEP:2 * STEP, :] = pltpu.roll(first, LANES - 1, 1)
        shifted = twice[spare, pl.ds(lag & (STEP - 1), STEP), :]
        return pl.ds(pl.multiple_of(template * STEP, STEP), STEP), shifted

    @pl.loop(0, (count + UNROLL - 1) // UNROLL)
    def _(index):
        done = [one_pick(slots[index * UNROLL + spare], spare) for spare in range(UNROLL)]
        for rows, shifted in done:
            acc[rows, :] += shifted

    for group in range(STEP // 4):
        parts = [acc[pl.ds(4 * group + j, STEP, stride=STEP), :] for j in range(4)]
        turned = jnp.concatenate(parts, axis=0).T
        dense[pl.ds(group, OUT_BLOCKS, stride=8), :] = turned[:OUT_BLOCKS]
    for part in range(out_ref.shape[1] // LANES):
        rows = dense[pl.ds(part, out_ref.shape[0], stride=3), :]
        out_ref[:, part * LANES:(part + 1) * LANES] = rows.astype(out_ref.dtype)


SMEM = pl.BlockSpec(memory_space=pltpu.SMEM)
VMEM = pl.BlockSpec(memory_space=pltpu.VMEM)
ANY = pl.BlockSpec(memory_space=pl.ANY)
HBM = pl.BlockSpec(memory_space=pltpu.HBM)


def with_scales(index, channel_mask, tiles):
    return pl.pallas_call(
        scales_kernel,
        out_shape=jax.ShapeDtypeStruct((3 * tiles.shape[0], STEP, LANES), jnp.bfloat16),
        in_specs=[SMEM, HBM, VMEM],
        out_specs=VMEM,
        scratch_shapes=[pltpu.SMEM(channel_mask.shape, jnp.int32), pltpu.SemaphoreType.DMA],
        compiler_params=pltpu.CompilerParams(vmem_limit_bytes=4 * 1024 * 1024),
        cost_estimate=pl.CostEstimate(flops=2_000_000, transcendentals=25_000, bytes_accessed=300_000),
        name="record_scales",
    )(index, channel_mask, tiles)


def slot_waves(index, pick_station, pick_lag, template_waves, peers):
    group_size = pick_station.shape[0]
    return pl.pallas_call(
        select_kernel,
        out_shape=(
            jax.ShapeDtypeStruct((peers, SLOT_ROWS, LANES), jnp.bfloat16),
            jax.ShapeDtypeStruct((CAP, peers), jnp.int32),
        ),
        in_specs=[SMEM, HBM, HBM, HBM],
        out_specs=(VMEM, VMEM),
        scratch_shapes=[
            pltpu.VMEM((group_size, peers), jnp.int32),
            pltpu.VMEM((group_size, peers), jnp.int32),
            pltpu.VMEM(template_waves.shape, jnp.bfloat16),
            pltpu.VMEM((peers * SLOT_ROWS, LANES), jnp.float32),
            pltpu.SemaphoreType.DMA((3,)),
        ],
        compiler_params=pltpu.CompilerParams(vmem_limit_bytes=6 * 1024 * 1024),
        cost_estimate=pl.CostEstimate(flops=16_000_000, transcendentals=100, bytes_accessed=620_000),
        name="select_waves",
    )(index, pick_station, pick_lag, template_waves)


def partial_stack(meta, index, rows, received):
    group_size = meta.shape[1]
    peers = received.shape[0]
    slot_count = peers * CAP
    lines = NT * group_size // LANES
    records = 2 * rows[0].shape[0] // 3
    return pl.pallas_call(
        stack_kernel,
        out_shape=jax.ShapeDtypeStruct((slot_count, lines * LANES // slot_count), jnp.bfloat16),
        in_specs=[SMEM, SMEM, ANY, ANY, ANY],
        out_specs=VMEM,
        scratch_shapes=[
            pltpu.VMEM(received.shape, jnp.bfloat16),
            pltpu.VMEM((2,) + rows[0].shape, jnp.bfloat16),
            pltpu.VMEM((records, STEP, LANES), jnp.float32),
            pltpu.VMEM((records, TURNS * STEP, LANES), jnp.bfloat16),
            pltpu.VMEM((peers * SLOT_ROWS, LANES), jnp.float32),
            pltpu.VMEM(((group_size + 1) * STEP, LANES), jnp.float32),
            pltpu.VMEM((UNROLL, 2 * STEP, LANES), jnp.float32),
            pltpu.VMEM((lines, LANES), jnp.float32),
            pltpu.SMEM((slot_count + UNROLL,), jnp.int32),
            pltpu.SemaphoreType.DMA((3,)),
        ],
        compiler_params=pltpu.CompilerParams(vmem_limit_bytes=16 * 1024 * 1024),
        cost_estimate=pl.CostEstimate(flops=200_000_000, transcendentals=0, bytes_accessed=8_000_000),
        name="stack_picks",
    )(meta, index, *rows, received)


def body(station_data, channel_mask, template_waves, pick_station, pick_lag):
    sta_size = lax.axis_size("sta")
    tpl_size = lax.axis_size("tpl")
    group_size = pick_station.shape[0]
    stations_here = station_data.shape[1]
    index = jnp.stack([lax.axis_index("sta"), lax.axis_index("tpl")]).astype(jnp.int32)

    waves = template_waves.reshape(group_size, 3, L).transpose(1, 0, 2)
    outgoing, meta = slot_waves(index, pick_station, pick_lag, waves, sta_size)
    received = lax.all_to_all(outgoing, "sta", split_axis=0, concat_axis=0, tiled=True)

    tiles = station_data.reshape(3, stations_here, BLOCKS, STEP).transpose(0, 1, 3, 2)
    tiles = jnp.pad(tiles, ((0, 0), (0, 0), (0, 0), (0, LANES - BLOCKS)))
    own = with_scales(index, channel_mask, tiles.reshape(3 * stations_here, STEP, LANES))
    row = [own]
    for hop in range(2, tpl_size, 2):
        row.append(lax.ppermute(own, "tpl", [(i, (i + hop) % tpl_size) for i in range(tpl_size)]))
    row = jnp.concatenate(row, axis=0)
    rows = [row, lax.ppermute(row, "tpl", [(i, i ^ 1) for i in range(tpl_size)])]

    partial_sums = partial_stack(meta, index, rows, received)
    arrived = lax.all_to_all(partial_sums, "sta", split_axis=0, concat_axis=0, tiled=True)
    arrived = arrived.reshape(sta_size, CAP, -1).astype(jnp.float32)
    return jnp.sum(arrived, axis=0).reshape(NT // sta_size, group_size)


def solution(mesh):
    in_specs = (
        P(None, ("sta", "tpl"), None),
        P(None, "sta"),
        P("tpl", "sta", None, None),
        P("tpl", None),
        P("tpl", None),
    )
    return jax.shard_map(body, mesh=mesh, in_specs=in_specs, out_specs=P("sta", "tpl"), check_vma=False)
```

```python
import jax
import jax.numpy as jnp
from jax import lax
from jax.experimental import pallas as pl
from jax.experimental.pallas import tpu as pltpu
from jax.sharding import PartitionSpec as P

NT = 1536
L = 640
LAGS = 1024
SAMPLES = 3200
CAP = 4
STEP = 32
LANES = 128
BLOCKS = SAMPLES // STEP
OUT_BLOCKS = NT // STEP
TILES = L // LANES
TURNS = 8
UNROLL = 8
SLOT_ROWS = 64
RECORDS = 6
STATION_BITS = 4
EPSILON = 1e-05
VALID = 1 << 27


def exclusive_prefix(values):
    lanes = values.shape[-1]
    groups = values.reshape(-1, 8, lanes)
    row = lax.broadcasted_iota(jnp.int32, groups.shape, 1)
    total = groups
    for shift in (1, 2, 4):
        total = total + jnp.where(row >= shift, pltpu.roll(total, shift, 1), 0.0)
    inner = jnp.where(row >= 1, pltpu.roll(total, 1, 1), 0.0).reshape(-1, STEP // 8, 8, lanes)
    last = total.reshape(-1, STEP // 8, 8, lanes)[:, :, 7:8]
    pieces = [inner[:, 0:1]]
    carry = last[:, 0:1]
    for group in range(1, STEP // 8):
        pieces.append(inner[:, group:group + 1] + carry)
        carry = carry + last[:, group:group + 1]
    return jnp.concatenate(pieces, axis=1).reshape(values.shape)


def window_sums(values):
    width = values.shape[-1]
    span = L // STEP
    ahead = pltpu.roll(values, width - span, 1) - values
    two = jnp.sum(values.reshape(-1, STEP, width), axis=1)
    two = two + pltpu.roll(two, width - 1, 1)
    four = two + pltpu.roll(two, width - 2, 1)
    eight = four + pltpu.roll(four, width - 4, 1)
    sixteen = eight + pltpu.roll(eight, width - 8, 1)
    whole = sixteen + pltpu.roll(four, width - 16, 1)
    inner = exclusive_prefix(ahead).reshape(-1, STEP, width)
    return whole[:, None, :] + inner


def select_kernel(index_ref, station_ref, waves_ref, out_ref, staged):
    group_size = station_ref.shape[0]
    square = (group_size, group_size)
    row = lax.broadcasted_iota(jnp.int32, square, 0)
    column = lax.broadcasted_iota(jnp.int32, square, 1)
    owners = station_ref[...] >> STATION_BITS
    down = jnp.sum(jnp.where(column == index_ref[0], owners, 0), axis=1, keepdims=True)
    down = jnp.broadcast_to(down, square)
    across = jnp.sum(jnp.where(row == column, down, 0), axis=0, keepdims=True)
    same = (down == across) & (row < column)
    place = jnp.sum(same.astype(jnp.int32), axis=0, keepdims=True)
    slot = across * CAP + place
    peers = out_ref.shape[0]
    peer = lax.broadcasted_iota(jnp.int32, (peers, group_size), 0)
    selects = [(peer * CAP + k == slot).astype(jnp.float32).astype(jnp.bfloat16) for k in range(CAP)]
    select = jnp.concatenate(selects, axis=0)
    for c in range(3):
        values = waves_ref[c].astype(jnp.float32)
        centred = values - jnp.mean(values, axis=-1, keepdims=True)
        power = jnp.mean(centred * centred, axis=-1, keepdims=True)
        unit = (centred / jnp.sqrt(power + EPSILON)).astype(jnp.bfloat16)
        picked = jnp.dot(select, unit, preferred_element_type=jnp.float32)
        for tile in range(TILES):
            columns = slice(tile * LANES, (tile + 1) * LANES)
            for k in range(CAP):
                at = (c * TILES + tile) * CAP + k
                staged[pl.ds(at, peers, stride=SLOT_ROWS), :] = picked[k * peers:(k + 1) * peers, columns]
    for at in range(3 * TILES * CAP, SLOT_ROWS):
        staged[pl.ds(at, peers, stride=SLOT_ROWS), :] = jnp.zeros((peers, LANES), jnp.float32)
    out_ref[...] = staged[...].astype(jnp.bfloat16).reshape(out_ref.shape)


def owner_of(here, core, hop, hops):
    return ((here - 2 * hop) & (2 * hops - 1)) ^ core


def scales_kernel(index_ref, mask_hbm, station_ref, lag_ref, near_ref, far_ref, scales, entries,
                  meta_vmem, meta, mask_ref, sems):
    mask_copy = pltpu.make_async_copy(mask_hbm, mask_ref, sems.at[0])
    mask_copy.start()
    square = station_ref.shape
    row = lax.broadcasted_iota(jnp.int32, square, 0)
    column = lax.broadcasted_iota(jnp.int32, square, 1)
    stations = station_ref[...]
    landing = (stations >> STATION_BITS) == index_ref[0]
    earlier = (column < row).astype(jnp.float32).astype(jnp.bfloat16)
    arrival = jnp.dot(earlier, landing.astype(jnp.float32).astype(jnp.bfloat16), preferred_element_type=jnp.float32)
    local = stations & (2**STATION_BITS - 1)
    packed = VALID + (column << 22) + (lag_ref[...] << 9) + (local << 5) + row
    for k in range(CAP):
        held = landing & (arrival.astype(jnp.int32) == k)
        meta_vmem[k:k + 1, :] = jnp.sum(jnp.where(held, packed, 0), axis=0, keepdims=True)
    meta_copy = pltpu.make_async_copy(meta_vmem, meta, sems.at[1])
    meta_copy.start()

    here = index_ref[1]
    hops = near_ref.shape[0] // RECORDS
    mask_copy.wait()
    for core, tile_ref in enumerate((near_ref, far_ref)):
        for hop in range(hops):
            owner = owner_of(here, core, hop, hops)
            values = tile_ref[hop * RECORDS:(hop + 1) * RECORDS].reshape(RECORDS * STEP, LANES)
            mean_one = window_sums(values) * (1.0 / L)
            mean_two = window_sums(values * values) * (1.0 / L)
            factor = lax.rsqrt(mean_two - mean_one * mean_one + EPSILON)
            for record in range(RECORDS):
                weight = mask_ref[record >> 1, owner * 2 + (record & 1)].astype(jnp.float32) * (1.0 / L)
                scales[owner * RECORDS + record] = factor[record] * weight

    meta_copy.wait()

    def list_slot(slot, count):
        packed = meta[slot & (CAP - 1), slot >> 2]
        entries[count] = packed + ((slot & (CAP - 1)) << 20)
        return count + (packed >> 27)

    total = meta.shape[1] * CAP
    count = lax.fori_loop(0, total, list_slot, jnp.int32(0), unroll=16)
    for spare in range(UNROLL):
        entries[count + spare] = -1
    entries[total + UNROLL] = count


def stack_kernel(entries, index_ref, near_ref, far_ref, scales_hbm, waves_hbm, out_ref,
                 waves_ref, tiles, scales, frames, units, acc, twice, dense, sems):
    here = index_ref[1]
    hops = near_ref.shape[0] // RECORDS
    row_copies = [pltpu.make_async_copy(row_ref, tiles.at[core], sems.at[core])
                  for core, row_ref in enumerate((near_ref, far_ref))]
    waves_copy = pltpu.make_async_copy(waves_hbm, waves_ref, sems.at[2])
    scales_copy = pltpu.make_async_copy(scales_hbm, scales, sems.at[3])
    for copy in row_copies + [waves_copy, scales_copy]:
        copy.start()
    count = entries[entries.shape[0] - 1]
    acc[...] = jnp.zeros_like(acc)

    for core, copy in enumerate(row_copies):
        copy.wait()
        for hop in range(hops):
            first = owner_of(here, core, hop, hops) * RECORDS
            at = RECORDS * hop
            values = tiles[core, at:at + RECORDS].reshape(RECORDS * STEP, LANES).astype(jnp.bfloat16)
            for turn in range(TURNS):
                rolled = values if turn == 0 else pltpu.roll(values, LANES - turn, 1)
                frames[pl.ds(first, RECORDS), turn * STEP:(turn + 1) * STEP, :] = (
                    rolled.reshape(RECORDS, STEP, LANES)
                )
    waves_copy.wait()
    units[...] = waves_ref[...].reshape(units.shape).astype(jnp.float32)
    scales_copy.wait()
    row = lax.broadcasted_iota(jnp.int32, (STEP, LANES), 0)
    lane = lax.broadcasted_iota(jnp.int32, (STEP, LANES), 1)
    own = lane >= row

    def one_pick(entry, spare):
        held = entry >= 0
        packed = jnp.maximum(entry, 0)
        template = jnp.where(held, packed & 31, acc.shape[0] // STEP - 1)
        first_row = ((packed >> 22) & 31) * SLOT_ROWS + ((packed >> 20) & (CAP - 1))
        station = (packed >> 5) & 15
        lag = (packed >> 9) & 2047
        total = jnp.zeros((STEP, LANES), jnp.float32)
        for c in range(3):
            record = (station >> 1) * RECORDS + 2 * c + (station & 1)
            before = jnp.zeros((STEP, LANES), jnp.float32)
            columns = []
            for tile in range(TILES):
                at = first_row + (c * TILES + tile) * CAP
                wave = units[pl.ds(at, STEP, stride=0), :]
                spread = pltpu.roll(wave, 0, 1, stride=1, stride_axis=0)
                columns.append(jnp.where(own, spread, before).astype(jnp.bfloat16))
                before = spread
            columns.append(jnp.where(own, 0.0, before).astype(jnp.bfloat16))
            left = jnp.concatenate(
                [jnp.concatenate(columns[i:i + 2], axis=1) for i in range(0, TILES + 1, 2)], axis=0
            )
            product = jnp.dot(left, frames[record], preferred_element_type=jnp.float32)
            summed = product[:STEP]
            for part in range(1, (TILES + 1) // 2):
                later = product[part * STEP:(part + 1) * STEP]
                summed = summed + pltpu.roll(later, LANES - TURNS * part, 1)
            total = total + summed * scales[record]
        first = pltpu.roll(total, LANES - (lag >> 5), 1)
        twice[spare, 0:STEP, :] = first
        twice[spare, STEP:2 * STEP, :] = pltpu.roll(first, LANES - 1, 1)
        shifted = twice[spare, pl.ds(lag & (STEP - 1), STEP), :]
        return pl.ds(pl.multiple_of(template * STEP, STEP), STEP), shifted

    @pl.loop(0, (count + UNROLL - 1) // UNROLL)
    def _(index):
        done = [one_pick(entries[index * UNROLL + spare], spare) for spare in range(UNROLL)]
        for rows, shifted in done:
            acc[rows, :] += shifted

    for group in range(STEP // 4):
        parts = [acc[pl.ds(4 * group + j, STEP, stride=STEP), :] for j in range(4)]
        turned = jnp.concatenate(parts, axis=0).T
        dense[pl.ds(group, OUT_BLOCKS, stride=8), :] = turned[:OUT_BLOCKS]
    for part in range(out_ref.shape[1] // LANES):
        rows = dense[pl.ds(part, out_ref.shape[0], stride=3), :]
        out_ref[:, part * LANES:(part + 1) * LANES] = rows.astype(out_ref.dtype)


SMEM = pl.BlockSpec(memory_space=pltpu.SMEM)
VMEM = pl.BlockSpec(memory_space=pltpu.VMEM)
ANY = pl.BlockSpec(memory_space=pl.ANY)
HBM = pl.BlockSpec(memory_space=pltpu.HBM)


def slot_waves(index, pick_station, template_waves, peers):
    return pl.pallas_call(
        select_kernel,
        out_shape=jax.ShapeDtypeStruct((peers, SLOT_ROWS, LANES), jnp.bfloat16),
        in_specs=[SMEM, VMEM, VMEM],
        out_specs=VMEM,
        scratch_shapes=[pltpu.VMEM((peers * SLOT_ROWS, LANES), jnp.float32)],
        compiler_params=pltpu.CompilerParams(vmem_limit_bytes=4 * 1024 * 1024),
        cost_estimate=pl.CostEstimate(flops=16_000_000, transcendentals=100, bytes_accessed=620_000),
        name="select_waves",
    )(index, pick_station, template_waves)


def scales_and_entries(index, channel_mask, pick_station, pick_lag, rows):
    slot_count = pick_station.shape[1] * CAP
    return pl.pallas_call(
        scales_kernel,
        out_shape=(
            jax.ShapeDtypeStruct((2 * rows[0].shape[0], STEP, LANES), jnp.float32),
            jax.ShapeDtypeStruct((slot_count + UNROLL + 1,), jnp.int32),
        ),
        in_specs=[SMEM, HBM, VMEM, VMEM, VMEM, VMEM],
        out_specs=(VMEM, SMEM),
        scratch_shapes=[
            pltpu.VMEM((CAP, pick_station.shape[1]), jnp.int32),
            pltpu.SMEM((CAP, pick_station.shape[1]), jnp.int32),
            pltpu.SMEM(channel_mask.shape, jnp.int32),
            pltpu.SemaphoreType.DMA((2,)),
        ],
        compiler_params=pltpu.CompilerParams(vmem_limit_bytes=8 * 1024 * 1024),
        cost_estimate=pl.CostEstimate(flops=6000_000_000, transcendentals=200_000, bytes_accessed=2_000_000),
        name="record_scales",
    )(index, channel_mask, pick_station, pick_lag, *rows)


def partial_stack(entries, index, rows, scales, received, group_size):
    peers = received.shape[0]
    slot_count = peers * CAP
    lines = NT * group_size // LANES
    records = scales.shape[0]
    return pl.pallas_call(
        stack_kernel,
        out_shape=jax.ShapeDtypeStruct((slot_count, lines * LANES // slot_count), jnp.bfloat16),
        in_specs=[SMEM, SMEM, ANY, ANY, ANY, ANY],
        out_specs=VMEM,
        scratch_shapes=[
            pltpu.VMEM(received.shape, jnp.bfloat16),
            pltpu.VMEM((2,) + rows[0].shape, jnp.float32),
            pltpu.VMEM(scales.shape, jnp.float32),
            pltpu.VMEM((records, TURNS * STEP, LANES), jnp.bfloat16),
            pltpu.VMEM((peers * SLOT_ROWS, LANES), jnp.float32),
            pltpu.VMEM(((group_size + 1) * STEP, LANES), jnp.float32),
            pltpu.VMEM((UNROLL, 2 * STEP, LANES), jnp.float32),
            pltpu.VMEM((lines, LANES), jnp.float32),
            pltpu.SemaphoreType.DMA((4,)),
        ],
        compiler_params=pltpu.CompilerParams(vmem_limit_bytes=16 * 1024 * 1024),
        cost_estimate=pl.CostEstimate(flops=200_000_000, transcendentals=0, bytes_accessed=8_000_000),
        name="stack_picks",
    )(entries, index, *rows, scales, received)


def body(station_data, channel_mask, template_waves, pick_station, pick_lag):
    sta_size = lax.axis_size("sta")
    tpl_size = lax.axis_size("tpl")
    group_size = pick_station.shape[0]
    stations_here = station_data.shape[1]
    index = jnp.stack([lax.axis_index("sta"), lax.axis_index("tpl")]).astype(jnp.int32)

    tiles = station_data.reshape(3, stations_here, BLOCKS, STEP).transpose(0, 1, 3, 2)
    tiles = jnp.pad(tiles, ((0, 0), (0, 0), (0, 0), (0, LANES - BLOCKS)))
    own = tiles.reshape(3 * stations_here, STEP, LANES)
    near = [own]
    for hop in range(2, tpl_size, 2):
        near.append(lax.ppermute(own, "tpl", [(i, (i + hop) % tpl_size) for i in range(tpl_size)]))
    near = jnp.concatenate(near, axis=0)
    rows = [near, lax.ppermute(near, "tpl", [(i, i ^ 1) for i in range(tpl_size)])]

    waves = template_waves.reshape(group_size, 3, L).transpose(1, 0, 2)
    outgoing = slot_waves(index, pick_station, waves, sta_size)
    received = lax.all_to_all(outgoing, "sta", split_axis=0, concat_axis=0, tiled=True)

    scales, entries = scales_and_entries(index, channel_mask, pick_station, pick_lag, rows)
    partial_sums = partial_stack(entries, index, rows, scales, received, group_size)
    arrived = lax.all_to_all(partial_sums, "sta", split_axis=0, concat_axis=0, tiled=True)
    arrived = arrived.reshape(sta_size, CAP, -1).astype(jnp.float32)
    return jnp.sum(arrived, axis=0).reshape(NT // sta_size, group_size)


def solution(mesh):
    in_specs = (
        P(None, ("sta", "tpl"), None),
        P(None, "sta"),
        P("tpl", "sta", None, None),
        P("tpl", None),
        P("tpl", None),
    )
    return jax.shard_map(body, mesh=mesh, in_specs=in_specs, out_specs=P("sta", "tpl"), check_vma=False)
```

```python
import jax
import jax.numpy as jnp
from jax import lax
from jax.experimental import pallas as pl
from jax.experimental.pallas import tpu as pltpu
from jax.sharding import PartitionSpec as P

NT = 1536
L = 640
LAGS = 1024
SAMPLES = 3200
CAP = 4
STEP = 32
LANES = 128
BLOCKS = SAMPLES // STEP
OUT_BLOCKS = NT // STEP
TILES = L // LANES
TURNS = 8
UNROLL = 8
SLOT_ROWS = 64
RECORDS = 6
STATION_BITS = 4
EPSILON = 1e-05
VALID = 1 << 27


def exclusive_prefix(values):
    lanes = values.shape[-1]
    groups = values.reshape(-1, 8, lanes)
    row = lax.broadcasted_iota(jnp.int32, groups.shape, 1)
    total = groups
    for shift in (1, 2, 4):
        total = total + jnp.where(row >= shift, pltpu.roll(total, shift, 1), 0.0)
    inner = jnp.where(row >= 1, pltpu.roll(total, 1, 1), 0.0).reshape(-1, STEP // 8, 8, lanes)
    last = total.reshape(-1, STEP // 8, 8, lanes)[:, :, 7:8]
    pieces = [inner[:, 0:1]]
    carry = last[:, 0:1]
    for group in range(1, STEP // 8):
        pieces.append(inner[:, group:group + 1] + carry)
        carry = carry + last[:, group:group + 1]
    return jnp.concatenate(pieces, axis=1).reshape(values.shape)


def window_sums(values):
    width = values.shape[-1]
    span = L // STEP
    ahead = pltpu.roll(values, width - span, 1) - values
    two = jnp.sum(values.reshape(-1, STEP, width), axis=1)
    two = two + pltpu.roll(two, width - 1, 1)
    four = two + pltpu.roll(two, width - 2, 1)
    eight = four + pltpu.roll(four, width - 4, 1)
    sixteen = eight + pltpu.roll(eight, width - 8, 1)
    whole = sixteen + pltpu.roll(four, width - 16, 1)
    inner = exclusive_prefix(ahead).reshape(-1, STEP, width)
    return whole[:, None, :] + inner


def select_kernel(index_ref, station_ref, waves_ref, out_ref, staged):
    group_size = station_ref.shape[0]
    square = (group_size, group_size)
    row = lax.broadcasted_iota(jnp.int32, square, 0)
    column = lax.broadcasted_iota(jnp.int32, square, 1)
    owners = station_ref[...] >> STATION_BITS
    down = jnp.sum(jnp.where(column == index_ref[0], owners, 0), axis=1, keepdims=True)
    down = jnp.broadcast_to(down, square)
    across = jnp.sum(jnp.where(row == column, down, 0), axis=0, keepdims=True)
    same = (down == across) & (row < column)
    place = jnp.sum(same.astype(jnp.int32), axis=0, keepdims=True)
    slot = across * CAP + place
    peers = out_ref.shape[0]
    line = lax.broadcasted_iota(jnp.int32, (2 * CAP * peers, group_size), 0)
    wanted = (line >> 3) * CAP + (line & (CAP - 1)) == slot
    selects = [wanted & ((line >> 2) & 1 == half) for half in range(2)]
    select = jnp.concatenate([part.astype(jnp.float32) for part in selects], axis=1).astype(jnp.bfloat16)
    pieces = []
    for c in range(3):
        values = waves_ref[c].astype(jnp.float32)
        centred = values - jnp.mean(values, axis=-1, keepdims=True)
        power = jnp.mean(centred * centred, axis=-1, keepdims=True)
        unit = (centred / jnp.sqrt(power + EPSILON)).astype(jnp.bfloat16)
        pieces += [unit[:, tile * LANES:(tile + 1) * LANES] for tile in range(TILES)]
    pieces.append(jnp.zeros((group_size, LANES), jnp.bfloat16))
    for pair in range(len(pieces) // 2):
        both = jnp.concatenate(pieces[2 * pair:2 * pair + 2], axis=0)
        picked = jnp.dot(select, both, preferred_element_type=jnp.float32)
        staged[:, 2 * CAP * pair:2 * CAP * (pair + 1), :] = picked.reshape(peers, 2 * CAP, LANES)
    out_ref[...] = staged[...].astype(jnp.bfloat16)


def owner_of(here, core, hop, hops):
    return ((here - 2 * hop) & (2 * hops - 1)) ^ core


def scales_kernel(index_ref, mask_hbm, station_ref, lag_ref, near_ref, far_ref, scales, entries,
                  meta_vmem, meta, mask_ref, sems):
    mask_copy = pltpu.make_async_copy(mask_hbm, mask_ref, sems.at[0])
    mask_copy.start()
    square = station_ref.shape
    row = lax.broadcasted_iota(jnp.int32, square, 0)
    column = lax.broadcasted_iota(jnp.int32, square, 1)
    stations = station_ref[...]
    landing = (stations >> STATION_BITS) == index_ref[0]
    earlier = (column < row).astype(jnp.float32).astype(jnp.bfloat16)
    arrival = jnp.dot(earlier, landing.astype(jnp.float32).astype(jnp.bfloat16), preferred_element_type=jnp.float32)
    local = stations & (2**STATION_BITS - 1)
    packed = VALID + (column << 22) + (lag_ref[...] << 9) + (local << 5) + row
    for k in range(CAP):
        held = landing & (arrival.astype(jnp.int32) == k)
        meta_vmem[k:k + 1, :] = jnp.sum(jnp.where(held, packed, 0), axis=0, keepdims=True)
    meta_copy = pltpu.make_async_copy(meta_vmem, meta, sems.at[1])
    meta_copy.start()

    here = index_ref[1]
    hops = near_ref.shape[0] // RECORDS
    mask_copy.wait()
    for core, tile_ref in enumerate((near_ref, far_ref)):
        for hop in range(hops):
            owner = owner_of(here, core, hop, hops)
            values = tile_ref[hop * RECORDS:(hop + 1) * RECORDS].reshape(RECORDS * STEP, LANES)
            mean_one = window_sums(values) * (1.0 / L)
            mean_two = window_sums(values * values) * (1.0 / L)
            factor = lax.rsqrt(mean_two - mean_one * mean_one + EPSILON)
            for record in range(RECORDS):
                weight = mask_ref[record >> 1, owner * 2 + (record & 1)].astype(jnp.float32) * (1.0 / L)
                scales[owner * RECORDS + record] = factor[record] * weight

    meta_copy.wait()

    def list_slot(slot, count):
        packed = meta[slot & (CAP - 1), slot >> 2]
        entries[count] = packed + ((slot & (CAP - 1)) << 20)
        return count + (packed >> 27)

    total = meta.shape[1] * CAP
    count = lax.fori_loop(0, total, list_slot, jnp.int32(0), unroll=16)
    for spare in range(UNROLL):
        entries[count + spare] = -1
    entries[total + UNROLL] = count


def stack_kernel(entries, index_ref, near_ref, far_ref, scales, waves_ref, out_ref,
                 frames, units, acc, twice, dense):
    here = index_ref[1]
    hops = near_ref.shape[0] // RECORDS
    count = entries[entries.shape[0] - 1]
    acc[...] = jnp.zeros_like(acc)
    units[...] = waves_ref[...].reshape(units.shape).astype(jnp.float32)

    for core, tile_ref in enumerate((near_ref, far_ref)):
        for hop in range(hops):
            first = owner_of(here, core, hop, hops) * RECORDS
            at = RECORDS * hop
            values = tile_ref[at:at + RECORDS].reshape(RECORDS * STEP, LANES).astype(jnp.bfloat16)
            for turn in range(TURNS):
                rolled = values if turn == 0 else pltpu.roll(values, LANES - turn, 1)
                frames[pl.ds(first, RECORDS), turn * STEP:(turn + 1) * STEP, :] = (
                    rolled.reshape(RECORDS, STEP, LANES)
                )
    row = lax.broadcasted_iota(jnp.int32, (STEP, LANES), 0)
    lane = lax.broadcasted_iota(jnp.int32, (STEP, LANES), 1)
    own = lane >= row

    def one_pick(entry, spare):
        held = entry >= 0
        packed = jnp.maximum(entry, 0)
        template = jnp.where(held, packed & 31, acc.shape[0] // STEP - 1)
        first_row = ((packed >> 22) & 31) * SLOT_ROWS + ((packed >> 20) & (CAP - 1))
        station = (packed >> 5) & 15
        lag = (packed >> 9) & 2047
        total = jnp.zeros((STEP, LANES), jnp.float32)
        for c in range(3):
            record = (station >> 1) * RECORDS + 2 * c + (station & 1)
            before = jnp.zeros((STEP, LANES), jnp.float32)
            columns = []
            for tile in range(TILES):
                at = first_row + (c * TILES + tile) * CAP
                wave = units[pl.ds(at, STEP, stride=0), :]
                spread = pltpu.roll(wave, 0, 1, stride=1, stride_axis=0)
                columns.append(jnp.where(own, spread, before).astype(jnp.bfloat16))
                before = spread
            columns.append(jnp.where(own, 0.0, before).astype(jnp.bfloat16))
            left = jnp.concatenate(
                [jnp.concatenate(columns[i:i + 2], axis=1) for i in range(0, TILES + 1, 2)], axis=0
            )
            product = jnp.dot(left, frames[record], preferred_element_type=jnp.float32)
            summed = product[:STEP]
            for part in range(1, (TILES + 1) // 2):
                later = product[part * STEP:(part + 1) * STEP]
                summed = summed + pltpu.roll(later, LANES - TURNS * part, 1)
            total = total + summed * scales[record]
        first = pltpu.roll(total, LANES - (lag >> 5), 1)
        twice[spare, 0:STEP, :] = first
        twice[spare, STEP:2 * STEP, :] = pltpu.roll(first, LANES - 1, 1)
        shifted = twice[spare, pl.ds(lag & (STEP - 1), STEP), :]
        return pl.ds(pl.multiple_of(template * STEP, STEP), STEP), shifted

    @pl.loop(0, (count + UNROLL - 1) // UNROLL)
    def _(index):
        done = [one_pick(entries[index * UNROLL + spare], spare) for spare in range(UNROLL)]
        for rows, shifted in done:
            acc[rows, :] += shifted

    for group in range(STEP // 4):
        parts = [acc[pl.ds(4 * group + j, STEP, stride=STEP), :] for j in range(4)]
        turned = jnp.concatenate(parts, axis=0).T
        dense[pl.ds(group, OUT_BLOCKS, stride=8), :] = turned[:OUT_BLOCKS]
    for part in range(out_ref.shape[1] // LANES):
        rows = dense[pl.ds(part, out_ref.shape[0], stride=3), :]
        out_ref[:, part * LANES:(part + 1) * LANES] = rows.astype(out_ref.dtype)


SMEM = pl.BlockSpec(memory_space=pltpu.SMEM)
VMEM = pl.BlockSpec(memory_space=pltpu.VMEM)
HBM = pl.BlockSpec(memory_space=pltpu.HBM)


def slot_waves(index, pick_station, template_waves, peers):
    return pl.pallas_call(
        select_kernel,
        out_shape=jax.ShapeDtypeStruct((peers, SLOT_ROWS, LANES), jnp.bfloat16),
        in_specs=[SMEM, VMEM, VMEM],
        out_specs=VMEM,
        scratch_shapes=[pltpu.VMEM((peers, SLOT_ROWS, LANES), jnp.float32)],
        compiler_params=pltpu.CompilerParams(vmem_limit_bytes=4 * 1024 * 1024),
        cost_estimate=pl.CostEstimate(flops=16_000_000, transcendentals=100, bytes_accessed=620_000),
        name="select_waves",
    )(index, pick_station, template_waves)


def scales_and_entries(index, channel_mask, pick_station, pick_lag, rows):
    slot_count = pick_station.shape[1] * CAP
    return pl.pallas_call(
        scales_kernel,
        out_shape=(
            jax.ShapeDtypeStruct((2 * rows[0].shape[0], STEP, LANES), jnp.float32),
            jax.ShapeDtypeStruct((slot_count + UNROLL + 1,), jnp.int32),
        ),
        in_specs=[SMEM, HBM, VMEM, VMEM, VMEM, VMEM],
        out_specs=(VMEM, SMEM),
        scratch_shapes=[
            pltpu.VMEM((CAP, pick_station.shape[1]), jnp.int32),
            pltpu.SMEM((CAP, pick_station.shape[1]), jnp.int32),
            pltpu.SMEM(channel_mask.shape, jnp.int32),
            pltpu.SemaphoreType.DMA((2,)),
        ],
        compiler_params=pltpu.CompilerParams(vmem_limit_bytes=8 * 1024 * 1024),
        cost_estimate=pl.CostEstimate(flops=6000_000_000, transcendentals=200_000, bytes_accessed=2_000_000),
        name="record_scales",
    )(index, channel_mask, pick_station, pick_lag, *rows)


def partial_stack(entries, index, rows, scales, received, group_size):
    peers = received.shape[0]
    slot_count = peers * CAP
    lines = NT * group_size // LANES
    records = scales.shape[0]
    return pl.pallas_call(
        stack_kernel,
        out_shape=jax.ShapeDtypeStruct((slot_count, lines * LANES // slot_count), jnp.bfloat16),
        in_specs=[SMEM, SMEM, VMEM, VMEM, VMEM, VMEM],
        out_specs=VMEM,
        scratch_shapes=[
            pltpu.VMEM((records, TURNS * STEP, LANES), jnp.bfloat16),
            pltpu.VMEM((peers * SLOT_ROWS, LANES), jnp.float32),
            pltpu.VMEM(((group_size + 1) * STEP, LANES), jnp.float32),
            pltpu.VMEM((UNROLL, 2 * STEP, LANES), jnp.float32),
            pltpu.VMEM((lines, LANES), jnp.float32),
        ],
        compiler_params=pltpu.CompilerParams(vmem_limit_bytes=16 * 1024 * 1024),
        cost_estimate=pl.CostEstimate(flops=200_000_000, transcendentals=0, bytes_accessed=8_000_000),
        name="stack_picks",
    )(entries, index, *rows, scales, received)


def body(station_data, channel_mask, template_waves, pick_station, pick_lag):
    sta_size = lax.axis_size("sta")
    tpl_size = lax.axis_size("tpl")
    group_size = pick_station.shape[0]
    stations_here = station_data.shape[1]
    index = jnp.stack([lax.axis_index("sta"), lax.axis_index("tpl")]).astype(jnp.int32)

    tiles = station_data.reshape(3, stations_here, BLOCKS, STEP).transpose(0, 1, 3, 2)
    tiles = jnp.pad(tiles, ((0, 0), (0, 0), (0, 0), (0, LANES - BLOCKS)))
    own = tiles.reshape(3 * stations_here, STEP, LANES)
    near = [own]
    for hop in range(2, tpl_size, 2):
        near.append(lax.ppermute(own, "tpl", [(i, (i + hop) % tpl_size) for i in range(tpl_size)]))
    near = jnp.concatenate(near, axis=0)
    rows = [near, lax.ppermute(near, "tpl", [(i, i ^ 1) for i in range(tpl_size)])]

    waves = template_waves.reshape(group_size, 3, L).transpose(1, 0, 2)
    outgoing = slot_waves(index, pick_station, waves, sta_size)
    received = lax.all_to_all(outgoing, "sta", split_axis=0, concat_axis=0, tiled=True)

    scales, entries = scales_and_entries(index, channel_mask, pick_station, pick_lag, rows)
    partial_sums = partial_stack(entries, index, rows, scales, received, group_size)
    arrived = lax.all_to_all(partial_sums, "sta", split_axis=0, concat_axis=0, tiled=True)
    arrived = arrived.reshape(sta_size, CAP, -1).astype(jnp.float32)
    return jnp.sum(arrived, axis=0).reshape(NT // sta_size, group_size)


def solution(mesh):
    in_specs = (
        P(None, ("sta", "tpl"), None),
        P(None, "sta"),
        P("tpl", "sta", None, None),
        P("tpl", None),
        P("tpl", None),
    )
    return jax.shard_map(body, mesh=mesh, in_specs=in_specs, out_specs=P("sta", "tpl"), check_vma=False)
```

```python
import jax
import jax.numpy as jnp
from jax import lax
from jax.experimental import pallas as pl
from jax.experimental.pallas import tpu as pltpu
from jax.sharding import PartitionSpec as P

NT = 1536
L = 640
LAGS = 1024
SAMPLES = 3200
CAP = 4
STEP = 32
LANES = 128
BLOCKS = SAMPLES // STEP
OUT_BLOCKS = NT // STEP
TILES = L // LANES
TURNS = 8
UNROLL = 16
SLOT_ROWS = 64
RECORDS = 6
STATION_BITS = 4
EPSILON = 1e-05
VALID = 1 << 27


def exclusive_prefix(values):
    lanes = values.shape[-1]
    groups = values.reshape(-1, 8, lanes)
    row = lax.broadcasted_iota(jnp.int32, groups.shape, 1)
    total = groups
    for shift in (1, 2, 4):
        total = total + jnp.where(row >= shift, pltpu.roll(total, shift, 1), 0.0)
    inner = jnp.where(row >= 1, pltpu.roll(total, 1, 1), 0.0).reshape(-1, STEP // 8, 8, lanes)
    last = total.reshape(-1, STEP // 8, 8, lanes)[:, :, 7:8]
    pieces = [inner[:, 0:1]]
    carry = last[:, 0:1]
    for group in range(1, STEP // 8):
        pieces.append(inner[:, group:group + 1] + carry)
        carry = carry + last[:, group:group + 1]
    return jnp.concatenate(pieces, axis=1).reshape(values.shape)


def window_sums(values):
    width = values.shape[-1]
    span = L // STEP
    ahead = pltpu.roll(values, width - span, 1) - values
    two = jnp.sum(values.reshape(-1, STEP, width), axis=1)
    two = two + pltpu.roll(two, width - 1, 1)
    four = two + pltpu.roll(two, width - 2, 1)
    eight = four + pltpu.roll(four, width - 4, 1)
    sixteen = eight + pltpu.roll(eight, width - 8, 1)
    whole = sixteen + pltpu.roll(four, width - 16, 1)
    inner = exclusive_prefix(ahead).reshape(-1, STEP, width)
    return whole[:, None, :] + inner


def select_kernel(index_ref, station_ref, waves_ref, out_ref, staged):
    group_size = station_ref.shape[0]
    square = (group_size, group_size)
    row = lax.broadcasted_iota(jnp.int32, square, 0)
    column = lax.broadcasted_iota(jnp.int32, square, 1)
    owners = station_ref[...] >> STATION_BITS
    down = jnp.sum(jnp.where(column == index_ref[0], owners, 0), axis=1, keepdims=True)
    down = jnp.broadcast_to(down, square)
    across = jnp.sum(jnp.where(row == column, down, 0), axis=0, keepdims=True)
    same = (down == across) & (row < column)
    place = jnp.sum(same.astype(jnp.int32), axis=0, keepdims=True)
    slot = across * CAP + place
    peers = out_ref.shape[0]
    line = lax.broadcasted_iota(jnp.int32, (2 * CAP * peers, group_size), 0)
    wanted = (line >> 3) * CAP + (line & (CAP - 1)) == slot
    selects = [wanted & ((line >> 2) & 1 == half) for half in range(2)]
    select = jnp.concatenate([part.astype(jnp.float32) for part in selects], axis=1).astype(jnp.bfloat16)
    pieces = []
    for c in range(3):
        values = waves_ref[c].astype(jnp.float32)
        centred = values - jnp.mean(values, axis=-1, keepdims=True)
        power = jnp.mean(centred * centred, axis=-1, keepdims=True)
        unit = (centred / jnp.sqrt(power + EPSILON)).astype(jnp.bfloat16)
        pieces += [unit[:, tile * LANES:(tile + 1) * LANES] for tile in range(TILES)]
    pieces.append(jnp.zeros((group_size, LANES), jnp.bfloat16))
    for pair in range(len(pieces) // 2):
        both = jnp.concatenate(pieces[2 * pair:2 * pair + 2], axis=0)
        picked = jnp.dot(select, both, preferred_element_type=jnp.float32)
        staged[:, 2 * CAP * pair:2 * CAP * (pair + 1), :] = picked.reshape(peers, 2 * CAP, LANES)
    out_ref[...] = staged[...].astype(jnp.bfloat16)


def owner_of(here, core, hop, hops):
    return ((here - 2 * hop) & (2 * hops - 1)) ^ core


def scales_kernel(index_ref, mask_hbm, station_ref, lag_ref, near_ref, far_ref, scales, entries,
                  meta_vmem, meta, mask_ref, sems):
    mask_copy = pltpu.make_async_copy(mask_hbm, mask_ref, sems.at[0])
    mask_copy.start()
    square = station_ref.shape
    row = lax.broadcasted_iota(jnp.int32, square, 0)
    column = lax.broadcasted_iota(jnp.int32, square, 1)
    stations = station_ref[...]
    landing = (stations >> STATION_BITS) == index_ref[0]
    earlier = (column < row).astype(jnp.float32).astype(jnp.bfloat16)
    arrival = jnp.dot(earlier, landing.astype(jnp.float32).astype(jnp.bfloat16), preferred_element_type=jnp.float32)
    local = stations & (2**STATION_BITS - 1)
    packed = VALID + (column << 22) + (lag_ref[...] << 9) + (local << 5) + row
    for k in range(CAP):
        held = landing & (arrival.astype(jnp.int32) == k)
        meta_vmem[k:k + 1, :] = jnp.sum(jnp.where(held, packed, 0), axis=0, keepdims=True)
    meta_copy = pltpu.make_async_copy(meta_vmem, meta, sems.at[1])
    meta_copy.start()

    here = index_ref[1]
    hops = near_ref.shape[0] // RECORDS
    mask_copy.wait()
    for core, tile_ref in enumerate((near_ref, far_ref)):
        for hop in range(hops):
            owner = owner_of(here, core, hop, hops)
            values = tile_ref[hop * RECORDS:(hop + 1) * RECORDS].reshape(RECORDS * STEP, LANES)
            mean_one = window_sums(values) * (1.0 / L)
            mean_two = window_sums(values * values) * (1.0 / L)
            factor = lax.rsqrt(mean_two - mean_one * mean_one + EPSILON)
            for record in range(RECORDS):
                weight = mask_ref[record >> 1, owner * 2 + (record & 1)].astype(jnp.float32) * (1.0 / L)
                scales[owner * RECORDS + record] = factor[record] * weight

    meta_copy.wait()

    def list_slot(slot, count):
        packed = meta[slot & (CAP - 1), slot >> 2]
        entries[count] = packed + ((slot & (CAP - 1)) << 20)
        return count + (packed >> 27)

    total = meta.shape[1] * CAP
    count = lax.fori_loop(0, total, list_slot, jnp.int32(0), unroll=16)
    for spare in range(UNROLL):
        entries[count + spare] = -1
    entries[total + UNROLL] = count


def stack_kernel(entries, index_ref, near_ref, far_ref, scales, waves_ref, out_ref,
                 frames, units, acc, twice, dense):
    here = index_ref[1]
    hops = near_ref.shape[0] // RECORDS
    count = entries[entries.shape[0] - 1]
    acc[...] = jnp.zeros_like(acc)
    units[...] = waves_ref[...].reshape(units.shape).astype(jnp.float32)

    for core, tile_ref in enumerate((near_ref, far_ref)):
        for hop in range(hops):
            first = owner_of(here, core, hop, hops) * RECORDS
            at = RECORDS * hop
            values = tile_ref[at:at + RECORDS].reshape(RECORDS * STEP, LANES).astype(jnp.bfloat16)
            for turn in range(TURNS):
                rolled = values if turn == 0 else pltpu.roll(values, LANES - turn, 1)
                frames[pl.ds(first, RECORDS), turn * STEP:(turn + 1) * STEP, :] = (
                    rolled.reshape(RECORDS, STEP, LANES)
                )
    row = lax.broadcasted_iota(jnp.int32, (STEP, LANES), 0)
    lane = lax.broadcasted_iota(jnp.int32, (STEP, LANES), 1)
    own = lane >= row

    def one_pick(entry, spare):
        held = entry >= 0
        packed = jnp.maximum(entry, 0)
        template = jnp.where(held, packed & 31, acc.shape[0] // STEP - 1)
        first_row = ((packed >> 22) & 31) * SLOT_ROWS + ((packed >> 20) & (CAP - 1))
        station = (packed >> 5) & 15
        lag = (packed >> 9) & 2047
        total = jnp.zeros((STEP, LANES), jnp.float32)
        for c in range(3):
            record = (station >> 1) * RECORDS + 2 * c + (station & 1)
            before = jnp.zeros((STEP, LANES), jnp.float32)
            columns = []
            for tile in range(TILES):
                at = first_row + (c * TILES + tile) * CAP
                wave = units[pl.ds(at, STEP, stride=0), :]
                spread = pltpu.roll(wave, 0, 1, stride=1, stride_axis=0)
                columns.append(jnp.where(own, spread, before).astype(jnp.bfloat16))
                before = spread
            columns.append(jnp.where(own, 0.0, before).astype(jnp.bfloat16))
            left = jnp.concatenate(
                [jnp.concatenate(columns[i:i + 2], axis=1) for i in range(0, TILES + 1, 2)], axis=0
            )
            product = jnp.dot(left, frames[record], preferred_element_type=jnp.float32)
            summed = product[:STEP]
            for part in range(1, (TILES + 1) // 2):
                later = product[part * STEP:(part + 1) * STEP]
                summed = summed + pltpu.roll(later, LANES - TURNS * part, 1)
            total = total + summed * scales[record]
        first = pltpu.roll(total, LANES - (lag >> 5), 1)
        twice[spare, 0:STEP, :] = first
        twice[spare, STEP:2 * STEP, :] = pltpu.roll(first, LANES - 1, 1)
        shifted = twice[spare, pl.ds(lag & (STEP - 1), STEP), :]
        return pl.ds(pl.multiple_of(template * STEP, STEP), STEP), shifted

    @pl.loop(0, (count + UNROLL - 1) // UNROLL)
    def _(index):
        done = [one_pick(entries[index * UNROLL + spare], spare) for spare in range(UNROLL)]
        for rows, shifted in done:
            acc[rows, :] += shifted

    for group in range(STEP // 4):
        parts = [acc[pl.ds(4 * group + j, STEP, stride=STEP), :] for j in range(4)]
        turned = jnp.concatenate(parts, axis=0).T
        dense[pl.ds(group, OUT_BLOCKS, stride=8), :] = turned[:OUT_BLOCKS]
    for part in range(out_ref.shape[1] // LANES):
        rows = dense[pl.ds(part, out_ref.shape[0], stride=3), :]
        out_ref[:, part * LANES:(part + 1) * LANES] = rows.astype(out_ref.dtype)


SMEM = pl.BlockSpec(memory_space=pltpu.SMEM)
VMEM = pl.BlockSpec(memory_space=pltpu.VMEM)
HBM = pl.BlockSpec(memory_space=pltpu.HBM)


def slot_waves(index, pick_station, template_waves, peers):
    return pl.pallas_call(
        select_kernel,
        out_shape=jax.ShapeDtypeStruct((peers, SLOT_ROWS, LANES), jnp.bfloat16),
        in_specs=[SMEM, VMEM, VMEM],
        out_specs=VMEM,
        scratch_shapes=[pltpu.VMEM((peers, SLOT_ROWS, LANES), jnp.float32)],
        compiler_params=pltpu.CompilerParams(vmem_limit_bytes=4 * 1024 * 1024),
        cost_estimate=pl.CostEstimate(flops=16_000_000, transcendentals=100, bytes_accessed=620_000),
        name="select_waves",
    )(index, pick_station, template_waves)


def scales_and_entries(index, channel_mask, pick_station, pick_lag, rows):
    slot_count = pick_station.shape[1] * CAP
    return pl.pallas_call(
        scales_kernel,
        out_shape=(
            jax.ShapeDtypeStruct((2 * rows[0].shape[0], STEP, LANES), jnp.float32),
            jax.ShapeDtypeStruct((slot_count + UNROLL + 1,), jnp.int32),
        ),
        in_specs=[SMEM, HBM, VMEM, VMEM, VMEM, VMEM],
        out_specs=(VMEM, SMEM),
        scratch_shapes=[
            pltpu.VMEM((CAP, pick_station.shape[1]), jnp.int32),
            pltpu.SMEM((CAP, pick_station.shape[1]), jnp.int32),
            pltpu.SMEM(channel_mask.shape, jnp.int32),
            pltpu.SemaphoreType.DMA((2,)),
        ],
        compiler_params=pltpu.CompilerParams(vmem_limit_bytes=8 * 1024 * 1024),
        cost_estimate=pl.CostEstimate(flops=6000_000_000, transcendentals=200_000, bytes_accessed=2_000_000),
        name="record_scales",
    )(index, channel_mask, pick_station, pick_lag, *rows)


def partial_stack(entries, index, rows, scales, received, group_size):
    peers = received.shape[0]
    slot_count = peers * CAP
    lines = NT * group_size // LANES
    records = scales.shape[0]
    return pl.pallas_call(
        stack_kernel,
        out_shape=jax.ShapeDtypeStruct((slot_count, lines * LANES // slot_count), jnp.bfloat16),
        in_specs=[SMEM, SMEM, VMEM, VMEM, VMEM, VMEM],
        out_specs=VMEM,
        scratch_shapes=[
            pltpu.VMEM((records, TURNS * STEP, LANES), jnp.bfloat16),
            pltpu.VMEM((peers * SLOT_ROWS, LANES), jnp.float32),
            pltpu.VMEM(((group_size + 1) * STEP, LANES), jnp.float32),
            pltpu.VMEM((UNROLL, 2 * STEP, LANES), jnp.float32),
            pltpu.VMEM((lines, LANES), jnp.float32),
        ],
        compiler_params=pltpu.CompilerParams(vmem_limit_bytes=16 * 1024 * 1024),
        cost_estimate=pl.CostEstimate(flops=200_000_000, transcendentals=0, bytes_accessed=8_000_000),
        name="stack_picks",
    )(entries, index, *rows, scales, received)


def body(station_data, channel_mask, template_waves, pick_station, pick_lag):
    sta_size = lax.axis_size("sta")
    tpl_size = lax.axis_size("tpl")
    group_size = pick_station.shape[0]
    stations_here = station_data.shape[1]
    index = jnp.stack([lax.axis_index("sta"), lax.axis_index("tpl")]).astype(jnp.int32)

    tiles = station_data.reshape(3, stations_here, BLOCKS, STEP).transpose(0, 1, 3, 2)
    tiles = jnp.pad(tiles, ((0, 0), (0, 0), (0, 0), (0, LANES - BLOCKS)))
    own = tiles.reshape(3 * stations_here, STEP, LANES)
    near = [own]
    for hop in range(2, tpl_size, 2):
        near.append(lax.ppermute(own, "tpl", [(i, (i + hop) % tpl_size) for i in range(tpl_size)]))
    near = jnp.concatenate(near, axis=0)
    rows = [near, lax.ppermute(near, "tpl", [(i, i ^ 1) for i in range(tpl_size)])]

    waves = template_waves.reshape(group_size, 3, L).transpose(1, 0, 2)
    outgoing = slot_waves(index, pick_station, waves, sta_size)
    received = lax.all_to_all(outgoing, "sta", split_axis=0, concat_axis=0, tiled=True)

    scales, entries = scales_and_entries(index, channel_mask, pick_station, pick_lag, rows)
    partial_sums = partial_stack(entries, index, rows, scales, received, group_size)
    arrived = lax.all_to_all(partial_sums, "sta", split_axis=0, concat_axis=0, tiled=True)
    arrived = arrived.reshape(sta_size, CAP, -1).astype(jnp.float32)
    return jnp.sum(arrived, axis=0).reshape(NT // sta_size, group_size)


def solution(mesh):
    in_specs = (
        P(None, ("sta", "tpl"), None),
        P(None, "sta"),
        P("tpl", "sta", None, None),
        P("tpl", None),
        P("tpl", None),
    )
    return jax.shard_map(body, mesh=mesh, in_specs=in_specs, out_specs=P("sta", "tpl"), check_vma=False)
```

```python
import jax
import jax.numpy as jnp
from jax import lax
from jax.experimental import pallas as pl
from jax.experimental.pallas import tpu as pltpu
from jax.sharding import PartitionSpec as P

NT = 1536
L = 640
LAGS = 1024
SAMPLES = 3200
CAP = 4
STEP = 32
LANES = 128
BLOCKS = SAMPLES // STEP
OUT_BLOCKS = NT // STEP
TILES = L // LANES
TURNS = 8
EARLY = 5
UNROLL = 8
SLOT_ROWS = 64
RECORDS = 6
STATION_BITS = 4
EPSILON = 1e-05
VALID = 1 << 27


def exclusive_prefix(values):
    lanes = values.shape[-1]
    groups = values.reshape(-1, 8, lanes)
    row = lax.broadcasted_iota(jnp.int32, groups.shape, 1)
    total = groups
    for shift in (1, 2, 4):
        total = total + jnp.where(row >= shift, pltpu.roll(total, shift, 1), 0.0)
    inner = jnp.where(row >= 1, pltpu.roll(total, 1, 1), 0.0).reshape(-1, STEP // 8, 8, lanes)
    last = total.reshape(-1, STEP // 8, 8, lanes)[:, :, 7:8]
    pieces = [inner[:, 0:1]]
    carry = last[:, 0:1]
    for group in range(1, STEP // 8):
        pieces.append(inner[:, group:group + 1] + carry)
        carry = carry + last[:, group:group + 1]
    return jnp.concatenate(pieces, axis=1).reshape(values.shape)


def window_sums(values):
    width = values.shape[-1]
    span = L // STEP
    ahead = pltpu.roll(values, width - span, 1) - values
    two = jnp.sum(values.reshape(-1, STEP, width), axis=1)
    two = two + pltpu.roll(two, width - 1, 1)
    four = two + pltpu.roll(two, width - 2, 1)
    eight = four + pltpu.roll(four, width - 4, 1)
    sixteen = eight + pltpu.roll(eight, width - 8, 1)
    whole = sixteen + pltpu.roll(four, width - 16, 1)
    inner = exclusive_prefix(ahead).reshape(-1, STEP, width)
    return whole[:, None, :] + inner


def select_kernel(index_ref, station_ref, waves_ref, out_ref, staged):
    group_size = station_ref.shape[0]
    square = (group_size, group_size)
    row = lax.broadcasted_iota(jnp.int32, square, 0)
    column = lax.broadcasted_iota(jnp.int32, square, 1)
    owners = station_ref[...] >> STATION_BITS
    down = jnp.sum(jnp.where(column == index_ref[0], owners, 0), axis=1, keepdims=True)
    down = jnp.broadcast_to(down, square)
    across = jnp.sum(jnp.where(row == column, down, 0), axis=0, keepdims=True)
    same = (down == across) & (row < column)
    place = jnp.sum(same.astype(jnp.int32), axis=0, keepdims=True)
    slot = across * CAP + place
    peers = out_ref.shape[0]
    line = lax.broadcasted_iota(jnp.int32, (2 * CAP * peers, group_size), 0)
    wanted = (line >> 3) * CAP + (line & (CAP - 1)) == slot
    selects = [wanted & ((line >> 2) & 1 == half) for half in range(2)]
    select = jnp.concatenate([part.astype(jnp.float32) for part in selects], axis=1).astype(jnp.bfloat16)
    pieces = []
    for c in range(3):
        values = waves_ref[c].astype(jnp.float32)
        centred = values - jnp.mean(values, axis=-1, keepdims=True)
        power = jnp.mean(centred * centred, axis=-1, keepdims=True)
        unit = (centred / jnp.sqrt(power + EPSILON)).astype(jnp.bfloat16)
        pieces += [unit[:, tile * LANES:(tile + 1) * LANES] for tile in range(TILES)]
    pieces.append(jnp.zeros((group_size, LANES), jnp.bfloat16))
    for pair in range(len(pieces) // 2):
        both = jnp.concatenate(pieces[2 * pair:2 * pair + 2], axis=0)
        picked = jnp.dot(select, both, preferred_element_type=jnp.float32)
        staged[:, 2 * CAP * pair:2 * CAP * (pair + 1), :] = picked.reshape(peers, 2 * CAP, LANES)
    out_ref[...] = staged[...].astype(jnp.bfloat16)


def owner_of(here, core, hop, hops):
    return ((here - 2 * hop) & (2 * hops - 1)) ^ core


def scales_kernel(index_ref, mask_hbm, station_ref, lag_ref, near_ref, far_ref, scales, early, entries,
                  meta_vmem, meta, mask_ref, sems):
    mask_copy = pltpu.make_async_copy(mask_hbm, mask_ref, sems.at[0])
    mask_copy.start()
    square = station_ref.shape
    row = lax.broadcasted_iota(jnp.int32, square, 0)
    column = lax.broadcasted_iota(jnp.int32, square, 1)
    stations = station_ref[...]
    landing = (stations >> STATION_BITS) == index_ref[0]
    earlier = (column < row).astype(jnp.float32).astype(jnp.bfloat16)
    arrival = jnp.dot(earlier, landing.astype(jnp.float32).astype(jnp.bfloat16), preferred_element_type=jnp.float32)
    local = stations & (2**STATION_BITS - 1)
    packed = VALID + (column << 22) + (lag_ref[...] << 9) + (local << 5) + row
    for k in range(CAP):
        held = landing & (arrival.astype(jnp.int32) == k)
        meta_vmem[k:k + 1, :] = jnp.sum(jnp.where(held, packed, 0), axis=0, keepdims=True)
    meta_copy = pltpu.make_async_copy(meta_vmem, meta, sems.at[1])
    meta_copy.start()

    here = index_ref[1]
    hops = near_ref.shape[0] // RECORDS
    mask_copy.wait()
    for core, tile_ref in enumerate((near_ref, far_ref)):
        for hop in range(hops):
            owner = owner_of(here, core, hop, hops)
            first = owner * RECORDS
            values = tile_ref[hop * RECORDS:(hop + 1) * RECORDS].reshape(RECORDS * STEP, LANES)
            rounded = values.astype(jnp.bfloat16)
            for turn in range(EARLY):
                rolled = rounded if turn == 0 else pltpu.roll(rounded, LANES - turn, 1)
                early[pl.ds(first, RECORDS), turn * STEP:(turn + 1) * STEP, :] = rolled.reshape(RECORDS, STEP, LANES)
            mean_one = window_sums(values) * (1.0 / L)
            mean_two = window_sums(values * values) * (1.0 / L)
            factor = lax.rsqrt(mean_two - mean_one * mean_one + EPSILON)
            for record in range(RECORDS):
                weight = mask_ref[record >> 1, owner * 2 + (record & 1)].astype(jnp.float32) * (1.0 / L)
                scales[first + record] = factor[record] * weight

    meta_copy.wait()

    def list_slot(slot, count):
        packed = meta[slot & (CAP - 1), slot >> 2]
        entries[count] = packed + ((slot & (CAP - 1)) << 20)
        return count + (packed >> 27)

    total = meta.shape[1] * CAP
    count = lax.fori_loop(0, total, list_slot, jnp.int32(0), unroll=16)
    for spare in range(UNROLL):
        entries[count + spare] = -1
    entries[total + UNROLL] = count


def stack_kernel(entries, early, scales, waves_ref, out_ref, late, units, acc, twice, dense):
    count = entries[entries.shape[0] - 1]
    acc[...] = jnp.zeros_like(acc)
    units[...] = waves_ref[...].reshape(units.shape).astype(jnp.float32)

    for first in range(0, early.shape[0], RECORDS):
        values = early[first:first + RECORDS, :STEP, :].reshape(RECORDS * STEP, LANES)
        for turn in range(EARLY, TURNS):
            rolled = pltpu.roll(values, LANES - turn, 1).reshape(RECORDS, STEP, LANES)
            late[first:first + RECORDS, (turn - EARLY) * STEP:(turn - EARLY + 1) * STEP, :] = rolled
    row = lax.broadcasted_iota(jnp.int32, (STEP, LANES), 0)
    lane = lax.broadcasted_iota(jnp.int32, (STEP, LANES), 1)
    own = lane >= row

    def one_pick(entry, spare):
        held = entry >= 0
        packed = jnp.maximum(entry, 0)
        template = jnp.where(held, packed & 31, acc.shape[0] // STEP - 1)
        first_row = ((packed >> 22) & 31) * SLOT_ROWS + ((packed >> 20) & (CAP - 1))
        station = (packed >> 5) & 15
        lag = (packed >> 9) & 2047
        total = jnp.zeros((STEP, LANES), jnp.float32)
        for c in range(3):
            record = (station >> 1) * RECORDS + 2 * c + (station & 1)
            before = jnp.zeros((STEP, LANES), jnp.float32)
            columns = []
            for tile in range(TILES):
                at = first_row + (c * TILES + tile) * CAP
                wave = units[pl.ds(at, STEP, stride=0), :]
                spread = pltpu.roll(wave, 0, 1, stride=1, stride_axis=0)
                columns.append(jnp.where(own, spread, before).astype(jnp.bfloat16))
                before = spread
            columns.append(jnp.where(own, 0.0, before).astype(jnp.bfloat16))
            left = jnp.concatenate(
                [jnp.concatenate(columns[i:i + 2], axis=1) for i in range(0, TILES + 1, 2)], axis=0
            )
            frames = jnp.concatenate([early[record], late[record]], axis=0)
            product = jnp.dot(left, frames, preferred_element_type=jnp.float32)
            summed = product[:STEP]
            for part in range(1, (TILES + 1) // 2):
                later = product[part * STEP:(part + 1) * STEP]
                summed = summed + pltpu.roll(later, LANES - TURNS * part, 1)
            total = total + summed * scales[record]
        first = pltpu.roll(total, LANES - (lag >> 5), 1)
        twice[spare, 0:STEP, :] = first
        twice[spare, STEP:2 * STEP, :] = pltpu.roll(first, LANES - 1, 1)
        shifted = twice[spare, pl.ds(lag & (STEP - 1), STEP), :]
        return pl.ds(pl.multiple_of(template * STEP, STEP), STEP), shifted

    @pl.loop(0, (count + UNROLL - 1) // UNROLL)
    def _(index):
        done = [one_pick(entries[index * UNROLL + spare], spare) for spare in range(UNROLL)]
        for rows, shifted in done:
            acc[rows, :] += shifted

    for group in range(STEP // 4):
        parts = [acc[pl.ds(4 * group + j, STEP, stride=STEP), :] for j in range(4)]
        turned = jnp.concatenate(parts, axis=0).T
        dense[pl.ds(group, OUT_BLOCKS, stride=8), :] = turned[:OUT_BLOCKS]
    for part in range(out_ref.shape[1] // LANES):
        rows = dense[pl.ds(part, out_ref.shape[0], stride=3), :]
        out_ref[:, part * LANES:(part + 1) * LANES] = rows.astype(out_ref.dtype)


SMEM = pl.BlockSpec(memory_space=pltpu.SMEM)
VMEM = pl.BlockSpec(memory_space=pltpu.VMEM)
HBM = pl.BlockSpec(memory_space=pltpu.HBM)


def slot_waves(index, pick_station, template_waves, peers):
    return pl.pallas_call(
        select_kernel,
        out_shape=jax.ShapeDtypeStruct((peers, SLOT_ROWS, LANES), jnp.bfloat16),
        in_specs=[SMEM, VMEM, VMEM],
        out_specs=VMEM,
        scratch_shapes=[pltpu.VMEM((peers, SLOT_ROWS, LANES), jnp.float32)],
        compiler_params=pltpu.CompilerParams(vmem_limit_bytes=4 * 1024 * 1024),
        cost_estimate=pl.CostEstimate(flops=16_000_000, transcendentals=100, bytes_accessed=620_000),
        name="select_waves",
    )(index, pick_station, template_waves)


def scales_and_entries(index, channel_mask, pick_station, pick_lag, rows):
    slot_count = pick_station.shape[1] * CAP
    return pl.pallas_call(
        scales_kernel,
        out_shape=(
            jax.ShapeDtypeStruct((2 * rows[0].shape[0], STEP, LANES), jnp.float32),
            jax.ShapeDtypeStruct((2 * rows[0].shape[0], EARLY * STEP, LANES), jnp.bfloat16),
            jax.ShapeDtypeStruct((slot_count + UNROLL + 1,), jnp.int32),
        ),
        in_specs=[SMEM, HBM, VMEM, VMEM, VMEM, VMEM],
        out_specs=(VMEM, VMEM, SMEM),
        scratch_shapes=[
            pltpu.VMEM((CAP, pick_station.shape[1]), jnp.int32),
            pltpu.SMEM((CAP, pick_station.shape[1]), jnp.int32),
            pltpu.SMEM(channel_mask.shape, jnp.int32),
            pltpu.SemaphoreType.DMA((2,)),
        ],
        compiler_params=pltpu.CompilerParams(vmem_limit_bytes=8 * 1024 * 1024),
        cost_estimate=pl.CostEstimate(flops=6000_000_000, transcendentals=200_000, bytes_accessed=2_000_000),
        name="record_scales",
    )(index, channel_mask, pick_station, pick_lag, *rows)


def partial_stack(entries, early, scales, received, group_size):
    peers = received.shape[0]
    slot_count = peers * CAP
    lines = NT * group_size // LANES
    records = scales.shape[0]
    return pl.pallas_call(
        stack_kernel,
        out_shape=jax.ShapeDtypeStruct((slot_count, lines * LANES // slot_count), jnp.bfloat16),
        in_specs=[SMEM, VMEM, VMEM, VMEM],
        out_specs=VMEM,
        scratch_shapes=[
            pltpu.VMEM((records, (TURNS - EARLY) * STEP, LANES), jnp.bfloat16),
            pltpu.VMEM((peers * SLOT_ROWS, LANES), jnp.float32),
            pltpu.VMEM(((group_size + 1) * STEP, LANES), jnp.float32),
            pltpu.VMEM((UNROLL, 2 * STEP, LANES), jnp.float32),
            pltpu.VMEM((lines, LANES), jnp.float32),
        ],
        compiler_params=pltpu.CompilerParams(vmem_limit_bytes=16 * 1024 * 1024),
        cost_estimate=pl.CostEstimate(flops=200_000_000, transcendentals=0, bytes_accessed=8_000_000),
        name="stack_picks",
    )(entries, early, scales, received)


def body(station_data, channel_mask, template_waves, pick_station, pick_lag):
    sta_size = lax.axis_size("sta")
    tpl_size = lax.axis_size("tpl")
    group_size = pick_station.shape[0]
    stations_here = station_data.shape[1]
    index = jnp.stack([lax.axis_index("sta"), lax.axis_index("tpl")]).astype(jnp.int32)

    tiles = station_data.reshape(3, stations_here, BLOCKS, STEP).transpose(0, 1, 3, 2)
    tiles = jnp.pad(tiles, ((0, 0), (0, 0), (0, 0), (0, LANES - BLOCKS)))
    own = tiles.reshape(3 * stations_here, STEP, LANES)
    near = [own]
    for hop in range(2, tpl_size, 2):
        near.append(lax.ppermute(own, "tpl", [(i, (i + hop) % tpl_size) for i in range(tpl_size)]))
    near = jnp.concatenate(near, axis=0)
    rows = [near, lax.ppermute(near, "tpl", [(i, i ^ 1) for i in range(tpl_size)])]

    waves = template_waves.reshape(group_size, 3, L).transpose(1, 0, 2)
    outgoing = slot_waves(index, pick_station, waves, sta_size)
    received = lax.all_to_all(outgoing, "sta", split_axis=0, concat_axis=0, tiled=True)

    scales, early, entries = scales_and_entries(index, channel_mask, pick_station, pick_lag, rows)
    partial_sums = partial_stack(entries, early, scales, received, group_size)
    arrived = lax.all_to_all(partial_sums, "sta", split_axis=0, concat_axis=0, tiled=True)
    arrived = arrived.reshape(sta_size, CAP, -1).astype(jnp.float32)
    return jnp.sum(arrived, axis=0).reshape(NT // sta_size, group_size)


def solution(mesh):
    in_specs = (
        P(None, ("sta", "tpl"), None),
        P(None, "sta"),
        P("tpl", "sta", None, None),
        P("tpl", None),
        P("tpl", None),
    )
    return jax.shard_map(body, mesh=mesh, in_specs=in_specs, out_specs=P("sta", "tpl"), check_vma=False)
```

```python
import jax
import jax.numpy as jnp
from jax import lax
from jax.experimental import pallas as pl
from jax.experimental.pallas import tpu as pltpu
from jax.sharding import PartitionSpec as P

NT = 1536
L = 640
LAGS = 1024
SAMPLES = 3200
CAP = 4
STEP = 32
LANES = 128
BLOCKS = SAMPLES // STEP
OUT_BLOCKS = NT // STEP
TILES = L // LANES
TURNS = 8
EARLY = 3
UNROLL = 8
SLOT_ROWS = 64
RECORDS = 6
STATION_BITS = 4
EPSILON = 1e-05
VALID = 1 << 27


def exclusive_prefix(values):
    lanes = values.shape[-1]
    groups = values.reshape(-1, 8, lanes)
    row = lax.broadcasted_iota(jnp.int32, groups.shape, 1)
    total = groups
    for shift in (1, 2, 4):
        total = total + jnp.where(row >= shift, pltpu.roll(total, shift, 1), 0.0)
    inner = jnp.where(row >= 1, pltpu.roll(total, 1, 1), 0.0).reshape(-1, STEP // 8, 8, lanes)
    last = total.reshape(-1, STEP // 8, 8, lanes)[:, :, 7:8]
    pieces = [inner[:, 0:1]]
    carry = last[:, 0:1]
    for group in range(1, STEP // 8):
        pieces.append(inner[:, group:group + 1] + carry)
        carry = carry + last[:, group:group + 1]
    return jnp.concatenate(pieces, axis=1).reshape(values.shape)


def window_sums(values):
    width = values.shape[-1]
    span = L // STEP
    ahead = pltpu.roll(values, width - span, 1) - values
    two = jnp.sum(values.reshape(-1, STEP, width), axis=1)
    two = two + pltpu.roll(two, width - 1, 1)
    four = two + pltpu.roll(two, width - 2, 1)
    eight = four + pltpu.roll(four, width - 4, 1)
    sixteen = eight + pltpu.roll(eight, width - 8, 1)
    whole = sixteen + pltpu.roll(four, width - 16, 1)
    inner = exclusive_prefix(ahead).reshape(-1, STEP, width)
    return whole[:, None, :] + inner


def select_kernel(index_ref, station_ref, waves_ref, out_ref, staged):
    group_size = station_ref.shape[0]
    square = (group_size, group_size)
    row = lax.broadcasted_iota(jnp.int32, square, 0)
    column = lax.broadcasted_iota(jnp.int32, square, 1)
    owners = station_ref[...] >> STATION_BITS
    down = jnp.sum(jnp.where(column == index_ref[0], owners, 0), axis=1, keepdims=True)
    down = jnp.broadcast_to(down, square)
    across = jnp.sum(jnp.where(row == column, down, 0), axis=0, keepdims=True)
    same = (down == across) & (row < column)
    place = jnp.sum(same.astype(jnp.int32), axis=0, keepdims=True)
    slot = across * CAP + place
    peers = out_ref.shape[0]
    line = lax.broadcasted_iota(jnp.int32, (2 * CAP * peers, group_size), 0)
    wanted = (line >> 3) * CAP + (line & (CAP - 1)) == slot
    selects = [wanted & ((line >> 2) & 1 == half) for half in range(2)]
    select = jnp.concatenate([part.astype(jnp.float32) for part in selects], axis=1).astype(jnp.bfloat16)
    pieces = []
    for c in range(3):
        values = waves_ref[c].astype(jnp.float32)
        centred = values - jnp.mean(values, axis=-1, keepdims=True)
        power = jnp.mean(centred * centred, axis=-1, keepdims=True)
        unit = (centred / jnp.sqrt(power + EPSILON)).astype(jnp.bfloat16)
        pieces += [unit[:, tile * LANES:(tile + 1) * LANES] for tile in range(TILES)]
    pieces.append(jnp.zeros((group_size, LANES), jnp.bfloat16))
    for pair in range(len(pieces) // 2):
        both = jnp.concatenate(pieces[2 * pair:2 * pair + 2], axis=0)
        picked = jnp.dot(select, both, preferred_element_type=jnp.float32)
        staged[:, 2 * CAP * pair:2 * CAP * (pair + 1), :] = picked.reshape(peers, 2 * CAP, LANES)
    out_ref[...] = staged[...].astype(jnp.bfloat16)


def owner_of(here, core, hop, hops):
    return ((here - 2 * hop) & (2 * hops - 1)) ^ core


def scales_kernel(index_ref, mask_hbm, station_ref, lag_ref, near_ref, far_ref, scales, early, entries,
                  meta_vmem, meta, mask_ref, sems):
    mask_copy = pltpu.make_async_copy(mask_hbm, mask_ref, sems.at[0])
    mask_copy.start()
    square = station_ref.shape
    row = lax.broadcasted_iota(jnp.int32, square, 0)
    column = lax.broadcasted_iota(jnp.int32, square, 1)
    stations = station_ref[...]
    landing = (stations >> STATION_BITS) == index_ref[0]
    earlier = (column < row).astype(jnp.float32).astype(jnp.bfloat16)
    arrival = jnp.dot(earlier, landing.astype(jnp.float32).astype(jnp.bfloat16), preferred_element_type=jnp.float32)
    local = stations & (2**STATION_BITS - 1)
    packed = VALID + (column << 22) + (lag_ref[...] << 9) + (local << 5) + row
    for k in range(CAP):
        held = landing & (arrival.astype(jnp.int32) == k)
        meta_vmem[k:k + 1, :] = jnp.sum(jnp.where(held, packed, 0), axis=0, keepdims=True)
    meta_copy = pltpu.make_async_copy(meta_vmem, meta, sems.at[1])
    meta_copy.start()

    here = index_ref[1]
    hops = near_ref.shape[0] // RECORDS
    mask_copy.wait()
    for core, tile_ref in enumerate((near_ref, far_ref)):
        for hop in range(hops):
            owner = owner_of(here, core, hop, hops)
            first = owner * RECORDS
            values = tile_ref[hop * RECORDS:(hop + 1) * RECORDS].reshape(RECORDS * STEP, LANES)
            rounded = values.astype(jnp.bfloat16)
            for turn in range(EARLY):
                rolled = rounded if turn == 0 else pltpu.roll(rounded, LANES - turn, 1)
                early[pl.ds(first, RECORDS), turn * STEP:(turn + 1) * STEP, :] = rolled.reshape(RECORDS, STEP, LANES)
            mean_one = window_sums(values) * (1.0 / L)
            mean_two = window_sums(values * values) * (1.0 / L)
            factor = lax.rsqrt(mean_two - mean_one * mean_one + EPSILON)
            for record in range(RECORDS):
                weight = mask_ref[record >> 1, owner * 2 + (record & 1)].astype(jnp.float32) * (1.0 / L)
                scales[first + record] = factor[record] * weight

    meta_copy.wait()

    def list_slot(slot, count):
        packed = meta[slot & (CAP - 1), slot >> 2]
        entries[count] = packed + ((slot & (CAP - 1)) << 20)
        return count + (packed >> 27)

    total = meta.shape[1] * CAP
    count = lax.fori_loop(0, total, list_slot, jnp.int32(0), unroll=16)
    for spare in range(UNROLL):
        entries[count + spare] = -1
    entries[total + UNROLL] = count


def stack_kernel(entries, early, scales, waves_ref, out_ref, late, units, acc, twice, dense):
    count = entries[entries.shape[0] - 1]
    acc[...] = jnp.zeros_like(acc)
    units[...] = waves_ref[...].reshape(units.shape).astype(jnp.float32)

    for first in range(0, early.shape[0], RECORDS):
        values = early[first:first + RECORDS, :STEP, :].reshape(RECORDS * STEP, LANES)
        for turn in range(EARLY, TURNS):
            rolled = pltpu.roll(values, LANES - turn, 1).reshape(RECORDS, STEP, LANES)
            late[first:first + RECORDS, (turn - EARLY) * STEP:(turn - EARLY + 1) * STEP, :] = rolled
    row = lax.broadcasted_iota(jnp.int32, (STEP, LANES), 0)
    lane = lax.broadcasted_iota(jnp.int32, (STEP, LANES), 1)
    own = lane >= row

    def one_pick(entry, spare):
        held = entry >= 0
        packed = jnp.maximum(entry, 0)
        template = jnp.where(held, packed & 31, acc.shape[0] // STEP - 1)
        first_row = ((packed >> 22) & 31) * SLOT_ROWS + ((packed >> 20) & (CAP - 1))
        station = (packed >> 5) & 15
        lag = (packed >> 9) & 2047
        total = jnp.zeros((STEP, LANES), jnp.float32)
        for c in range(3):
            record = (station >> 1) * RECORDS + 2 * c + (station & 1)
            before = jnp.zeros((STEP, LANES), jnp.float32)
            columns = []
            for tile in range(TILES):
                at = first_row + (c * TILES + tile) * CAP
                wave = units[pl.ds(at, STEP, stride=0), :]
                spread = pltpu.roll(wave, 0, 1, stride=1, stride_axis=0)
                columns.append(jnp.where(own, spread, before).astype(jnp.bfloat16))
                before = spread
            columns.append(jnp.where(own, 0.0, before).astype(jnp.bfloat16))
            left = jnp.concatenate(
                [jnp.concatenate(columns[i:i + 2], axis=1) for i in range(0, TILES + 1, 2)], axis=0
            )
            frames = jnp.concatenate([early[record], late[record]], axis=0)
            product = jnp.dot(left, frames, preferred_element_type=jnp.float32)
            summed = product[:STEP]
            for part in range(1, (TILES + 1) // 2):
                later = product[part * STEP:(part + 1) * STEP]
                summed = summed + pltpu.roll(later, LANES - TURNS * part, 1)
            total = total + summed * scales[record]
        first = pltpu.roll(total, LANES - (lag >> 5), 1)
        twice[spare, 0:STEP, :] = first
        twice[spare, STEP:2 * STEP, :] = pltpu.roll(first, LANES - 1, 1)
        shifted = twice[spare, pl.ds(lag & (STEP - 1), STEP), :]
        return pl.ds(pl.multiple_of(template * STEP, STEP), STEP), shifted

    @pl.loop(0, (count + UNROLL - 1) // UNROLL)
    def _(index):
        done = [one_pick(entries[index * UNROLL + spare], spare) for spare in range(UNROLL)]
        for rows, shifted in done:
            acc[rows, :] += shifted

    for group in range(STEP // 4):
        parts = [acc[pl.ds(4 * group + j, STEP, stride=STEP), :] for j in range(4)]
        turned = jnp.concatenate(parts, axis=0).T
        dense[pl.ds(group, OUT_BLOCKS, stride=8), :] = turned[:OUT_BLOCKS]
    for part in range(out_ref.shape[1] // LANES):
        rows = dense[pl.ds(part, out_ref.shape[0], stride=3), :]
        out_ref[:, part * LANES:(part + 1) * LANES] = rows.astype(out_ref.dtype)


SMEM = pl.BlockSpec(memory_space=pltpu.SMEM)
VMEM = pl.BlockSpec(memory_space=pltpu.VMEM)
HBM = pl.BlockSpec(memory_space=pltpu.HBM)


def slot_waves(index, pick_station, template_waves, peers):
    return pl.pallas_call(
        select_kernel,
        out_shape=jax.ShapeDtypeStruct((peers, SLOT_ROWS, LANES), jnp.bfloat16),
        in_specs=[SMEM, VMEM, VMEM],
        out_specs=VMEM,
        scratch_shapes=[pltpu.VMEM((peers, SLOT_ROWS, LANES), jnp.float32)],
        compiler_params=pltpu.CompilerParams(vmem_limit_bytes=60 * 10260 * 1024),
        cost_estimate=pl.CostEstimate(flops=16_000_000, transcendentals=100, bytes_accessed=620_000),
        name="select_waves",
    )(index, pick_station, template_waves)


def scales_and_entries(index, channel_mask, pick_station, pick_lag, rows):
    slot_count = pick_station.shape[1] * CAP
    return pl.pallas_call(
        scales_kernel,
        out_shape=(
            jax.ShapeDtypeStruct((2 * rows[0].shape[0], STEP, LANES), jnp.float32),
            jax.ShapeDtypeStruct((2 * rows[0].shape[0], EARLY * STEP, LANES), jnp.bfloat16),
            jax.ShapeDtypeStruct((slot_count + UNROLL + 1,), jnp.int32),
        ),
        in_specs=[SMEM, HBM, VMEM, VMEM, VMEM, VMEM],
        out_specs=(VMEM, VMEM, SMEM),
        scratch_shapes=[
            pltpu.VMEM((CAP, pick_station.shape[1]), jnp.int32),
            pltpu.SMEM((CAP, pick_station.shape[1]), jnp.int32),
            pltpu.SMEM(channel_mask.shape, jnp.int32),
            pltpu.SemaphoreType.DMA((2,)),
        ],
        compiler_params=pltpu.CompilerParams(vmem_limit_bytes=8 * 1024 * 1024),
        cost_estimate=pl.CostEstimate(flops=6000_000_000, transcendentals=200_000, bytes_accessed=2_000_000),
        name="record_scales",
    )(index, channel_mask, pick_station, pick_lag, *rows)


def partial_stack(entries, early, scales, received, group_size):
    peers = received.shape[0]
    slot_count = peers * CAP
    lines = NT * group_size // LANES
    records = scales.shape[0]
    return pl.pallas_call(
        stack_kernel,
        out_shape=jax.ShapeDtypeStruct((slot_count, lines * LANES // slot_count), jnp.bfloat16),
        in_specs=[SMEM, VMEM, VMEM, VMEM],
        out_specs=VMEM,
        scratch_shapes=[
            pltpu.VMEM((records, (TURNS - EARLY) * STEP, LANES), jnp.bfloat16),
            pltpu.VMEM((peers * SLOT_ROWS, LANES), jnp.float32),
            pltpu.VMEM(((group_size + 1) * STEP, LANES), jnp.float32),
            pltpu.VMEM((UNROLL, 2 * STEP, LANES), jnp.float32),
            pltpu.VMEM((lines, LANES), jnp.float32),
        ],
        compiler_params=pltpu.CompilerParams(vmem_limit_bytes=16 * 1024 * 1024),
        cost_estimate=pl.CostEstimate(flops=200_000_000, transcendentals=0, bytes_accessed=8_000_000),
        name="stack_picks",
    )(entries, early, scales, received)


def body(station_data, channel_mask, template_waves, pick_station, pick_lag):
    sta_size = lax.axis_size("sta")
    tpl_size = lax.axis_size("tpl")
    group_size = pick_station.shape[0]
    stations_here = station_data.shape[1]
    index = jnp.stack([lax.axis_index("sta"), lax.axis_index("tpl")]).astype(jnp.int32)

    tiles = station_data.reshape(3, stations_here, BLOCKS, STEP).transpose(0, 1, 3, 2)
    tiles = jnp.pad(tiles, ((0, 0), (0, 0), (0, 0), (0, LANES - BLOCKS)))
    own = tiles.reshape(3 * stations_here, STEP, LANES)
    near = [own]
    for hop in range(2, tpl_size, 2):
        near.append(lax.ppermute(own, "tpl", [(i, (i + hop) % tpl_size) for i in range(tpl_size)]))
    near = jnp.concatenate(near, axis=0)
    rows = [near, lax.ppermute(near, "tpl", [(i, i ^ 1) for i in range(tpl_size)])]

    waves = template_waves.reshape(group_size, 3, L).transpose(1, 0, 2)
    outgoing = slot_waves(index, pick_station, waves, sta_size)
    received = lax.all_to_all(outgoing, "sta", split_axis=0, concat_axis=0, tiled=True)

    scales, early, entries = scales_and_entries(index, channel_mask, pick_station, pick_lag, rows)
    partial_sums = partial_stack(entries, early, scales, received, group_size)
    arrived = lax.all_to_all(partial_sums, "sta", split_axis=0, concat_axis=0, tiled=True)
    arrived = arrived.reshape(sta_size, CAP, -1).astype(jnp.float32)
    return jnp.sum(arrived, axis=0).reshape(NT // sta_size, group_size)


def solution(mesh):
    in_specs = (
        P(None, ("sta", "tpl"), None),
        P(None, "sta"),
        P("tpl", "sta", None, None),
        P("tpl", None),
        P("tpl", None),
    )
    return jax.shard_map(body, mesh=mesh, in_specs=in_specs, out_specs=P("sta", "tpl"), check_vma=False)
```

```python
import jax
import jax.numpy as jnp
from jax import lax
from jax.experimental import pallas as pl
from jax.experimental.pallas import tpu as pltpu
from jax.sharding import PartitionSpec as P

NT = 1536
L = 640
LAGS = 1024
SAMPLES = 3200
CAP = 4
STEP = 32
LANES = 128
BLOCKS = SAMPLES // STEP
OUT_BLOCKS = NT // STEP
TILES = L // LANES
TURNS = 8
EARLY = 2
UNROLL = 8
SLOT_ROWS = 64
RECORDS = 6
STATION_BITS = 4
EPSILON = 1e-05
VALID = 1 << 27


def exclusive_prefix(values):
    lanes = values.shape[-1]
    groups = values.reshape(-1, 8, lanes)
    row = lax.broadcasted_iota(jnp.int32, groups.shape, 1)
    total = groups
    for shift in (1, 2, 4):
        total = total + jnp.where(row >= shift, pltpu.roll(total, shift, 1), 0.0)
    inner = jnp.where(row >= 1, pltpu.roll(total, 1, 1), 0.0).reshape(-1, STEP // 8, 8, lanes)
    last = total.reshape(-1, STEP // 8, 8, lanes)[:, :, 7:8]
    pieces = [inner[:, 0:1]]
    carry = last[:, 0:1]
    for group in range(1, STEP // 8):
        pieces.append(inner[:, group:group + 1] + carry)
        carry = carry + last[:, group:group + 1]
    return jnp.concatenate(pieces, axis=1).reshape(values.shape)


def window_sums(values):
    width = values.shape[-1]
    span = L // STEP
    ahead = pltpu.roll(values, width - span, 1) - values
    two = jnp.sum(values.reshape(-1, STEP, width), axis=1)
    two = two + pltpu.roll(two, width - 1, 1)
    four = two + pltpu.roll(two, width - 2, 1)
    eight = four + pltpu.roll(four, width - 4, 1)
    sixteen = eight + pltpu.roll(eight, width - 8, 1)
    whole = sixteen + pltpu.roll(four, width - 16, 1)
    inner = exclusive_prefix(ahead).reshape(-1, STEP, width)
    return whole[:, None, :] + inner


def select_kernel(index_ref, station_ref, waves_ref, out_ref, staged):
    group_size = station_ref.shape[0]
    square = (group_size, group_size)
    row = lax.broadcasted_iota(jnp.int32, square, 0)
    column = lax.broadcasted_iota(jnp.int32, square, 1)
    owners = station_ref[...] >> STATION_BITS
    down = jnp.sum(jnp.where(column == index_ref[0], owners, 0), axis=1, keepdims=True)
    down = jnp.broadcast_to(down, square)
    across = jnp.sum(jnp.where(row == column, down, 0), axis=0, keepdims=True)
    same = (down == across) & (row < column)
    place = jnp.sum(same.astype(jnp.int32), axis=0, keepdims=True)
    slot = across * CAP + place
    peers = out_ref.shape[0]
    line = lax.broadcasted_iota(jnp.int32, (2 * CAP * peers, group_size), 0)
    wanted = (line >> 3) * CAP + (line & (CAP - 1)) == slot
    selects = [wanted & ((line >> 2) & 1 == half) for half in range(2)]
    select = jnp.concatenate([part.astype(jnp.float32) for part in selects], axis=1).astype(jnp.bfloat16)
    pieces = []
    for c in range(3):
        values = waves_ref[c].astype(jnp.float32)
        centred = values - jnp.mean(values, axis=-1, keepdims=True)
        power = jnp.mean(centred * centred, axis=-1, keepdims=True)
        unit = (centred / jnp.sqrt(power + EPSILON)).astype(jnp.bfloat16)
        pieces += [unit[:, tile * LANES:(tile + 1) * LANES] for tile in range(TILES)]
    pieces.append(jnp.zeros((group_size, LANES), jnp.bfloat16))
    for pair in range(len(pieces) // 2):
        both = jnp.concatenate(pieces[2 * pair:2 * pair + 2], axis=0)
        picked = jnp.dot(select, both, preferred_element_type=jnp.float32)
        staged[:, 2 * CAP * pair:2 * CAP * (pair + 1), :] = picked.reshape(peers, 2 * CAP, LANES)
    out_ref[...] = staged[...].astype(jnp.bfloat16)


def owner_of(here, core, hop, hops):
    return ((here - 2 * hop) & (2 * hops - 1)) ^ core


def scales_kernel(index_ref, mask_hbm, station_ref, lag_ref, near_ref, far_ref, scales, early, entries,
                  meta_vmem, meta, mask_ref, sems):
    mask_copy = pltpu.make_async_copy(mask_hbm, mask_ref, sems.at[0])
    mask_copy.start()
    square = station_ref.shape
    row = lax.broadcasted_iota(jnp.int32, square, 0)
    column = lax.broadcasted_iota(jnp.int32, square, 1)
    stations = station_ref[...]
    landing = (stations >> STATION_BITS) == index_ref[0]
    earlier = (column < row).astype(jnp.float32).astype(jnp.bfloat16)
    arrival = jnp.dot(earlier, landing.astype(jnp.float32).astype(jnp.bfloat16), preferred_element_type=jnp.float32)
    local = stations & (2**STATION_BITS - 1)
    packed = VALID + (column << 22) + (lag_ref[...] << 9) + (local << 5) + row
    for k in range(CAP):
        held = landing & (arrival.astype(jnp.int32) == k)
        meta_vmem[k:k + 1, :] = jnp.sum(jnp.where(held, packed, 0), axis=0, keepdims=True)
    meta_copy = pltpu.make_async_copy(meta_vmem, meta, sems.at[1])
    meta_copy.start()

    here = index_ref[1]
    hops = near_ref.shape[0] // RECORDS
    mask_copy.wait()
    for core, tile_ref in enumerate((near_ref, far_ref)):
        for hop in range(hops):
            owner = owner_of(here, core, hop, hops)
            first = owner * RECORDS
            values = tile_ref[hop * RECORDS:(hop + 1) * RECORDS].reshape(RECORDS * STEP, LANES)
            rounded = values.astype(jnp.bfloat16)
            for turn in range(EARLY):
                rolled = rounded if turn == 0 else pltpu.roll(rounded, LANES - turn, 1)
                early[pl.ds(first, RECORDS), turn * STEP:(turn + 1) * STEP, :] = rolled.reshape(RECORDS, STEP, LANES)
            mean_one = window_sums(values) * (1.0 / L)
            mean_two = window_sums(values * values) * (1.0 / L)
            factor = lax.rsqrt(mean_two - mean_one * mean_one + EPSILON)
            for record in range(RECORDS):
                weight = mask_ref[record >> 1, owner * 2 + (record & 1)].astype(jnp.float32) * (1.0 / L)
                scales[first + record] = factor[record] * weight

    meta_copy.wait()

    def list_slot(slot, count):
        packed = meta[slot & (CAP - 1), slot >> 2]
        entries[count] = packed + ((slot & (CAP - 1)) << 20)
        return count + (packed >> 27)

    total = meta.shape[1] * CAP
    count = lax.fori_loop(0, total, list_slot, jnp.int32(0), unroll=16)
    for spare in range(UNROLL):
        entries[count + spare] = -1
    entries[total + UNROLL] = count


def stack_kernel(entries, early, scales, waves_ref, out_ref, late, units, acc, twice, dense):
    count = entries[entries.shape[0] - 1]
    acc[...] = jnp.zeros_like(acc)
    units[...] = waves_ref[...].reshape(units.shape).astype(jnp.float32)

    for first in range(0, early.shape[0], RECORDS):
        values = early[first:first + RECORDS, :STEP, :].reshape(RECORDS * STEP, LANES)
        for turn in range(EARLY, TURNS):
            rolled = pltpu.roll(values, LANES - turn, 1).reshape(RECORDS, STEP, LANES)
            late[first:first + RECORDS, (turn - EARLY) * STEP:(turn - EARLY + 1) * STEP, :] = rolled
    row = lax.broadcasted_iota(jnp.int32, (STEP, LANES), 0)
    lane = lax.broadcasted_iota(jnp.int32, (STEP, LANES), 1)
    own = lane >= row

    def one_pick(entry, spare):
        held = entry >= 0
        packed = jnp.maximum(entry, 0)
        template = jnp.where(held, packed & 31, acc.shape[0] // STEP - 1)
        first_row = ((packed >> 22) & 31) * SLOT_ROWS + ((packed >> 20) & (CAP - 1))
        station = (packed >> 5) & 15
        lag = (packed >> 9) & 2047
        total = jnp.zeros((STEP, LANES), jnp.float32)
        for c in range(3):
            record = (station >> 1) * RECORDS + 2 * c + (station & 1)
            before = jnp.zeros((STEP, LANES), jnp.float32)
            columns = []
            for tile in range(TILES):
                at = first_row + (c * TILES + tile) * CAP
                wave = units[pl.ds(at, STEP, stride=0), :]
                spread = pltpu.roll(wave, 0, 1, stride=1, stride_axis=0)
                columns.append(jnp.where(own, spread, before).astype(jnp.bfloat16))
                before = spread
            columns.append(jnp.where(own, 0.0, before).astype(jnp.bfloat16))
            left = jnp.concatenate(
                [jnp.concatenate(columns[i:i + 2], axis=1) for i in range(0, TILES + 1, 2)], axis=0
            )
            frames = jnp.concatenate([early[record], late[record]], axis=0)
            product = jnp.dot(left, frames, preferred_element_type=jnp.float32)
            summed = product[:STEP]
            for part in range(1, (TILES + 1) // 2):
                later = product[part * STEP:(part + 1) * STEP]
                summed = summed + pltpu.roll(later, LANES - TURNS * part, 1)
            total = total + summed * scales[record]
        first = pltpu.roll(total, LANES - (lag >> 5), 1)
        twice[spare, 0:STEP, :] = first
        twice[spare, STEP:2 * STEP, :] = pltpu.roll(first, LANES - 1, 1)
        shifted = twice[spare, pl.ds(lag & (STEP - 1), STEP), :]
        return pl.ds(pl.multiple_of(template * STEP, STEP), STEP), shifted

    @pl.loop(0, (count + UNROLL - 1) // UNROLL)
    def _(index):
        done = [one_pick(entries[index * UNROLL + spare], spare) for spare in range(UNROLL)]
        for rows, shifted in done:
            acc[rows, :] += shifted

    for group in range(STEP // 4):
        parts = [acc[pl.ds(4 * group + j, STEP, stride=STEP), :] for j in range(4)]
        turned = jnp.concatenate(parts, axis=0).T
        dense[pl.ds(group, OUT_BLOCKS, stride=8), :] = turned[:OUT_BLOCKS]
    for part in range(out_ref.shape[1] // LANES):
        rows = dense[pl.ds(part, out_ref.shape[0], stride=3), :]
        out_ref[:, part * LANES:(part + 1) * LANES] = rows.astype(out_ref.dtype)


SMEM = pl.BlockSpec(memory_space=pltpu.SMEM)
VMEM = pl.BlockSpec(memory_space=pltpu.VMEM)
HBM = pl.BlockSpec(memory_space=pltpu.HBM)


def slot_waves(index, pick_station, template_waves, peers):
    return pl.pallas_call(
        select_kernel,
        out_shape=jax.ShapeDtypeStruct((peers, SLOT_ROWS, LANES), jnp.bfloat16),
        in_specs=[SMEM, VMEM, VMEM],
        out_specs=VMEM,
        scratch_shapes=[pltpu.VMEM((peers, SLOT_ROWS, LANES), jnp.float32)],
        compiler_params=pltpu.CompilerParams(vmem_limit_bytes=4 * 1024 * 1024),
        cost_estimate=pl.CostEstimate(flops=16_000_000, transcendentals=100, bytes_accessed=620_000),
        name="select_waves",
    )(index, pick_station, template_waves)


def scales_and_entries(index, channel_mask, pick_station, pick_lag, rows):
    slot_count = pick_station.shape[1] * CAP
    return pl.pallas_call(
        scales_kernel,
        out_shape=(
            jax.ShapeDtypeStruct((2 * rows[0].shape[0], STEP, LANES), jnp.float32),
            jax.ShapeDtypeStruct((2 * rows[0].shape[0], EARLY * STEP, LANES), jnp.bfloat16),
            jax.ShapeDtypeStruct((slot_count + UNROLL + 1,), jnp.int32),
        ),
        in_specs=[SMEM, HBM, VMEM, VMEM, VMEM, VMEM],
        out_specs=(VMEM, VMEM, SMEM),
        scratch_shapes=[
            pltpu.VMEM((CAP, pick_station.shape[1]), jnp.int32),
            pltpu.SMEM((CAP, pick_station.shape[1]), jnp.int32),
            pltpu.SMEM(channel_mask.shape, jnp.int32),
            pltpu.SemaphoreType.DMA((2,)),
        ],
        compiler_params=pltpu.CompilerParams(vmem_limit_bytes=8 * 1024 * 1024),
        cost_estimate=pl.CostEstimate(flops=6000_000_000, transcendentals=200_000, bytes_accessed=2_000_000),
        name="record_scales",
    )(index, channel_mask, pick_station, pick_lag, *rows)


def partial_stack(entries, early, scales, received, group_size):
    peers = received.shape[0]
    slot_count = peers * CAP
    lines = NT * group_size // LANES
    records = scales.shape[0]
    return pl.pallas_call(
        stack_kernel,
        out_shape=jax.ShapeDtypeStruct((slot_count, lines * LANES // slot_count), jnp.bfloat16),
        in_specs=[SMEM, VMEM, VMEM, VMEM],
        out_specs=VMEM,
        scratch_shapes=[
            pltpu.VMEM((records, (TURNS - EARLY) * STEP, LANES), jnp.bfloat16),
            pltpu.VMEM((peers * SLOT_ROWS, LANES), jnp.float32),
            pltpu.VMEM(((group_size + 1) * STEP, LANES), jnp.float32),
            pltpu.VMEM((UNROLL, 2 * STEP, LANES), jnp.float32),
            pltpu.VMEM((lines, LANES), jnp.float32),
        ],
        compiler_params=pltpu.CompilerParams(vmem_limit_bytes=16 * 1024 * 1024),
        cost_estimate=pl.CostEstimate(flops=200_000_000, transcendentals=0, bytes_accessed=8_000_000),
        name="stack_picks",
    )(entries, early, scales, received)


def body(station_data, channel_mask, template_waves, pick_station, pick_lag):
    sta_size = lax.axis_size("sta")
    tpl_size = lax.axis_size("tpl")
    group_size = pick_station.shape[0]
    stations_here = station_data.shape[1]
    index = jnp.stack([lax.axis_index("sta"), lax.axis_index("tpl")]).astype(jnp.int32)

    tiles = station_data.reshape(3, stations_here, BLOCKS, STEP).transpose(0, 1, 3, 2)
    tiles = jnp.pad(tiles, ((0, 0), (0, 0), (0, 0), (0, LANES - BLOCKS)))
    own = tiles.reshape(3 * stations_here, STEP, LANES)
    near = [own]
    for hop in range(2, tpl_size, 2):
        near.append(lax.ppermute(own, "tpl", [(i, (i + hop) % tpl_size) for i in range(tpl_size)]))
    near = jnp.concatenate(near, axis=0)
    rows = [near, lax.ppermute(near, "tpl", [(i, i ^ 1) for i in range(tpl_size)])]

    waves = template_waves.reshape(group_size, 3, L).transpose(1, 0, 2)
    outgoing = slot_waves(index, pick_station, waves, sta_size)
    received = lax.all_to_all(outgoing, "sta", split_axis=0, concat_axis=0, tiled=True)

    scales, early, entries = scales_and_entries(index, channel_mask, pick_station, pick_lag, rows)
    partial_sums = partial_stack(entries, early, scales, received, group_size)
    arrived = lax.all_to_all(partial_sums, "sta", split_axis=0, concat_axis=0, tiled=True)
    arrived = arrived.reshape(sta_size, CAP, -1).astype(jnp.float32)
    return jnp.sum(arrived, axis=0).reshape(NT // sta_size, group_size)


def solution(mesh):
    in_specs = (
        P(None, ("sta", "tpl"), None),
        P(None, "sta"),
        P("tpl", "sta", None, None),
        P("tpl", None),
        P("tpl", None),
    )
    return jax.shard_map(body, mesh=mesh, in_specs=in_specs, out_specs=P("sta", "tpl"), check_vma=False)
```

```python
import jax
import jax.numpy as jnp
from jax import lax
from jax.experimental import pallas as pl
from jax.experimental.pallas import tpu as pltpu
from jax.sharding import PartitionSpec as P

NT = 1536
L = 640
LAGS = 1024
SAMPLES = 3200
CAP = 4
STEP = 32
LANES = 128
BLOCKS = SAMPLES // STEP
OUT_BLOCKS = NT // STEP
TILES = L // LANES
TURNS = 8
UNROLL = 6
SLOT_ROWS = 64
RECORDS = 6
STATION_BITS = 4
EPSILON = 1e-05
VALID = 1 << 27


def exclusive_prefix(values):
    lanes = values.shape[-1]
    groups = values.reshape(-1, 8, lanes)
    row = lax.broadcasted_iota(jnp.int32, groups.shape, 1)
    total = groups
    for shift in (1, 2, 4):
        total = total + jnp.where(row >= shift, pltpu.roll(total, shift, 1), 0.0)
    inner = jnp.where(row >= 1, pltpu.roll(total, 1, 1), 0.0).reshape(-1, STEP // 8, 8, lanes)
    last = total.reshape(-1, STEP // 8, 8, lanes)[:, :, 7:8]
    pieces = [inner[:, 0:1]]
    carry = last[:, 0:1]
    for group in range(1, STEP // 8):
        pieces.append(inner[:, group:group + 1] + carry)
        carry = carry + last[:, group:group + 1]
    return jnp.concatenate(pieces, axis=1).reshape(values.shape)


def window_sums(values):
    width = values.shape[-1]
    span = L // STEP
    ahead = pltpu.roll(values, width - span, 1) - values
    two = jnp.sum(values.reshape(-1, STEP, width), axis=1)
    two = two + pltpu.roll(two, width - 1, 1)
    four = two + pltpu.roll(two, width - 2, 1)
    eight = four + pltpu.roll(four, width - 4, 1)
    sixteen = eight + pltpu.roll(eight, width - 8, 1)
    whole = sixteen + pltpu.roll(four, width - 16, 1)
    inner = exclusive_prefix(ahead).reshape(-1, STEP, width)
    return whole[:, None, :] + inner


def select_kernel(index_ref, station_ref, waves_ref, out_ref, staged):
    group_size = station_ref.shape[0]
    square = (group_size, group_size)
    row = lax.broadcasted_iota(jnp.int32, square, 0)
    column = lax.broadcasted_iota(jnp.int32, square, 1)
    owners = station_ref[...] >> STATION_BITS
    down = jnp.sum(jnp.where(column == index_ref[0], owners, 0), axis=1, keepdims=True)
    down = jnp.broadcast_to(down, square)
    across = jnp.sum(jnp.where(row == column, down, 0), axis=0, keepdims=True)
    same = (down == across) & (row < column)
    place = jnp.sum(same.astype(jnp.int32), axis=0, keepdims=True)
    slot = across * CAP + place
    peers = out_ref.shape[0]
    line = lax.broadcasted_iota(jnp.int32, (2 * CAP * peers, group_size), 0)
    wanted = (line >> 3) * CAP + (line & (CAP - 1)) == slot
    selects = [wanted & ((line >> 2) & 1 == half) for half in range(2)]
    select = jnp.concatenate([part.astype(jnp.float32) for part in selects], axis=1).astype(jnp.bfloat16)
    pieces = []
    for c in range(3):
        values = waves_ref[c].astype(jnp.float32)
        centred = values - jnp.mean(values, axis=-1, keepdims=True)
        power = jnp.mean(centred * centred, axis=-1, keepdims=True)
        unit = (centred / jnp.sqrt(power + EPSILON)).astype(jnp.bfloat16)
        pieces += [unit[:, tile * LANES:(tile + 1) * LANES] for tile in range(TILES)]
    pieces.append(jnp.zeros((group_size, LANES), jnp.bfloat16))
    for pair in range(len(pieces) // 2):
        both = jnp.concatenate(pieces[2 * pair:2 * pair + 2], axis=0)
        picked = jnp.dot(select, both, preferred_element_type=jnp.float32)
        staged[:, 2 * CAP * pair:2 * CAP * (pair + 1), :] = picked.reshape(peers, 2 * CAP, LANES)
    out_ref[...] = staged[...].astype(jnp.bfloat16)


def owner_of(here, core, hop, hops):
    return ((here - 2 * hop) & (2 * hops - 1)) ^ core


def scales_kernel(index_ref, mask_hbm, station_ref, lag_ref, near_ref, far_ref, scales, entries,
                  meta_vmem, meta, mask_ref, sems):
    mask_copy = pltpu.make_async_copy(mask_hbm, mask_ref, sems.at[0])
    mask_copy.start()
    square = station_ref.shape
    row = lax.broadcasted_iota(jnp.int32, square, 0)
    column = lax.broadcasted_iota(jnp.int32, square, 1)
    stations = station_ref[...]
    landing = (stations >> STATION_BITS) == index_ref[0]
    earlier = (column < row).astype(jnp.float32).astype(jnp.bfloat16)
    arrival = jnp.dot(earlier, landing.astype(jnp.float32).astype(jnp.bfloat16), preferred_element_type=jnp.float32)
    local = stations & (2**STATION_BITS - 1)
    packed = VALID + (column << 22) + (lag_ref[...] << 9) + (local << 5) + row
    for k in range(CAP):
        held = landing & (arrival.astype(jnp.int32) == k)
        meta_vmem[k:k + 1, :] = jnp.sum(jnp.where(held, packed, 0), axis=0, keepdims=True)
    meta_copy = pltpu.make_async_copy(meta_vmem, meta, sems.at[1])
    meta_copy.start()

    here = index_ref[1]
    hops = near_ref.shape[0] // RECORDS
    mask_copy.wait()
    for core, tile_ref in enumerate((near_ref, far_ref)):
        for hop in range(hops):
            owner = owner_of(here, core, hop, hops)
            values = tile_ref[hop * RECORDS:(hop + 1) * RECORDS].reshape(RECORDS * STEP, LANES)
            mean_one = window_sums(values) * (1.0 / L)
            mean_two = window_sums(values * values) * (1.0 / L)
            factor = lax.rsqrt(mean_two - mean_one * mean_one + EPSILON)
            for record in range(RECORDS):
                weight = mask_ref[record >> 1, owner * 2 + (record & 1)].astype(jnp.float32) * (1.0 / L)
                scales[owner * RECORDS + record] = factor[record] * weight

    meta_copy.wait()

    def list_slot(slot, count):
        packed = meta[slot & (CAP - 1), slot >> 2]
        entries[count] = packed + ((slot & (CAP - 1)) << 20)
        return count + (packed >> 27)

    total = meta.shape[1] * CAP
    count = lax.fori_loop(0, total, list_slot, jnp.int32(0), unroll=16)
    for spare in range(UNROLL):
        entries[count + spare] = -1
    entries[total + UNROLL] = count


def stack_kernel(entries, index_ref, near_ref, far_ref, scales, waves_ref, out_ref,
                 frames, units, acc, twice, dense):
    here = index_ref[1]
    hops = near_ref.shape[0] // RECORDS
    count = entries[entries.shape[0] - 1]
    acc[...] = jnp.zeros_like(acc)
    units[...] = waves_ref[...].reshape(units.shape).astype(jnp.float32)

    for core, tile_ref in enumerate((near_ref, far_ref)):
        for hop in range(hops):
            first = owner_of(here, core, hop, hops) * RECORDS
            at = RECORDS * hop
            values = tile_ref[at:at + RECORDS].reshape(RECORDS * STEP, LANES).astype(jnp.bfloat16)
            for turn in range(TURNS):
                rolled = values if turn == 0 else pltpu.roll(values, LANES - turn, 1)
                frames[pl.ds(first, RECORDS), turn * STEP:(turn + 1) * STEP, :] = (
                    rolled.reshape(RECORDS, STEP, LANES)
                )
    row = lax.broadcasted_iota(jnp.int32, (STEP, LANES), 0)
    lane = lax.broadcasted_iota(jnp.int32, (STEP, LANES), 1)
    own = lane >= row

    def one_pick(entry, spare):
        held = entry >= 0
        packed = jnp.maximum(entry, 0)
        template = jnp.where(held, packed & 31, acc.shape[0] // STEP - 1)
        first_row = ((packed >> 22) & 31) * SLOT_ROWS + ((packed >> 20) & (CAP - 1))
        station = (packed >> 5) & 15
        lag = (packed >> 9) & 2047
        total = jnp.zeros((STEP, LANES), jnp.float32)
        for c in range(3):
            record = (station >> 1) * RECORDS + 2 * c + (station & 1)
            before = jnp.zeros((STEP, LANES), jnp.float32)
            columns = []
            for tile in range(TILES):
                at = first_row + (c * TILES + tile) * CAP
                wave = units[pl.ds(at, STEP, stride=0), :]
                spread = pltpu.roll(wave, 0, 1, stride=1, stride_axis=0)
                columns.append(jnp.where(own, spread, before).astype(jnp.bfloat16))
                before = spread
            columns.append(jnp.where(own, 0.0, before).astype(jnp.bfloat16))
            left = jnp.concatenate(
                [jnp.concatenate(columns[i:i + 2], axis=1) for i in range(0, TILES + 1, 2)], axis=0
            )
            product = jnp.dot(left, frames[record], preferred_element_type=jnp.float32)
            summed = product[:STEP]
            for part in range(1, (TILES + 1) // 2):
                later = product[part * STEP:(part + 1) * STEP]
                summed = summed + pltpu.roll(later, LANES - TURNS * part, 1)
            total = total + summed * scales[record]
        first = pltpu.roll(total, LANES - (lag >> 5), 1)
        twice[spare, 0:STEP, :] = first
        twice[spare, STEP:2 * STEP, :] = pltpu.roll(first, LANES - 1, 1)
        shifted = twice[spare, pl.ds(lag & (STEP - 1), STEP), :]
        return pl.ds(pl.multiple_of(template * STEP, STEP), STEP), shifted

    @pl.loop(0, (count + UNROLL - 1) // UNROLL)
    def _(index):
        done = [one_pick(entries[index * UNROLL + spare], spare) for spare in range(UNROLL)]
        for rows, shifted in done:
            acc[rows, :] += shifted

    for group in range(STEP // 4):
        parts = [acc[pl.ds(4 * group + j, STEP, stride=STEP), :] for j in range(4)]
        turned = jnp.concatenate(parts, axis=0).T
        dense[pl.ds(group, OUT_BLOCKS, stride=8), :] = turned[:OUT_BLOCKS]
    for part in range(out_ref.shape[1] // LANES):
        rows = dense[pl.ds(part, out_ref.shape[0], stride=3), :]
        out_ref[:, part * LANES:(part + 1) * LANES] = rows.astype(out_ref.dtype)


SMEM = pl.BlockSpec(memory_space=pltpu.SMEM)
VMEM = pl.BlockSpec(memory_space=pltpu.VMEM)
HBM = pl.BlockSpec(memory_space=pltpu.HBM)


def slot_waves(index, pick_station, template_waves, peers):
    return pl.pallas_call(
        select_kernel,
        out_shape=jax.ShapeDtypeStruct((peers, SLOT_ROWS, LANES), jnp.bfloat16),
        in_specs=[SMEM, VMEM, VMEM],
        out_specs=VMEM,
        scratch_shapes=[pltpu.VMEM((peers, SLOT_ROWS, LANES), jnp.float32)],
        compiler_params=pltpu.CompilerParams(vmem_limit_bytes=4 * 1024 * 1024),
        cost_estimate=pl.CostEstimate(flops=16_000_000, transcendentals=100, bytes_accessed=620_000),
        name="select_waves",
    )(index, pick_station, template_waves)


def scales_and_entries(index, channel_mask, pick_station, pick_lag, rows):
    slot_count = pick_station.shape[1] * CAP
    return pl.pallas_call(
        scales_kernel,
        out_shape=(
            jax.ShapeDtypeStruct((2 * rows[0].shape[0], STEP, LANES), jnp.float32),
            jax.ShapeDtypeStruct((slot_count + UNROLL + 1,), jnp.int32),
        ),
        in_specs=[SMEM, HBM, VMEM, VMEM, VMEM, VMEM],
        out_specs=(VMEM, SMEM),
        scratch_shapes=[
            pltpu.VMEM((CAP, pick_station.shape[1]), jnp.int32),
            pltpu.SMEM((CAP, pick_station.shape[1]), jnp.int32),
            pltpu.SMEM(channel_mask.shape, jnp.int32),
            pltpu.SemaphoreType.DMA((2,)),
        ],
        compiler_params=pltpu.CompilerParams(vmem_limit_bytes=8 * 1024 * 1024),
        cost_estimate=pl.CostEstimate(flops=6000_000_000, transcendentals=200_000, bytes_accessed=2_000_000),
        name="record_scales",
    )(index, channel_mask, pick_station, pick_lag, *rows)


def partial_stack(entries, index, rows, scales, received, group_size):
    peers = received.shape[0]
    slot_count = peers * CAP
    lines = NT * group_size // LANES
    records = scales.shape[0]
    return pl.pallas_call(
        stack_kernel,
        out_shape=jax.ShapeDtypeStruct((slot_count, lines * LANES // slot_count), jnp.bfloat16),
        in_specs=[SMEM, SMEM, VMEM, VMEM, VMEM, VMEM],
        out_specs=VMEM,
        scratch_shapes=[
            pltpu.VMEM((records, TURNS * STEP, LANES), jnp.bfloat16),
            pltpu.VMEM((peers * SLOT_ROWS, LANES), jnp.float32),
            pltpu.VMEM(((group_size + 1) * STEP, LANES), jnp.float32),
            pltpu.VMEM((UNROLL, 2 * STEP, LANES), jnp.float32),
            pltpu.VMEM((lines, LANES), jnp.float32),
        ],
        compiler_params=pltpu.CompilerParams(vmem_limit_bytes=16 * 1024 * 1024),
        cost_estimate=pl.CostEstimate(flops=200_000_000, transcendentals=0, bytes_accessed=8_000_000),
        name="stack_picks",
    )(entries, index, *rows, scales, received)


def body(station_data, channel_mask, template_waves, pick_station, pick_lag):
    sta_size = lax.axis_size("sta")
    tpl_size = lax.axis_size("tpl")
    group_size = pick_station.shape[0]
    stations_here = station_data.shape[1]
    index = jnp.stack([lax.axis_index("sta"), lax.axis_index("tpl")]).astype(jnp.int32)

    tiles = station_data.reshape(3, stations_here, BLOCKS, STEP).transpose(0, 1, 3, 2)
    tiles = jnp.pad(tiles, ((0, 0), (0, 0), (0, 0), (0, LANES - BLOCKS)))
    own = tiles.reshape(3 * stations_here, STEP, LANES)
    near = [own]
    for hop in range(2, tpl_size, 2):
        near.append(lax.ppermute(own, "tpl", [(i, (i + hop) % tpl_size) for i in range(tpl_size)]))
    near = jnp.concatenate(near, axis=0)
    rows = [near, lax.ppermute(near, "tpl", [(i, i ^ 1) for i in range(tpl_size)])]

    waves = template_waves.reshape(group_size, 3, L).transpose(1, 0, 2)
    outgoing = slot_waves(index, pick_station, waves, sta_size)
    received = lax.all_to_all(outgoing, "sta", split_axis=0, concat_axis=0, tiled=True)

    scales, entries = scales_and_entries(index, channel_mask, pick_station, pick_lag, rows)
    partial_sums = partial_stack(entries, index, rows, scales, received, group_size)
    arrived = lax.all_to_all(partial_sums, "sta", split_axis=0, concat_axis=0, tiled=True)
    arrived = arrived.reshape(sta_size, CAP, -1).astype(jnp.float32)
    return jnp.sum(arrived, axis=0).reshape(NT // sta_size, group_size)


def solution(mesh):
    in_specs = (
        P(None, ("sta", "tpl"), None),
        P(None, "sta"),
        P("tpl", "sta", None, None),
        P("tpl", None),
        P("tpl", None),
    )
    return jax.shard_map(body, mesh=mesh, in_specs=in_specs, out_specs=P("sta", "tpl"), check_vma=False)
```
